32 devices in a mesh: dp: 8 (over y, x, core), seq: 4 (over z).
Axes of the slice: x: 2, y: 2, z: 4, core: 2. Of those that a mesh axis runs over, the one named last changes fastest.
Arguments:
- inputs: bfloat16 [8, 1024, 1024], P('dp', 'seq'), may hold values from -6 to 6
- positions: int32 [8, 1024], P('dp', 'seq'), may hold values from 0 to 8191
- attn_gain: bfloat16 [1024], P(('dp', 'seq')), may hold values from 0.5 to 1.5
- qkv_weight: bfloat16 [1024, 3072], P(('dp', 'seq')), may hold values from -0.1875 to 0.1875
- attn_out_weight: bfloat16 [1024, 1024], P(('dp', 'seq')), may hold values from -3.5 to 3.5
- mlp_gain: bfloat16 [1024], P(('dp', 'seq')), may hold values from 0.5 to 1.5
- up_weight: bfloat16 [1024, 5248], P(('dp', 'seq')), may hold values from -0.1875 to 0.1875
- down_weight: bfloat16 [1024, 2624], P(('dp', 'seq')), may hold values from -0.125 to 0.125
- cotangent: bfloat16 [8, 1024, 1024], P('dp', 'seq'), may hold values from -6 to 6
Outputs:
- output: bfloat16 [8, 1024, 1024], P('dp', 'seq')
- input_grad: bfloat16 [8, 1024, 1024], P('dp', 'seq')
- attn_gain_grad: float32 [1024], P(('dp', 'seq'))
- qkv_grad: float32 [1024, 3072], P(('dp', 'seq'))
- attn_out_grad: float32 [1024, 1024], P(('dp', 'seq'))
- mlp_gain_grad: float32 [1024], P(('dp', 'seq'))
- up_grad: float32 [1024, 5248], P(('dp', 'seq'))
- down_grad: float32 [1024, 2624], P(('dp', 'seq'))
The draws below stay inside these ranges and needn't reach their ends.
All inputs are finite; a program needn't handle non-finite values.
Results may differ from the reference program's by a relative error of at most 0.019.
Values may be sent and summed in bfloat16 or wider, within the bound.
No kernel may reach another device: no remote copies, remote signals or barrier semaphores. Data moves between devices by JAX's collectives and lax.ppermute only.
A program may use at most 192 MiB of HBM per device.

```python
import jax
import jax.numpy as jnp
from jax import lax

D = 1024
HEADS = 16
HEAD_DIM = 64
FF = 2624
LENGTH = 1024
SEQS = 8


def with_ends(values, rng, low, top_value):
    dims = values.shape
    index_at = [jax.random.randint(jax.random.fold_in(rng, axis), (), 0, dims[axis]) for axis in range(len(dims))]
    values = values.at[tuple(index_at)].set(low)
    longest = dims.index(max(dims))
    index_at[longest] = (index_at[longest] + 1) % dims[longest]
    return values.at[tuple(index_at)].set(top_value)


def level_of(stream_key, extent, cuts, smallest, largest):
    level = 1.0
    for axis_at, shards_of in cuts:
        heights = jax.random.uniform(jax.random.fold_in(jax.random.fold_in(stream_key, 6), axis_at), (shards_of,), jnp.float32, smallest / len(cuts), largest / len(cuts))
        level = level * jnp.repeat(jnp.exp(heights), extent[axis_at] // shards_of).reshape((-1,) + (1,) * (len(extent) - 1 - axis_at))
    return level


def bell_draw(stream_key, dims, deviation, reach, shards=(), dtype=jnp.bfloat16):
    loudness = level_of(stream_key, dims, shards, -0.22, 0.18) if shards else 1.0
    drawn = jax.random.normal(stream_key, dims, jnp.float32) * deviation * loudness
    return jnp.minimum(jnp.maximum(drawn, -reach), reach).astype(dtype)


def setup_inputs(seed: int = 0) -> dict:
    keys = jax.random.split(jax.random.key(seed), 10)
    return {
        "inputs": bell_draw(keys[0], (SEQS, LENGTH, D), 1.0, 6.0, ((0, 8), (1, 4))),
        "positions": with_ends(jax.random.randint(keys[1], (SEQS, LENGTH), 0, 8192), jax.random.fold_in(keys[1], 1), 0, 8191).astype(jnp.int32),
        "attn_gain": jnp.clip(1.0 + 0.1 * jax.random.normal(keys[2], (D,), jnp.float32), 0.5, 1.5).astype(jnp.bfloat16),
        "qkv_weight": bell_draw(keys[3], (D, 3 * D), D ** -0.5, 0.1875, ((0, 32),)),
        "attn_out_weight": bell_draw(keys[4], (D, D), (max(1, 3 * D // LENGTH)) ** -0.5, 3.5, ((0, 32),)),
        "mlp_gain": jnp.clip(1.0 + 0.1 * jax.random.normal(keys[5], (D,), jnp.float32), 0.5, 1.5).astype(jnp.bfloat16),
        "up_weight": bell_draw(keys[6], (D, 2 * FF), D ** -0.5, 0.1875, ((0, 32),)),
        "down_weight": bell_draw(keys[7], (D, FF), FF ** -0.5, 0.125, ((0, 32),)),
        "cotangent": bell_draw(keys[8], (SEQS, LENGTH, D), 1.0, 6.0, ((0, 8), (1, 4))),
    }


norm_eps = 1e-05
rope_base = 160000.0
inv_root_two = 0.7071067811865476
precise = lax.Precision.HIGHEST

@jax.custom_vjp
def low(v):
    return lax.optimization_barrier(v.astype(jnp.bfloat16)).astype(jnp.float32)

@jax.custom_vjp
def low_back(v):
    return v

def low_keep(v):
    return (low(v), None)

def low_pass(kept, grad):
    return (grad,)

def back_keep(v):
    return (v, None)

def back_low(kept, grad):
    return (low(grad),)
low.defvjp(low_keep, low_pass)
low_back.defvjp(back_keep, back_low)

def normalize(values, gain):
    centre = lax.optimization_barrier(jnp.mean(values, axis=-1, keepdims=True))
    centred = values - centre
    spread = lax.rsqrt(lax.optimization_barrier(jnp.mean(centred * centred, axis=-1, keepdims=True)) + norm_eps)
    return centred * spread * gain

def rope_tables(seq_pos):
    exponent = jnp.arange(0, HEAD_DIM, 2).astype(jnp.float32) / HEAD_DIM
    frequency = rope_base ** (-exponent)
    angles = seq_pos.astype(jnp.float32)[:, None] * frequency[None, :]
    angles = jnp.concatenate([angles, angles], axis=-1)[:, None, :]
    return (jnp.cos(angles), jnp.sin(angles))

def rotate(values, cos_table, sin_table):
    half_dim = values.shape[-1] // 2
    turned = jnp.concatenate([-values[..., half_dim:], values[..., :half_dim]], axis=-1)
    return values * cos_table + turned * sin_table

def attention(queries, key_rows, values):
    seq_len = queries.shape[0]
    block_rows = min(512, seq_len)
    score_scale = HEAD_DIM ** (-0.5)

    def one_block(q_block):
        scores = low_back(jnp.einsum('qhd,khd->hqk', q_block, key_rows, precision=precise) * score_scale)
        row_peak = lax.optimization_barrier(jnp.max(scores, axis=-1, keepdims=True))
        exp_scores = jnp.exp(scores - row_peak)
        prob_rows = low(exp_scores / lax.optimization_barrier(jnp.sum(exp_scores, axis=-1, keepdims=True)))
        return jnp.einsum('hqk,khd->qhd', prob_rows, values, precision=precise)
    blocks = lax.map(jax.checkpoint(one_block), queries.reshape(seq_len // block_rows, block_rows, HEADS, HEAD_DIM))
    return blocks.reshape(seq_len, HEADS * HEAD_DIM)

def layer_forward(resid_in, gain_one, w_qkv, w_out, gain_two, w_up, w_down, cos_table, sin_table):
    seq_len = resid_in.shape[0]
    attn_in = low(normalize(resid_in, gain_one))
    mixed_rows = low_back(jnp.dot(attn_in, w_qkv, precision=precise))
    shaped = (seq_len, HEADS, HEAD_DIM)
    queries = low_back(low(rotate(mixed_rows[:, :D].reshape(shaped), cos_table, sin_table)))
    key_rows = low_back(low(rotate(mixed_rows[:, D:2 * D].reshape(shaped), cos_table, sin_table)))
    values = low_back(low(mixed_rows[:, 2 * D:].reshape(shaped)))
    attended = low_back(low(attention(queries, key_rows, values)))
    resid = resid_in + low_back(jnp.dot(attended, w_out, precision=precise))
    mlp_in = low(normalize(resid, gain_two))
    up_rows = low_back(jnp.dot(mlp_in, w_up, precision=precise))
    inner_act = up_rows[:, :FF]
    gate_act = up_rows[:, FF:]
    gelu_val = inner_act * (0.5 * (1.0 + jax.scipy.special.erf(inner_act * inv_root_two)))
    hidden = low(gelu_val * gate_act)
    return resid + low_back(jnp.dot(hidden, w_down.T, precision=precise))

def reference(inputs, positions, attn_gain, qkv_weight, attn_out_weight, mlp_gain, up_weight, down_weight, cotangent):
    weights = tuple((tensor.astype(jnp.float32) for tensor in (attn_gain, qkv_weight, attn_out_weight, mlp_gain, up_weight, down_weight)))

    def one_sequence(total_sums, item):
        seq_in, seq_pos, seq_cot = item
        cos_table, sin_table = rope_tables(seq_pos)

        def apply(resid_in, gain_one, w_qkv, w_out, gain_two, w_up, w_down):
            return layer_forward(resid_in, gain_one, w_qkv, w_out, gain_two, w_up, w_down, cos_table, sin_table)
        result, pullback = jax.vjp(apply, seq_in.astype(jnp.float32), weights[0], weights[1], weights[2], weights[3], weights[4], weights[5])
        grads = pullback(seq_cot.astype(jnp.float32))
        total_sums = tuple((total + grad_term for total, grad_term in zip(total_sums, grads[1:])))
        return (total_sums, (result.astype(jnp.bfloat16), grads[0].astype(jnp.bfloat16)))
    empty_sums = tuple((jnp.zeros(tensor.shape, jnp.float32) for tensor in weights))
    total_sums, (outputs, input_grads) = lax.scan(one_sequence, empty_sums, (inputs, positions, cotangent))
    return (outputs, input_grads, total_sums[0], total_sums[1], total_sums[2], total_sums[3], total_sums[4], total_sums[5])
```

```python
import jax
import jax.numpy as jnp
from jax import lax
from jax.sharding import PartitionSpec as P

HEADS = 16
HEAD_DIM = 64
FF = 2624


norm_eps = 1e-05
rope_base = 160000.0
inv_root_two = 0.7071067811865476
inv_root_tau = 0.3989422804014327


def for_sending(array):
    return jax.tree.map(lambda a: a.astype(jnp.bfloat16) if a.dtype == jnp.float32 else a, array)


def normalize(values):
    centre = jnp.mean(values, axis=-1, keepdims=True)
    centred = values - centre
    spread = lax.rsqrt(jnp.mean(centred * centred, axis=-1, keepdims=True) + norm_eps)
    return (centred * spread, spread)


def norm_back(grad_in, normed, spread, gain):
    scaled = grad_in * gain
    gain_term = jnp.sum(grad_in * normed, axis=0)
    centred = (
        scaled
        - jnp.mean(scaled, axis=-1, keepdims=True)
        - normed * jnp.mean(scaled * normed, axis=-1, keepdims=True)
    )
    return (spread * centred, gain_term)


def rope_tables(seq_pos):
    exponent = jnp.arange(0, HEAD_DIM, 2).astype(jnp.float32) / HEAD_DIM
    frequency = rope_base ** (-exponent)
    angles = seq_pos.astype(jnp.float32)[:, None] * frequency[None, :]
    angles = jnp.concatenate([angles, angles], axis=-1)[:, None, :]
    return (jnp.cos(angles), jnp.sin(angles))


def rotate(values, cos_table, sin_table):
    half_dim = values.shape[-1] // 2
    turned = jnp.concatenate([-values[..., half_dim:], values[..., :half_dim]], axis=-1)
    return values * cos_table + turned * sin_table


def rotate_back(grads, cos_table, sin_table):
    half_dim = grads.shape[-1] // 2
    weighted = grads * sin_table
    turned = jnp.concatenate([weighted[..., half_dim:], -weighted[..., :half_dim]], axis=-1)
    return grads * cos_table + turned


def gelu_parts(inner_act):
    normal_cdf = 0.5 * (1.0 + jax.scipy.special.erf(inner_act * inv_root_two))
    slope = normal_cdf + inner_act * jnp.exp(-0.5 * inner_act * inner_act) * inv_root_tau
    return (inner_act * normal_cdf, slope)


def project_heads(attn_in, w_qkv, cos_table, sin_table):
    token_count, model_width = attn_in.shape
    mixed_rows = jnp.dot(attn_in, w_qkv, preferred_element_type=jnp.float32)
    shaped = (token_count, HEADS, HEAD_DIM)
    queries = rotate(mixed_rows[:, :model_width].reshape(shaped), cos_table, sin_table)
    key_rows = rotate(
        mixed_rows[:, model_width : 2 * model_width].reshape(shaped), cos_table, sin_table
    )
    queries = queries.reshape(token_count, model_width).astype(jnp.bfloat16)
    key_rows = key_rows.reshape(token_count, model_width).astype(jnp.bfloat16)
    values = mixed_rows[:, 2 * model_width :].astype(jnp.bfloat16)
    return (queries, key_rows, values)


def attend_forward(q_heads, k_heads, v_heads):
    seq_len, columns = q_heads.shape
    head_count = columns // HEAD_DIM
    block_rows = min(512, seq_len)
    block_count = seq_len // block_rows
    score_scale = HEAD_DIM ** (-0.5)
    k_all = k_heads.reshape(seq_len, head_count, HEAD_DIM)
    v_all = v_heads.reshape(seq_len, head_count, HEAD_DIM)

    def one_block(q_block):
        scores = (
            jnp.einsum("qhd,khd->hqk", q_block, k_all, preferred_element_type=jnp.float32)
            * score_scale
        )
        row_peak = jnp.max(scores, axis=-1, keepdims=True)
        exp_scores = jnp.exp(scores - row_peak)
        totals = jnp.sum(exp_scores, axis=-1, keepdims=True)
        prob_rows = (exp_scores / totals).astype(jnp.bfloat16)
        attended = jnp.einsum("hqk,khd->qhd", prob_rows, v_all, preferred_element_type=jnp.float32)
        return (attended.astype(jnp.bfloat16), row_peak[..., 0] + jnp.log(totals[..., 0]))

    attended, log_totals = lax.map(
        one_block, q_heads.reshape(block_count, block_rows, head_count, HEAD_DIM)
    )
    return (attended.reshape(seq_len, columns), log_totals)


def attend_backward(q_heads, k_heads, v_heads, d_heads, log_totals):
    seq_len, columns = q_heads.shape
    head_count = columns // HEAD_DIM
    block_rows = min(512, seq_len)
    block_count = seq_len // block_rows
    score_scale = HEAD_DIM ** (-0.5)
    k_all = k_heads.reshape(seq_len, head_count, HEAD_DIM)
    v_all = v_heads.reshape(seq_len, head_count, HEAD_DIM)
    q_blocks = q_heads.reshape(block_count, block_rows, head_count, HEAD_DIM)
    d_blocks = d_heads.reshape(block_count, block_rows, head_count, HEAD_DIM)

    def one_block(carry, item):
        key_acc, value_acc = carry
        q_block, d_block, lse_block = item
        scores = (
            jnp.einsum("qhd,khd->hqk", q_block, k_all, preferred_element_type=jnp.float32)
            * score_scale
        )
        prob_rows = jnp.exp(scores - lse_block[..., None])
        value_acc = value_acc + jnp.einsum(
            "hqk,qhd->khd",
            prob_rows.astype(jnp.bfloat16),
            d_block,
            preferred_element_type=jnp.float32,
        )
        d_probs = jnp.einsum("qhd,khd->hqk", d_block, v_all, preferred_element_type=jnp.float32)
        d_scores = (
            prob_rows * (d_probs - jnp.sum(prob_rows * d_probs, axis=-1, keepdims=True))
        ).astype(jnp.bfloat16)
        d_query = (
            jnp.einsum("hqk,khd->qhd", d_scores, k_all, preferred_element_type=jnp.float32)
            * score_scale
        )
        key_acc = (
            key_acc
            + jnp.einsum("hqk,qhd->khd", d_scores, q_block, preferred_element_type=jnp.float32)
            * score_scale
        )
        return ((key_acc, value_acc), d_query.astype(jnp.bfloat16))

    empty_acc = jnp.zeros((seq_len, head_count, HEAD_DIM), jnp.float32)
    (key_acc, value_acc), d_query = lax.scan(
        one_block, (empty_acc, empty_acc), (q_blocks, d_blocks, log_totals)
    )
    d_q = d_query.reshape(seq_len, columns)
    d_k = key_acc.astype(jnp.bfloat16).reshape(seq_len, columns)
    d_v = value_acc.astype(jnp.bfloat16).reshape(seq_len, columns)
    return (d_q, d_k, d_v)


def add_sources(received):
    return tuple((jnp.sum(piece, axis=0) for piece in received))


def per_device(
    inputs,
    positions,
    attn_gain,
    qkv_weight,
    attn_out_weight,
    mlp_gain,
    up_weight,
    down_weight,
    cotangent,
):
    layer = (
        lax.all_gather(attn_gain, ("dp", "seq"), axis=0, tiled=True),
        lax.all_gather(qkv_weight, ("dp", "seq"), axis=0, tiled=True),
        lax.all_gather(attn_out_weight, ("dp", "seq"), axis=0, tiled=True),
        lax.all_gather(mlp_gain, ("dp", "seq"), axis=0, tiled=True),
        lax.all_gather(up_weight, ("dp", "seq"), axis=0, tiled=True),
        lax.all_gather(down_weight, ("dp", "seq"), axis=0, tiled=True),
    )
    gain_one, w_qkv, w_out, gain_two, w_up, w_down = layer
    token_count = inputs.shape[1]
    resid_in = inputs[0].astype(jnp.float32)
    cos_table, sin_table = rope_tables(positions[0])
    normed_one, spread_one = normalize(resid_in)
    attn_in = (normed_one * gain_one.astype(jnp.float32)).astype(jnp.bfloat16)
    queries, key_rows, values = project_heads(attn_in, w_qkv, cos_table, sin_table)
    q_heads, k_heads, v_heads = (
        lax.all_to_all(queries, "seq", split_axis=1, concat_axis=0, tiled=True),
        lax.all_to_all(key_rows, "seq", split_axis=1, concat_axis=0, tiled=True),
        lax.all_to_all(values, "seq", split_axis=1, concat_axis=0, tiled=True),
    )
    attended_heads, log_totals = attend_forward(q_heads, k_heads, v_heads)
    attended = lax.all_to_all(attended_heads, "seq", split_axis=0, concat_axis=1, tiled=True)
    resid = resid_in + jnp.dot(attended, w_out, preferred_element_type=jnp.float32)
    normed_two, spread_two = normalize(resid)
    mlp_in = (normed_two * gain_two.astype(jnp.float32)).astype(jnp.bfloat16)
    up_rows = jnp.dot(mlp_in, w_up, preferred_element_type=jnp.float32)
    inner_act = up_rows[:, :FF]
    gate_act = up_rows[:, FF:]
    gelu_val, gelu_slope = gelu_parts(inner_act)
    hidden = (gelu_val * gate_act).astype(jnp.bfloat16)
    output = resid + jnp.einsum("tf,df->td", hidden, w_down, preferred_element_type=jnp.float32)
    layer_back = (
        lax.all_gather(attn_gain, ("dp", "seq"), axis=0, tiled=True),
        lax.all_gather(qkv_weight, ("dp", "seq"), axis=0, tiled=True),
        lax.all_gather(attn_out_weight, ("dp", "seq"), axis=0, tiled=True),
        lax.all_gather(mlp_gain, ("dp", "seq"), axis=0, tiled=True),
        lax.all_gather(up_weight, ("dp", "seq"), axis=0, tiled=True),
        lax.all_gather(down_weight, ("dp", "seq"), axis=0, tiled=True),
    )
    gain_one, w_qkv, w_out, gain_two, w_up, w_down = layer_back
    d_out = cotangent[0]
    down_grad = jnp.einsum("td,tf->df", d_out, hidden, preferred_element_type=jnp.float32)
    d_hidden = jnp.dot(d_out, w_down, preferred_element_type=jnp.float32)
    d_up = jnp.concatenate([d_hidden * gate_act * gelu_slope, d_hidden * gelu_val], axis=1).astype(
        jnp.bfloat16
    )
    up_grad = jnp.einsum("tk,tn->kn", mlp_in, d_up, preferred_element_type=jnp.float32)
    d_mlp_in = jnp.einsum("tn,kn->tk", d_up, w_up, preferred_element_type=jnp.float32)
    d_norm_two, gain_two_grad = norm_back(
        d_mlp_in, normed_two, spread_two, gain_two.astype(jnp.float32)
    )
    d_resid = d_out.astype(jnp.float32) + d_norm_two
    d_resid_low = d_resid.astype(jnp.bfloat16)
    out_grad = jnp.einsum("tk,tn->kn", attended, d_resid_low, preferred_element_type=jnp.float32)
    d_attended = jnp.einsum(
        "tn,kn->tk", d_resid_low, w_out, preferred_element_type=jnp.float32
    ).astype(jnp.bfloat16)
    d_heads = lax.all_to_all(d_attended, "seq", split_axis=1, concat_axis=0, tiled=True)
    queries, key_rows, values = project_heads(attn_in, w_qkv, cos_table, sin_table)
    head_inputs = (
        lax.all_to_all(queries, "seq", split_axis=1, concat_axis=0, tiled=True),
        lax.all_to_all(key_rows, "seq", split_axis=1, concat_axis=0, tiled=True),
        lax.all_to_all(values, "seq", split_axis=1, concat_axis=0, tiled=True),
    )
    d_q, d_k, d_v = attend_backward(
        head_inputs[0], head_inputs[1], head_inputs[2], d_heads, log_totals
    )
    dq_rows, dk_rows, dv_rows = (
        lax.all_to_all(d_q, "seq", split_axis=0, concat_axis=1, tiled=True),
        lax.all_to_all(d_k, "seq", split_axis=0, concat_axis=1, tiled=True),
        lax.all_to_all(d_v, "seq", split_axis=0, concat_axis=1, tiled=True),
    )
    shaped = (token_count, HEADS, HEAD_DIM)
    dq_pre = rotate_back(dq_rows.astype(jnp.float32).reshape(shaped), cos_table, sin_table).reshape(
        token_count, -1
    )
    dk_pre = rotate_back(dk_rows.astype(jnp.float32).reshape(shaped), cos_table, sin_table).reshape(
        token_count, -1
    )
    d_mixed = jnp.concatenate(
        [dq_pre.astype(jnp.bfloat16), dk_pre.astype(jnp.bfloat16), dv_rows], axis=1
    )
    qkv_grad = jnp.einsum("tk,tn->kn", attn_in, d_mixed, preferred_element_type=jnp.float32)
    d_attn_in = jnp.einsum("tn,kn->tk", d_mixed, w_qkv, preferred_element_type=jnp.float32)
    d_norm_one, gain_one_grad = norm_back(
        d_attn_in, normed_one, spread_one, gain_one.astype(jnp.float32)
    )
    input_grad = (d_resid + d_norm_one).astype(jnp.bfloat16)
    all_sent = (
        lax.all_to_all(
            gain_one_grad[None].astype(jnp.bfloat16), "dp", split_axis=1, concat_axis=0, tiled=True
        ).astype(jnp.float32),
        lax.all_to_all(
            qkv_grad[None].astype(jnp.bfloat16), "dp", split_axis=1, concat_axis=0, tiled=True
        ).astype(jnp.float32),
        lax.all_to_all(
            out_grad[None].astype(jnp.bfloat16), "dp", split_axis=1, concat_axis=0, tiled=True
        ).astype(jnp.float32),
        lax.all_to_all(
            gain_two_grad[None].astype(jnp.bfloat16), "dp", split_axis=1, concat_axis=0, tiled=True
        ).astype(jnp.float32),
        lax.all_to_all(
            up_grad[None].astype(jnp.bfloat16), "dp", split_axis=1, concat_axis=0, tiled=True
        ).astype(jnp.float32),
        lax.all_to_all(
            down_grad[None].astype(jnp.bfloat16), "dp", split_axis=1, concat_axis=0, tiled=True
        ).astype(jnp.float32),
    )
    grads = jax.tree.map(
        lambda part: part.astype(jnp.float32),
        lax.psum_scatter(
            for_sending(add_sources(all_sent)), "seq", scatter_dimension=0, tiled=True
        ),
    )
    return (
        output.astype(jnp.bfloat16)[None],
        input_grad[None],
        grads[0],
        grads[1],
        grads[2],
        grads[3],
        grads[4],
        grads[5],
    )

QUAD_MESH = (8, 4)
FLAT = ("dp", "seq")


def pairs_of(step):
    found = []
    for dp in range(8):
        for seq in range(4):
            place = (dp // 4, dp // 2 % 2, dp % 2, seq // 2, seq % 2)
            target = step(*place)
            if target is not None:
                y, x, c, zh, zl = target
                found.append((dp * 4 + seq, (4 * y + 2 * x + c) * 4 + 2 * zh + zl))
    return found


TO_X = pairs_of(lambda y, x, c, zh, zl: (y, 1 - x, c, zh, zl))
TO_Y = pairs_of(lambda y, x, c, zh, zl: (1 - y, x, c, zh, zl))
TO_XY = pairs_of(lambda y, x, c, zh, zl: (1 - y, 1 - x, c, zh, zl))
TO_CORE = pairs_of(lambda y, x, c, zh, zl: (y, x, 1 - c, zh, zl))
TO_ZH = pairs_of(lambda y, x, c, zh, zl: (y, x, c, 1 - zh, zl))
TO_ZL = pairs_of(lambda y, x, c, zh, zl: (y, x, c, zh, 1 - zl))
TO_HOME = pairs_of(lambda y, x, c, zh, zl: (y, x, zh, c, zl))
ENTER = pairs_of(
    lambda y, x, c, zh, zl: (y, x, c, zh, 1 - zl) if c == zh else (y, x, zh, c, zl)
)
ENTER_MOVED = pairs_of(lambda y, x, c, zh, zl: None if c == zh else (y, x, c, zh, 1 - zl))


def send(array, pairs):
    return lax.ppermute(array, FLAT, pairs)


def pick(array, index, axis=0):
    return lax.dynamic_index_in_dim(array, index, axis, keepdims=False)


def in_order(bit, own, received, axis):
    return jnp.where(
        bit == 0, jnp.stack([own, received], axis), jnp.stack([received, own], axis)
    )


def enter_quad(block, place):
    at_home = place["c"] == place["zh"]
    first = send(block, ENTER)
    second = send(first, ENTER_MOVED)
    own = jnp.where(at_home, block, first)
    other = jnp.where(at_home, first, second)
    near = jnp.stack([own, other])
    return jnp.concatenate([near, send(near, TO_CORE)])


def quad_gather(block):
    near = jnp.stack([block, send(block, TO_ZL)])
    return jnp.concatenate([near, send(near, TO_CORE)])


def quad_scatter(parts):
    far = send(parts[2:].astype(jnp.bfloat16), TO_CORE)
    near = parts[:2] + far.astype(jnp.float32)
    return near[0] + send(near[1].astype(jnp.bfloat16), TO_ZL).astype(jnp.float32)


def gather_columns(slices, place):
    c, zl, zh, xy = place["c"], place["zl"], place["zh"], place["xy"]
    both = in_order(c, pick(slices, c), send(pick(slices, 1 - c), TO_CORE), 0)
    quad = in_order(zl, pick(both, zl, 1), send(pick(both, 1 - zl, 1), TO_ZL), 1)
    line = in_order(zh, quad, send(quad, TO_ZH), 1)
    pieces = jnp.stack([line, send(line, TO_X), send(line, TO_Y), send(line, TO_XY)])
    return jnp.stack([pick(pieces, xy ^ i) for i in range(4)])


def scatter_columns(grad, place):
    c, zl, zh, xy = place["c"], place["zl"], place["zh"], place["xy"]
    wide = jnp.float32
    total = pick(grad, xy).astype(wide)
    for i, pairs in ((1, TO_X), (2, TO_Y), (3, TO_XY)):
        total = total + send(pick(grad, xy ^ i), pairs).astype(wide)
    part = send(pick(total, 1 - zh, 1).astype(jnp.bfloat16), TO_ZH).astype(wide)
    quad = (pick(total, zh, 1) + part).astype(jnp.bfloat16)
    both = in_order(zl, pick(quad, zl, 1), send(pick(quad, 1 - zl, 1), TO_ZL), 0)
    rows = in_order(c, pick(both, c, 1), send(pick(both, 1 - c, 1), TO_CORE), 0)
    return rows.astype(wide)


def quad_device(
    inputs,
    positions,
    attn_gain,
    qkv_weight,
    attn_out_weight,
    mlp_gain,
    up_weight,
    down_weight,
    cotangent,
):
    dp, seq = lax.axis_index("dp"), lax.axis_index("seq")
    place = {"c": dp % 2, "xy": dp // 2, "zl": seq % 2, "zh": seq // 2}
    group = 2 * place["c"] + place["zl"]
    low, wide = jnp.bfloat16, jnp.float32
    rows, width = qkv_weight.shape[0], attn_out_weight.shape[1]
    tokens = inputs.shape[1]
    part, ff_part = width // 4, FF // 4
    heads = HEADS // 4

    pos = positions[0]
    pos_row = jnp.concatenate([pos // 128, pos % 128]).astype(low)
    pos_row = jnp.pad(pos_row[None], ((0, 15), (0, width - 2 * tokens)))
    entered = enter_quad(jnp.concatenate([inputs[0], pos_row]), place)
    all_in = entered[:, :tokens].reshape(4 * tokens, width)
    pos_all = entered[:, tokens, : 2 * tokens].astype(wide)
    pos_all = (pos_all[:, :tokens] * 128.0 + pos_all[:, tokens:]).reshape(4 * tokens)

    gain_one, gain_two = attn_gain.astype(wide)[:, None], mlp_gain.astype(wide)[:, None]
    qkv_scaled = (qkv_weight.astype(wide) * gain_one).astype(low)
    qkv_slices = qkv_scaled.reshape(rows, 3, 4, part).transpose(2, 0, 1, 3)
    w_qkv = gather_columns(qkv_slices.reshape(2, 2, rows, 3 * part), place)
    w_qkv = w_qkv.reshape(width, 3 * part)
    out_slices = attn_out_weight.reshape(rows, 4, part).transpose(1, 0, 2)
    w_out = gather_columns(out_slices.reshape(2, 2, rows, part), place).reshape(width, part)
    up_scaled = (up_weight.astype(wide) * gain_two).astype(low)
    ff_all = jnp.concatenate([up_scaled, down_weight], axis=1)
    ff_slices = ff_all.reshape(rows, 3, 4, ff_part).transpose(2, 1, 0, 3)
    ff_slices = ff_slices.reshape(2, 2, 3 * rows, ff_part)
    w_ff = gather_columns(ff_slices, place).reshape(32, 3, rows, ff_part)
    w_inner = w_ff[:, 0].reshape(width, ff_part)
    w_gate = w_ff[:, 1].reshape(width, ff_part)
    w_down = w_ff[:, 2].reshape(width, ff_part)
    w_cols = quad_gather(w_out)
    w_cols = jnp.stack([pick(w_cols, group ^ i) for i in range(4)], axis=1)
    w_rows = w_cols.reshape(4, part, width)
    w_rows = jnp.concatenate([pick(w_rows, group ^ i) for i in range(4)])

    cot = enter_quad(cotangent[0], place).reshape(4 * tokens, width)

    cos_table, sin_table = rope_tables(pos_all)
    normed_one, spread_one = normalize(all_in.astype(wide))
    low_one = normed_one.astype(low)
    mixed = jnp.dot(low_one, w_qkv, preferred_element_type=wide)
    shaped = (4 * tokens, heads, HEAD_DIM)
    queries = rotate(mixed[:, :part].reshape(shaped), cos_table, sin_table)
    key_rows = rotate(mixed[:, part : 2 * part].reshape(shaped), cos_table, sin_table)
    queries = queries.reshape(4 * tokens, part).astype(low)
    key_rows = key_rows.reshape(4 * tokens, part).astype(low)
    values = mixed[:, 2 * part :].astype(low)
    attended, log_totals = attend_forward(queries, key_rows, values)

    blocks = attended.reshape(2, 2, tokens, part)
    side = send(blocks, TO_ZL)[:, ::-1]
    near = jnp.stack([blocks, side])
    far = send(near, TO_CORE)[:, ::-1]
    every = jnp.concatenate([near, far]).reshape(4, 4 * tokens, part)
    every = every.transpose(1, 0, 2).reshape(4 * tokens, width)
    resid = all_in.astype(wide) + jnp.dot(every, w_rows, preferred_element_type=wide)
    normed_two, spread_two = normalize(resid)
    low_two = normed_two.astype(low)
    inner_act = jnp.dot(low_two, w_inner, preferred_element_type=wide)
    gate_act = jnp.dot(low_two, w_gate, preferred_element_type=wide)
    gelu_val, gelu_slope = gelu_parts(inner_act)
    hidden = (gelu_val * gate_act).astype(low)
    d_hidden = jnp.dot(cot, w_down, preferred_element_type=wide)
    d_inner = (d_hidden * gate_act * gelu_slope).astype(low)
    d_gate = (d_hidden * gelu_val).astype(low)

    def back(grad_rows, weight):
        return jnp.einsum("tn,kn->tk", grad_rows, weight, preferred_element_type=wide)

    def outer(left, right):
        return jnp.einsum("tk,tn->kn", left, right, preferred_element_type=wide)

    d_norm = back(d_inner, w_inner) + back(d_gate, w_gate)
    scaled = quad_scatter(d_norm.reshape(4, tokens, width))
    own_two, own_spread = normed_two[:tokens], spread_two[:tokens]

    def norm_grad(scaled, normed, spread):
        return spread * (
            scaled
            - jnp.mean(scaled, axis=-1, keepdims=True)
            - normed * jnp.mean(scaled * normed, axis=-1, keepdims=True)
        )

    d_resid = cot[:tokens].astype(wide) + norm_grad(scaled, own_two, own_spread)
    d_resid_all = quad_gather(d_resid.astype(low)).reshape(4 * tokens, width)
    d_attended = back(d_resid_all, w_rows[:part]).astype(low)
    d_q, d_k, d_v = attend_backward(queries, key_rows, values, d_attended, log_totals)

    out_parts = back(hidden, w_down)
    mlp_out = quad_scatter(out_parts.reshape(4, tokens, width))
    output = send((resid[:tokens] + mlp_out).astype(low), TO_HOME)

    ff_grad = jnp.stack(
        [outer(low_two, d_inner), outer(low_two, d_gate), outer(cot, hidden)]
    ).astype(low)
    ff_grad = ff_grad.reshape(3, 32, rows, ff_part).transpose(1, 0, 2, 3)
    ff_grad = scatter_columns(ff_grad.reshape(4, 2, 2, 2, 3 * rows, ff_part), place)
    ff_grad = ff_grad.reshape(4, 3, rows, ff_part).transpose(2, 1, 0, 3).reshape(rows, 3, FF)

    own_cols = lax.dynamic_slice(d_resid_all, (0, part * group), (4 * tokens, part))
    out_grad = outer(every, own_cols).astype(low).reshape(4, part, part)
    out_grad = jnp.stack([pick(out_grad, group ^ i) for i in range(4)])
    out_grad = scatter_columns(out_grad.reshape(4, 2, 2, 2, rows, part), place)
    out_grad = out_grad.reshape(4, rows, part).transpose(1, 0, 2).reshape(rows, width)

    dq_pre = rotate_back(d_q.astype(wide).reshape(shaped), cos_table, sin_table)
    dk_pre = rotate_back(d_k.astype(wide).reshape(shaped), cos_table, sin_table)
    d_mixed = jnp.concatenate(
        [
            dq_pre.reshape(4 * tokens, part).astype(low),
            dk_pre.reshape(4 * tokens, part).astype(low),
            d_v,
        ],
        axis=1,
    )
    d_norm = back(d_mixed, w_qkv)
    scaled = quad_scatter(d_norm.reshape(4, tokens, width))
    d_first = norm_grad(scaled, normed_one[:tokens], spread_one[:tokens])
    input_grad = send((d_resid + d_first).astype(low), TO_HOME)

    qkv_grad = outer(low_one, d_mixed).astype(low)
    qkv_grad = scatter_columns(qkv_grad.reshape(4, 2, 2, 2, rows, 3 * part), place)
    qkv_grad = qkv_grad.reshape(4, rows, 3, part).transpose(1, 2, 0, 3).reshape(rows, 3 * width)

    up_grad = ff_grad[:, :2].reshape(rows, 2 * FF)
    return (
        output[None],
        input_grad[None],
        jnp.sum(qkv_grad * qkv_weight.astype(wide), axis=1),
        qkv_grad * gain_one,
        out_grad,
        jnp.sum(up_grad * up_weight.astype(wide), axis=1),
        up_grad * gain_two,
        ff_grad[:, 2],
    )


def solution(mesh):
    return jax.shard_map(
        quad_device if tuple(mesh.shape.values()) == QUAD_MESH else per_device,
        mesh=mesh,
        in_specs=(
            P("dp", "seq", None),
            P("dp", "seq"),
            P(("dp", "seq")),
            P(("dp", "seq"), None),
            P(("dp", "seq"), None),
            P(("dp", "seq")),
            P(("dp", "seq"), None),
            P(("dp", "seq"), None),
            P("dp", "seq", None),
        ),
        out_specs=(
            P("dp", "seq", None),
            P("dp", "seq", None),
            P(("dp", "seq")),
            P(("dp", "seq"), None),
            P(("dp", "seq"), None),
            P(("dp", "seq")),
            P(("dp", "seq"), None),
            P(("dp", "seq"), None),
        ),
        check_vma=False,
    )
```

```python
import jax
import jax.numpy as jnp
from jax import lax
from jax.experimental import pallas as pl
from jax.experimental.pallas import tpu as pltpu
from jax.sharding import PartitionSpec as P

HEADS = 16
HEAD_DIM = 64
FF = 2624


norm_eps = 1e-05
rope_base = 160000.0
inv_root_two = 0.7071067811865476
inv_root_tau = 0.3989422804014327


def for_sending(array):
    return jax.tree.map(lambda a: a.astype(jnp.bfloat16) if a.dtype == jnp.float32 else a, array)


def normalize(values):
    centre = jnp.mean(values, axis=-1, keepdims=True)
    centred = values - centre
    spread = lax.rsqrt(jnp.mean(centred * centred, axis=-1, keepdims=True) + norm_eps)
    return (centred * spread, spread)


def norm_back(grad_in, normed, spread, gain):
    scaled = grad_in * gain
    gain_term = jnp.sum(grad_in * normed, axis=0)
    centred = (
        scaled
        - jnp.mean(scaled, axis=-1, keepdims=True)
        - normed * jnp.mean(scaled * normed, axis=-1, keepdims=True)
    )
    return (spread * centred, gain_term)


def rope_tables(seq_pos):
    exponent = jnp.arange(0, HEAD_DIM, 2).astype(jnp.float32) / HEAD_DIM
    frequency = rope_base ** (-exponent)
    angles = seq_pos.astype(jnp.float32)[:, None] * frequency[None, :]
    angles = jnp.concatenate([angles, angles], axis=-1)[:, None, :]
    return (jnp.cos(angles), jnp.sin(angles))


def rotate(values, cos_table, sin_table):
    half_dim = values.shape[-1] // 2
    turned = jnp.concatenate([-values[..., half_dim:], values[..., :half_dim]], axis=-1)
    return values * cos_table + turned * sin_table


def rotate_back(grads, cos_table, sin_table):
    half_dim = grads.shape[-1] // 2
    weighted = grads * sin_table
    turned = jnp.concatenate([weighted[..., half_dim:], -weighted[..., :half_dim]], axis=-1)
    return grads * cos_table + turned


def gelu_parts(inner_act):
    normal_cdf = 0.5 * (1.0 + jax.scipy.special.erf(inner_act * inv_root_two))
    slope = normal_cdf + inner_act * jnp.exp(-0.5 * inner_act * inner_act) * inv_root_tau
    return (inner_act * normal_cdf, slope)


def project_heads(attn_in, w_qkv, cos_table, sin_table):
    token_count, model_width = attn_in.shape
    mixed_rows = jnp.dot(attn_in, w_qkv, preferred_element_type=jnp.float32)
    shaped = (token_count, HEADS, HEAD_DIM)
    queries = rotate(mixed_rows[:, :model_width].reshape(shaped), cos_table, sin_table)
    key_rows = rotate(
        mixed_rows[:, model_width : 2 * model_width].reshape(shaped), cos_table, sin_table
    )
    queries = queries.reshape(token_count, model_width).astype(jnp.bfloat16)
    key_rows = key_rows.reshape(token_count, model_width).astype(jnp.bfloat16)
    values = mixed_rows[:, 2 * model_width :].astype(jnp.bfloat16)
    return (queries, key_rows, values)


def attend_forward(q_heads, k_heads, v_heads):
    seq_len, columns = q_heads.shape
    head_count = columns // HEAD_DIM
    block_rows = min(512, seq_len)
    block_count = seq_len // block_rows
    score_scale = HEAD_DIM ** (-0.5)
    k_all = k_heads.reshape(seq_len, head_count, HEAD_DIM)
    v_all = v_heads.reshape(seq_len, head_count, HEAD_DIM)

    def one_block(q_block):
        scores = (
            jnp.einsum("qhd,khd->hqk", q_block, k_all, preferred_element_type=jnp.float32)
            * score_scale
        )
        row_peak = jnp.max(scores, axis=-1, keepdims=True)
        exp_scores = jnp.exp(scores - row_peak)
        totals = jnp.sum(exp_scores, axis=-1, keepdims=True)
        prob_rows = (exp_scores / totals).astype(jnp.bfloat16)
        attended = jnp.einsum("hqk,khd->qhd", prob_rows, v_all, preferred_element_type=jnp.float32)
        return (attended.astype(jnp.bfloat16), row_peak[..., 0] + jnp.log(totals[..., 0]))

    attended, log_totals = lax.map(
        one_block, q_heads.reshape(block_count, block_rows, head_count, HEAD_DIM)
    )
    return (attended.reshape(seq_len, columns), log_totals)


def attend_backward(q_heads, k_heads, v_heads, d_heads, log_totals):
    seq_len, columns = q_heads.shape
    head_count = columns // HEAD_DIM
    block_rows = min(512, seq_len)
    block_count = seq_len // block_rows
    score_scale = HEAD_DIM ** (-0.5)
    k_all = k_heads.reshape(seq_len, head_count, HEAD_DIM)
    v_all = v_heads.reshape(seq_len, head_count, HEAD_DIM)
    q_blocks = q_heads.reshape(block_count, block_rows, head_count, HEAD_DIM)
    d_blocks = d_heads.reshape(block_count, block_rows, head_count, HEAD_DIM)

    def one_block(carry, item):
        key_acc, value_acc = carry
        q_block, d_block, lse_block = item
        scores = (
            jnp.einsum("qhd,khd->hqk", q_block, k_all, preferred_element_type=jnp.float32)
            * score_scale
        )
        prob_rows = jnp.exp(scores - lse_block[..., None])
        value_acc = value_acc + jnp.einsum(
            "hqk,qhd->khd",
            prob_rows.astype(jnp.bfloat16),
            d_block,
            preferred_element_type=jnp.float32,
        )
        d_probs = jnp.einsum("qhd,khd->hqk", d_block, v_all, preferred_element_type=jnp.float32)
        d_scores = (
            prob_rows * (d_probs - jnp.sum(prob_rows * d_probs, axis=-1, keepdims=True))
        ).astype(jnp.bfloat16)
        d_query = (
            jnp.einsum("hqk,khd->qhd", d_scores, k_all, preferred_element_type=jnp.float32)
            * score_scale
        )
        key_acc = (
            key_acc
            + jnp.einsum("hqk,qhd->khd", d_scores, q_block, preferred_element_type=jnp.float32)
            * score_scale
        )
        return ((key_acc, value_acc), d_query.astype(jnp.bfloat16))

    empty_acc = jnp.zeros((seq_len, head_count, HEAD_DIM), jnp.float32)
    (key_acc, value_acc), d_query = lax.scan(
        one_block, (empty_acc, empty_acc), (q_blocks, d_blocks, log_totals)
    )
    d_q = d_query.reshape(seq_len, columns)
    d_k = key_acc.astype(jnp.bfloat16).reshape(seq_len, columns)
    d_v = value_acc.astype(jnp.bfloat16).reshape(seq_len, columns)
    return (d_q, d_k, d_v)


def add_sources(received):
    return tuple((jnp.sum(piece, axis=0) for piece in received))


def per_device(
    inputs,
    positions,
    attn_gain,
    qkv_weight,
    attn_out_weight,
    mlp_gain,
    up_weight,
    down_weight,
    cotangent,
):
    layer = (
        lax.all_gather(attn_gain, ("dp", "seq"), axis=0, tiled=True),
        lax.all_gather(qkv_weight, ("dp", "seq"), axis=0, tiled=True),
        lax.all_gather(attn_out_weight, ("dp", "seq"), axis=0, tiled=True),
        lax.all_gather(mlp_gain, ("dp", "seq"), axis=0, tiled=True),
        lax.all_gather(up_weight, ("dp", "seq"), axis=0, tiled=True),
        lax.all_gather(down_weight, ("dp", "seq"), axis=0, tiled=True),
    )
    gain_one, w_qkv, w_out, gain_two, w_up, w_down = layer
    token_count = inputs.shape[1]
    resid_in = inputs[0].astype(jnp.float32)
    cos_table, sin_table = rope_tables(positions[0])
    normed_one, spread_one = normalize(resid_in)
    attn_in = (normed_one * gain_one.astype(jnp.float32)).astype(jnp.bfloat16)
    queries, key_rows, values = project_heads(attn_in, w_qkv, cos_table, sin_table)
    q_heads, k_heads, v_heads = (
        lax.all_to_all(queries, "seq", split_axis=1, concat_axis=0, tiled=True),
        lax.all_to_all(key_rows, "seq", split_axis=1, concat_axis=0, tiled=True),
        lax.all_to_all(values, "seq", split_axis=1, concat_axis=0, tiled=True),
    )
    attended_heads, log_totals = attend_forward(q_heads, k_heads, v_heads)
    attended = lax.all_to_all(attended_heads, "seq", split_axis=0, concat_axis=1, tiled=True)
    resid = resid_in + jnp.dot(attended, w_out, preferred_element_type=jnp.float32)
    normed_two, spread_two = normalize(resid)
    mlp_in = (normed_two * gain_two.astype(jnp.float32)).astype(jnp.bfloat16)
    up_rows = jnp.dot(mlp_in, w_up, preferred_element_type=jnp.float32)
    inner_act = up_rows[:, :FF]
    gate_act = up_rows[:, FF:]
    gelu_val, gelu_slope = gelu_parts(inner_act)
    hidden = (gelu_val * gate_act).astype(jnp.bfloat16)
    output = resid + jnp.einsum("tf,df->td", hidden, w_down, preferred_element_type=jnp.float32)
    layer_back = (
        lax.all_gather(attn_gain, ("dp", "seq"), axis=0, tiled=True),
        lax.all_gather(qkv_weight, ("dp", "seq"), axis=0, tiled=True),
        lax.all_gather(attn_out_weight, ("dp", "seq"), axis=0, tiled=True),
        lax.all_gather(mlp_gain, ("dp", "seq"), axis=0, tiled=True),
        lax.all_gather(up_weight, ("dp", "seq"), axis=0, tiled=True),
        lax.all_gather(down_weight, ("dp", "seq"), axis=0, tiled=True),
    )
    gain_one, w_qkv, w_out, gain_two, w_up, w_down = layer_back
    d_out = cotangent[0]
    down_grad = jnp.einsum("td,tf->df", d_out, hidden, preferred_element_type=jnp.float32)
    d_hidden = jnp.dot(d_out, w_down, preferred_element_type=jnp.float32)
    d_up = jnp.concatenate([d_hidden * gate_act * gelu_slope, d_hidden * gelu_val], axis=1).astype(
        jnp.bfloat16
    )
    up_grad = jnp.einsum("tk,tn->kn", mlp_in, d_up, preferred_element_type=jnp.float32)
    d_mlp_in = jnp.einsum("tn,kn->tk", d_up, w_up, preferred_element_type=jnp.float32)
    d_norm_two, gain_two_grad = norm_back(
        d_mlp_in, normed_two, spread_two, gain_two.astype(jnp.float32)
    )
    d_resid = d_out.astype(jnp.float32) + d_norm_two
    d_resid_low = d_resid.astype(jnp.bfloat16)
    out_grad = jnp.einsum("tk,tn->kn", attended, d_resid_low, preferred_element_type=jnp.float32)
    d_attended = jnp.einsum(
        "tn,kn->tk", d_resid_low, w_out, preferred_element_type=jnp.float32
    ).astype(jnp.bfloat16)
    d_heads = lax.all_to_all(d_attended, "seq", split_axis=1, concat_axis=0, tiled=True)
    queries, key_rows, values = project_heads(attn_in, w_qkv, cos_table, sin_table)
    head_inputs = (
        lax.all_to_all(queries, "seq", split_axis=1, concat_axis=0, tiled=True),
        lax.all_to_all(key_rows, "seq", split_axis=1, concat_axis=0, tiled=True),
        lax.all_to_all(values, "seq", split_axis=1, concat_axis=0, tiled=True),
    )
    d_q, d_k, d_v = attend_backward(
        head_inputs[0], head_inputs[1], head_inputs[2], d_heads, log_totals
    )
    dq_rows, dk_rows, dv_rows = (
        lax.all_to_all(d_q, "seq", split_axis=0, concat_axis=1, tiled=True),
        lax.all_to_all(d_k, "seq", split_axis=0, concat_axis=1, tiled=True),
        lax.all_to_all(d_v, "seq", split_axis=0, concat_axis=1, tiled=True),
    )
    shaped = (token_count, HEADS, HEAD_DIM)
    dq_pre = rotate_back(dq_rows.astype(jnp.float32).reshape(shaped), cos_table, sin_table).reshape(
        token_count, -1
    )
    dk_pre = rotate_back(dk_rows.astype(jnp.float32).reshape(shaped), cos_table, sin_table).reshape(
        token_count, -1
    )
    d_mixed = jnp.concatenate(
        [dq_pre.astype(jnp.bfloat16), dk_pre.astype(jnp.bfloat16), dv_rows], axis=1
    )
    qkv_grad = jnp.einsum("tk,tn->kn", attn_in, d_mixed, preferred_element_type=jnp.float32)
    d_attn_in = jnp.einsum("tn,kn->tk", d_mixed, w_qkv, preferred_element_type=jnp.float32)
    d_norm_one, gain_one_grad = norm_back(
        d_attn_in, normed_one, spread_one, gain_one.astype(jnp.float32)
    )
    input_grad = (d_resid + d_norm_one).astype(jnp.bfloat16)
    all_sent = (
        lax.all_to_all(
            gain_one_grad[None].astype(jnp.bfloat16), "dp", split_axis=1, concat_axis=0, tiled=True
        ).astype(jnp.float32),
        lax.all_to_all(
            qkv_grad[None].astype(jnp.bfloat16), "dp", split_axis=1, concat_axis=0, tiled=True
        ).astype(jnp.float32),
        lax.all_to_all(
            out_grad[None].astype(jnp.bfloat16), "dp", split_axis=1, concat_axis=0, tiled=True
        ).astype(jnp.float32),
        lax.all_to_all(
            gain_two_grad[None].astype(jnp.bfloat16), "dp", split_axis=1, concat_axis=0, tiled=True
        ).astype(jnp.float32),
        lax.all_to_all(
            up_grad[None].astype(jnp.bfloat16), "dp", split_axis=1, concat_axis=0, tiled=True
        ).astype(jnp.float32),
        lax.all_to_all(
            down_grad[None].astype(jnp.bfloat16), "dp", split_axis=1, concat_axis=0, tiled=True
        ).astype(jnp.float32),
    )
    grads = jax.tree.map(
        lambda part: part.astype(jnp.float32),
        lax.psum_scatter(
            for_sending(add_sources(all_sent)), "seq", scatter_dimension=0, tiled=True
        ),
    )
    return (
        output.astype(jnp.bfloat16)[None],
        input_grad[None],
        grads[0],
        grads[1],
        grads[2],
        grads[3],
        grads[4],
        grads[5],
    )


QUAD_MESH = (8, 4)
FLAT = ("dp", "seq")
LOW, WIDE = jnp.bfloat16, jnp.float32


def pairs_of(step):
    found = []
    for dp in range(8):
        for seq in range(4):
            place = (dp // 4, dp // 2 % 2, dp % 2, seq // 2, seq % 2)
            target = step(*place)
            if target is not None:
                y, x, c, zh, zl = target
                found.append((dp * 4 + seq, (4 * y + 2 * x + c) * 4 + 2 * zh + zl))
    return found


TO_X = pairs_of(lambda y, x, c, zh, zl: (y, 1 - x, c, zh, zl))
TO_Y = pairs_of(lambda y, x, c, zh, zl: (1 - y, x, c, zh, zl))
TO_XY = pairs_of(lambda y, x, c, zh, zl: (1 - y, 1 - x, c, zh, zl))
TO_CORE = pairs_of(lambda y, x, c, zh, zl: (y, x, 1 - c, zh, zl))
TO_ZH = pairs_of(lambda y, x, c, zh, zl: (y, x, c, 1 - zh, zl))
TO_ZL = pairs_of(lambda y, x, c, zh, zl: (y, x, c, zh, 1 - zl))
TO_FAR = pairs_of(lambda y, x, c, zh, zl: (y, x, 1 - c, zh, 1 - zl))
TO_HOME = pairs_of(lambda y, x, c, zh, zl: (y, x, zh, c, zl))
ENTER = pairs_of(
    lambda y, x, c, zh, zl: (y, x, c, zh, 1 - zl) if c == zh else (y, x, zh, c, zl)
)
ENTER_MOVED = pairs_of(lambda y, x, c, zh, zl: None if c == zh else (y, x, c, zh, 1 - zl))


def send(array, pairs):
    return lax.ppermute(array, FLAT, pairs)


def core_of(flat):
    return flat >> 2 & 1


def half_of(flat):
    return flat >> 1 & 1


def group_of(flat):
    return 2 * core_of(flat) + (flat & 1)


def square_of(flat):
    return flat >> 3


def mm(left, right):
    return lax.dot_general(left, right, (((1,), (0,)), ((), ())), preferred_element_type=WIDE)


def mm_t(left, right):
    return lax.dot_general(left, right, (((1,), (1,)), ((), ())), preferred_element_type=WIDE)


def t_mm(left, right):
    return lax.dot_general(left, right, (((0,), (0,)), ((), ())), preferred_element_type=WIDE)


def window(index, size):
    return pl.ds(pl.multiple_of(index * size, size), size)


def whole(array):
    rank = len(array.shape)
    return (array, array.shape, lambda *_: (0,) * rank)


def by_rows(array, rows, step=lambda b: b):
    return (array, (rows,) + array.shape[1:], lambda b, f: (step(b),) + (0,) * (len(array.shape) - 1))


def run(body, flat, grid, ins, outs, scratch=(), flops=0):
    moved = sum(a.size * a.dtype.itemsize for a, _, _ in ins)
    moved += sum(a.size * a.dtype.itemsize for a, _, _ in outs)
    return pl.pallas_call(
        body,
        grid_spec=pltpu.PrefetchScalarGridSpec(
            num_scalar_prefetch=1,
            grid=grid,
            in_specs=[pl.BlockSpec(block, index) for _, block, index in ins],
            out_specs=[pl.BlockSpec(block, index) for _, block, index in outs],
            scratch_shapes=list(scratch),
        ),
        out_shape=[a for a, _, _ in outs],
        cost_estimate=pl.CostEstimate(flops=flops, bytes_accessed=moved, transcendentals=0),
    )(flat, *[a for a, _, _ in ins])


def shape_of(*dims, dtype=LOW):
    return jax.ShapeDtypeStruct(dims, dtype)


def normed_of(x):
    centred = x - jnp.mean(x, axis=-1, keepdims=True)
    spread = lax.rsqrt(jnp.mean(centred * centred, axis=-1, keepdims=True) + norm_eps)
    return centred * spread, spread


def split_qkv(flat, weight, gain):
    rows, part = weight.shape[0], weight.shape[1] // 12

    def body(flat_ref, w_ref, gain_ref, *refs):
        held = refs[4]
        for s in range(4):
            for t in range(3):
                cols = w_ref[:, (4 * t + s) * part : (4 * t + s + 1) * part].astype(WIDE)
                held[s, :, t * part : (t + 1) * part] = (cols * gain_ref[...]).astype(LOW)
        for i in range(4):
            refs[i][...] = held[group_of(flat_ref[0]) ^ i]

    out = shape_of(rows, 3 * part)
    return run(
        body, flat, (1,), [whole(weight), whole(gain)], [whole(out)] * 4,
        [pltpu.VMEM((4, rows, 3 * part), LOW)],
    )


def split_rest(flat, out_weight, up_weight, down_weight, gain):
    rows, part, ff = out_weight.shape[0], out_weight.shape[1] // 4, down_weight.shape[1] // 4

    def body(flat_ref, out_ref, up_ref, down_ref, gain_ref, *refs):
        ups, downs = refs[8:]
        for s in range(4):
            for t in range(2):
                cols = up_ref[:, (4 * t + s) * ff : (4 * t + s + 1) * ff].astype(WIDE)
                ups[s, :, t * ff : (t + 1) * ff] = (cols * gain_ref[...]).astype(LOW)
            downs[s, :, :part] = out_ref[:, s * part : (s + 1) * part]
            downs[s, :, part:] = down_ref[:, s * ff : (s + 1) * ff]
        for i in range(4):
            refs[i][...] = ups[group_of(flat_ref[0]) ^ i]
            refs[4 + i][...] = downs[group_of(flat_ref[0]) ^ i]

    up, down = shape_of(rows, 2 * ff), shape_of(rows, part + ff)
    made = run(
        body, flat, (1,), [whole(a) for a in (out_weight, up_weight, down_weight, gain)],
        [whole(up)] * 4 + [whole(down)] * 4,
        [pltpu.VMEM((4, rows, 2 * ff), LOW), pltpu.VMEM((4, rows, part + ff), LOW)],
    )
    return made[:4], made[4:]


def quad_rows(flat, slices):
    rows, width = slices[0].shape
    parts = [slices[0]] + [
        send(slices[i], pairs) for i, pairs in ((1, TO_ZL), (2, TO_CORE), (3, TO_FAR))
    ]

    def body(flat_ref, *refs):
        for i in range(4):
            refs[4][group_of(flat_ref[0]) ^ i] = refs[i][...]

    return run(body, flat, (1,), [whole(p) for p in parts], [whole(shape_of(4, rows, width))])[0]


def line_rows(flat, quad):
    _, rows, width = quad.shape
    near = quad.reshape(2, 2 * rows, width)
    far = send(quad, TO_ZH).reshape(2, 2 * rows, width)

    def body(flat_ref, near_ref, far_ref, out_ref):
        half = half_of(flat_ref[0])
        for c in range(2):
            out_ref[c, half] = near_ref[c]
            out_ref[c, 1 - half] = far_ref[c]

    out = run(
        body, flat, (1,), [whole(near), whole(far)], [whole(shape_of(2, 2, 2 * rows, width))]
    )[0]
    return out.reshape(8 * rows, width)


def square_pieces(line, x_first):
    one, two = (TO_X, TO_Y) if x_first else (TO_Y, TO_X)
    first = send(line, one)
    second = send(line, two)
    third = send(first, two)
    return [line, first, second, third] if x_first else [line, second, first, third]


def enter_quad(flat, block, rows):
    height, width = block.shape
    extra = height - rows
    at_home = core_of(flat[0]) == half_of(flat[0])
    first = send(block, ENTER)
    near = send(first, TO_CORE)
    second = send(first, ENTER_MOVED)
    far = send(jnp.where(at_home, block, second), TO_CORE)

    def body(flat_ref, block_ref, first_ref, second_ref, near_ref, far_ref, *outs):
        home = core_of(flat_ref[0]) == half_of(flat_ref[0])
        here = (block_ref, first_ref, near_ref, far_ref)
        moved = (first_ref, second_ref, far_ref, near_ref)
        for k in range(4):
            for flag, source in ((home, here[k]), (jnp.logical_not(home), moved[k])):

                @pl.when(jnp.logical_and(pl.program_id(0) == k, flag))
                def _(source=source):
                    def step(r, carry):
                        outs[0][window(r, 32), :] = source[window(r, 32), :]
                        return carry

                    lax.fori_loop(0, rows // 32, step, 0)
                    if extra:
                        outs[1][...] = source[rows:, :]

    made = [shape_of(4 * rows, width)] + ([shape_of(4 * extra, width)] if extra else [])
    return run(
        body, flat, (4,), [whole(a) for a in (block, first, second, near, far)],
        [by_rows(m, m.shape[0] // 4) for m in made],
    )


def quad_gather(block):
    side = send(block, TO_ZL)
    return [block, side, send(block, TO_CORE), send(side, TO_CORE)]


def rope_lanes(seq_pos):
    exponent = jnp.arange(0, HEAD_DIM, 2).astype(WIDE) / HEAD_DIM
    angles = seq_pos[:, None] * (rope_base ** (-exponent))[None, :]
    cos_half, sin_half = jnp.cos(angles), jnp.sin(angles)
    return (
        jnp.concatenate([cos_half] * 4, axis=1),
        jnp.concatenate([-sin_half, sin_half] * 2, axis=1),
    )


def turned(v):
    half = HEAD_DIM // 2
    lane = lax.broadcasted_iota(jnp.int32, v.shape, 1)
    return jnp.where(
        lane % HEAD_DIM < half, pltpu.roll(v, 2 * HEAD_DIM - half, 1), pltpu.roll(v, half, 1)
    )


def project(flat, x, pieces, cos_table, sin_table):
    tokens, width = x.shape
    piece, columns = pieces[0].shape
    rows = tokens // 4

    def body(flat_ref, x_ref, *refs):
        weights, (cos_ref, sin_ref, n_ref, mix_ref) = refs[:4], refs[4:]
        n_ref[...] = normed_of(x_ref[...].astype(WIDE))[0].astype(LOW)
        square = square_of(flat_ref[0])
        mixed = sum(mm(n_ref[:, window(square ^ i, piece)], weights[i][...]) for i in range(4))
        turned_to = 2 * columns // 3
        for t in range(0, turned_to, 128):
            v = mixed[:, t : t + 128]
            mix_ref[:, t : t + 128] = (v * cos_ref[...] + turned(v) * sin_ref[...]).astype(LOW)
        mix_ref[:, turned_to:] = mixed[:, turned_to:].astype(LOW)

    return run(
        body, flat, (4,),
        [by_rows(x, rows)] + [whole(p) for p in pieces]
        + [by_rows(cos_table, rows), by_rows(sin_table, rows)],
        [by_rows(shape_of(tokens, width), rows), by_rows(shape_of(tokens, columns), rows)],
        flops=2 * tokens * width * columns,
    )


def attend(flat, mix):
    tokens, columns = mix.shape
    part = columns // 3
    rows = tokens // 4
    scale = HEAD_DIM ** (-0.5)

    def body(flat_ref, q_ref, k_ref, v_ref, out_ref, log_ref):
        lane = lax.broadcasted_iota(jnp.int32, (rows, part), 1) // HEAD_DIM
        log_lane = lax.broadcasted_iota(jnp.int32, (rows, 128), 1)
        total = jnp.zeros((rows, part), WIDE)
        logs = jnp.zeros((rows, 128), WIDE)
        queries = q_ref[...].astype(WIDE) * scale
        for h in range(part // HEAD_DIM):
            q_head = jnp.where(lane == h, queries, 0.0).astype(LOW)
            scores = mm_t(q_head, k_ref[...])
            peak = jnp.max(scores, axis=-1, keepdims=True)
            powers = jnp.exp(scores - peak)
            mass = jnp.sum(powers, axis=-1, keepdims=True)
            probs = (powers * (1.0 / mass)).astype(LOW)
            total = jnp.where(lane == h, mm(probs, v_ref[...]), total)
            logs = jnp.where(log_lane == h, peak + jnp.log(mass), logs)
        out_ref[...] = total.astype(LOW)
        log_ref[...] = logs

    return run(
        body, flat, (4,),
        [
            (mix, (rows, part), lambda b, f: (b, 0)),
            (mix, (tokens, part), lambda b, f: (0, 1)),
            (mix, (tokens, part), lambda b, f: (0, 2)),
        ],
        [by_rows(shape_of(tokens, part), rows), by_rows(shape_of(tokens, 128, dtype=WIDE), rows)],
        flops=16 * tokens * tokens * part,
    )


def token_parts(arrays, rows):
    return [by_rows(a, rows, lambda b, i=i: b ^ i) for i, a in enumerate(arrays)]


def join_heads(flat, x, heads, columns):
    tokens, width = x.shape
    rows, part = tokens // 4, width // 4

    def body(flat_ref, x_ref, *refs):
        parts, weights, (n_ref, own_ref, held) = refs[:4], refs[4:8], refs[8:]
        group, square = group_of(flat_ref[0]), square_of(flat_ref[0])
        for j in range(4):
            cols = window(group ^ j, part)
            held[:, cols] = x_ref[:, cols].astype(WIDE) + sum(
                mm(parts[i][...], weights[j][window(group ^ i ^ square, part), :])
                for i in range(4)
            )
        resid = held[...]
        n_ref[...] = normed_of(resid)[0].astype(LOW)

        @pl.when(pl.program_id(0) == 0)
        def _():
            own_ref[...] = held[...]

    return run(
        body, flat, (4,),
        [by_rows(x, rows)] + token_parts(heads, rows) + [whole(w) for w in columns],
        [by_rows(shape_of(tokens, width), rows), whole(shape_of(rows, width, dtype=WIDE))],
        [pltpu.VMEM((rows, width), WIDE)],
        flops=2 * tokens * width * width,
    )


def feed(flat, normed, cot, ups, downs):
    tokens, width = normed.shape
    piece, ff = ups[0].shape[0], ups[0].shape[1] // 2
    skip = downs[0].shape[1] - ff
    rows = tokens // 4

    def body(flat_ref, n_ref, cot_ref, *refs):
        up_refs, down_refs, (h_ref, d_ref) = refs[:4], refs[4:8], refs[8:]
        square = square_of(flat_ref[0])
        wide = sum(mm(n_ref[:, window(square ^ i, piece)], up_refs[i][...]) for i in range(4))
        d_hidden = sum(
            mm(cot_ref[:, window(square ^ i, piece)], down_refs[i][:, skip:]) for i in range(4)
        )
        inner, gate = wide[:, :ff], wide[:, ff:]
        cdf = 0.5 * (1.0 + lax.erf(inner * inv_root_two))
        slope = cdf + inner * jnp.exp(-0.5 * inner * inner) * inv_root_tau
        bent = inner * cdf
        h_ref[...] = (bent * gate).astype(LOW)
        d_ref[:, :ff] = (d_hidden * gate * slope).astype(LOW)
        d_ref[:, ff:] = (d_hidden * bent).astype(LOW)

    return run(
        body, flat, (4,),
        [by_rows(normed, rows), by_rows(cot, rows)] + [whole(w) for w in (*ups, *downs)],
        [by_rows(shape_of(tokens, ff), rows), by_rows(shape_of(tokens, 2 * ff), rows)],
        flops=6 * tokens * width * ff,
    )


def back_pair(flat, grads, pieces, odd):
    tokens = grads[0][0].shape[0]
    piece = pieces[0].shape[0]
    rows, width, count = tokens // 4, 4 * piece, len(grads)

    def body(flat_ref, *refs):
        arrays, weights, (near_ref, far_ref, held) = (
            refs[:count], refs[count : count + 4], refs[count + 4 :],
        )
        square = square_of(flat_ref[0])
        for i in range(4):
            held[:, window(square ^ i, piece)] = sum(
                mm_t(a[...], weights[i][:, at : at + a.shape[1]])
                for a, (_, at) in zip(arrays, grads)
            )

        @pl.when(pl.program_id(0) == 0)
        def _():
            near_ref[...] = held[...]

        @pl.when(pl.program_id(0) == 1)
        def _():
            far_ref[...] = held[...].astype(LOW)

    return run(
        body, flat, (2,),
        [by_rows(a, rows, lambda b: 2 * b + odd) for a, _ in grads] + [whole(p) for p in pieces],
        [whole(shape_of(rows, width, dtype=WIDE)), whole(shape_of(rows, width))],
        [pltpu.VMEM((rows, width), WIDE)],
        flops=tokens * width * sum(a.shape[1] for a, _ in grads),
    )


def quad_sum(flat, grads, pieces):
    near, far = back_pair(flat, grads, pieces, 1)
    side = send((near + send(far, TO_CORE).astype(WIDE)).astype(LOW), TO_ZL)
    own, far = back_pair(flat, grads, pieces, 0)
    return own, send(far, TO_CORE), side


def norm_pull(flat, x, terms, base, keep):
    rows, width = terms[0].shape
    step = rows // 4

    def body(flat_ref, x_ref, a_ref, b_ref, c_ref, base_ref, *outs):
        normed, spread = normed_of(x_ref[...].astype(WIDE))
        scaled = a_ref[...] + b_ref[...].astype(WIDE) + c_ref[...].astype(WIDE)
        grad = base_ref[...].astype(WIDE) + spread * (
            scaled
            - jnp.mean(scaled, axis=-1, keepdims=True)
            - normed * jnp.mean(scaled * normed, axis=-1, keepdims=True)
        )
        outs[0][...] = grad.astype(LOW)
        if keep:
            outs[1][...] = grad

    outs = [shape_of(rows, width)] + ([shape_of(rows, width, dtype=WIDE)] if keep else [])
    return run(
        body, flat, (4,), [by_rows(a, step) for a in (x, *terms, base)],
        [by_rows(o, step) for o in outs],
    )


def feed_grads(flat, normed, cot, d_up, hidden):
    tokens, width = normed.shape
    rows, piece = tokens // 4, width // 4
    ff = hidden.shape[1]

    def body(flat_ref, n_ref, cot_ref, d_ref, h_ref, *refs):
        outs, held = refs[:4], refs[4]
        square = square_of(flat_ref[0])

        @pl.when(pl.program_id(0) == 0)
        def _():
            held[...] = jnp.zeros_like(held)

        for i in range(4):
            cols = window(square ^ i, piece)
            held[i, :, : 2 * ff] += t_mm(n_ref[:, cols], d_ref[...])
            held[i, :, 2 * ff :] += t_mm(cot_ref[:, cols], h_ref[...])

        @pl.when(pl.program_id(0) == 3)
        def _():
            for i in range(4):
                outs[i][...] = held[i].astype(LOW)

    return run(
        body, flat, (4,), [by_rows(a, rows) for a in (normed, cot, d_up, hidden)],
        [whole(shape_of(piece, 3 * ff))] * 4, [pltpu.VMEM((4, piece, 3 * ff), WIDE)],
        flops=6 * tokens * width * ff,
    )


def heads_back(flat, d_all, heads, columns):
    rows, width = d_all[0].shape
    part = width // 4

    def body(flat_ref, *refs):
        blocks, parts, weights = refs[:4], refs[4:8], refs[8:12]
        d_ref, grad_ref, block, held, total = refs[12:]
        group, square = group_of(flat_ref[0]), square_of(flat_ref[0])
        at = pl.program_id(0)
        for k in range(4):

            @pl.when(at == k)
            def _(source=blocks[k]):
                def step(r, carry):
                    block[window(r, 32), :] = source[window(r, 32), :]
                    return carry

                lax.fori_loop(0, rows // 32, step, 0)

            held[k] = parts[k][...]

        @pl.when(at == 0)
        def _():
            total[...] = jnp.zeros_like(total)

        d_ref[...] = sum(
            mm_t(block[:, window(group ^ j, part)], weights[j][window(group ^ square, part), :])
            for j in range(4)
        ).astype(LOW)
        mine = block[:, window(group, part)]
        for i in range(4):
            total[i] += t_mm(held[group ^ square ^ i], mine)

        @pl.when(at == 3)
        def _():
            grad_ref[...] = total[...].astype(LOW)

    return run(
        body, flat, (4,),
        [whole(d) for d in d_all] + token_parts(heads, rows) + [whole(w) for w in columns],
        [by_rows(shape_of(4 * rows, part), rows), whole(shape_of(4, part, part))],
        [
            pltpu.VMEM((rows, width), LOW),
            pltpu.VMEM((4, rows, part), LOW),
            pltpu.VMEM((4, part, part), WIDE),
        ],
        flops=4 * 4 * rows * width * part,
    )


def attend_back(flat, mix, attended, d_attended, logs, cos_table, sin_table):
    tokens, columns = mix.shape
    part = columns // 3
    rows = tokens // 4
    scale = HEAD_DIM ** (-0.5)
    heads = part // HEAD_DIM

    def rotated(grad, cos, sin):
        halves = [grad[:, t : t + 128] for t in range(0, part, 128)]
        return jnp.concatenate([v * cos - turned(v) * sin for v in halves], axis=1).astype(LOW)

    def body(flat_ref, q_ref, k_ref, v_ref, o_ref, d_ref, log_ref, cos_ref, sin_ref, *refs):
        dq_ref, dk_ref, dv_ref, k_total, v_total = refs
        at = pl.program_id(0)

        @pl.when(at == 0)
        def _():
            k_total[...] = jnp.zeros_like(k_total)
            v_total[...] = jnp.zeros_like(v_total)

        lane = lax.broadcasted_iota(jnp.int32, (rows, part), 1) // HEAD_DIM
        queries = q_ref[...].astype(WIDE) * scale
        grads = d_ref[...].astype(WIDE)
        chosen = lax.broadcasted_iota(jnp.int32, (8, part), 0) == (
            lax.broadcasted_iota(jnp.int32, (8, part), 1) // HEAD_DIM
        )
        deltas = lax.dot_general(
            chosen.astype(WIDE), grads * o_ref[...].astype(WIDE), (((1,), (1,)), ((), ())),
            precision=lax.Precision.HIGHEST, preferred_element_type=WIDE,
        )
        d_query = jnp.zeros((rows, part), WIDE)
        for h in range(heads):
            q_head = jnp.where(lane == h, queries, 0.0).astype(LOW)
            d_head = jnp.where(lane == h, grads, 0.0).astype(LOW)
            probs = jnp.exp(mm_t(k_ref[...], q_head) - log_ref[h : h + 1, :])
            d_probs = mm_t(v_ref[...], d_head)
            d_scores = (probs * (d_probs - deltas[h : h + 1, :])).astype(LOW)
            v_total[...] += mm(probs.astype(LOW), d_head)
            k_total[...] += mm(d_scores, q_head)
            d_query = jnp.where(lane == h, t_mm(d_scores, k_ref[...]), d_query)
        here = window(at, rows)
        dq_ref[...] = rotated(d_query * scale, cos_ref[here, :], sin_ref[here, :])

        @pl.when(at == 3)
        def _():
            dk_ref[...] = rotated(k_total[...], cos_ref[...], sin_ref[...])
            dv_ref[...] = v_total[...].astype(LOW)

    out = shape_of(tokens, part)
    return run(
        body, flat, (4,),
        [
            (mix, (rows, part), lambda b, f: (b, 0)),
            (mix, (tokens, part), lambda b, f: (0, 1)),
            (mix, (tokens, part), lambda b, f: (0, 2)),
            by_rows(attended, rows),
            by_rows(d_attended, rows),
            (logs, (8, rows), lambda b, f: (0, b)),
            whole(cos_table),
            whole(sin_table),
        ],
        [by_rows(out, rows), whole(out), whole(out)],
        [pltpu.VMEM((tokens, part), WIDE)] * 2,
        flops=40 * tokens * tokens * part,
    )


def mixed_grads(flat, normed, d_mixed, out_grad):
    tokens, width = normed.shape
    rows, piece = tokens // 4, width // 4
    part = d_mixed[0].shape[1]

    def body(flat_ref, n_ref, *refs):
        grads, out_ref, outs, held = refs[:3], refs[3], refs[4:8], refs[8]
        square = square_of(flat_ref[0])

        @pl.when(pl.program_id(0) == 0)
        def _():
            held[...] = jnp.zeros_like(held)

        for i in range(4):
            cols = n_ref[:, window(square ^ i, piece)]
            for t in range(3):
                held[i, :, t * part : (t + 1) * part] += t_mm(cols, grads[t][...])

        @pl.when(pl.program_id(0) == 3)
        def _():
            for i in range(4):
                outs[i][:, : 3 * part] = held[i].astype(LOW)
                outs[i][:, 3 * part :] = out_ref[i]

    return run(
        body, flat, (4,),
        [by_rows(normed, rows)] + [by_rows(d, rows) for d in d_mixed] + [whole(out_grad)],
        [whole(shape_of(piece, 4 * part))] * 4, [pltpu.VMEM((4, piece, 3 * part), WIDE)],
        flops=6 * tokens * width * part,
    )


def owned_slices(flat, pieces):
    high, width = pieces[0].shape
    rows = high // 8
    terms = [pieces[0]] + [
        send(pieces[i], pairs) for i, pairs in ((1, TO_X), (2, TO_Y), (3, TO_XY))
    ]
    terms = [t.reshape(2, 2, 2 * rows, width) for t in terms]

    def fold(flat_ref, *refs):
        half = half_of(flat_ref[0])
        refs[4][0] = sum(refs[i][0, half].astype(WIDE) for i in range(4))
        refs[5][0] = sum(refs[i][0, 1 - half].astype(WIDE) for i in range(4)).astype(LOW)

    kept, sent = run(
        fold, flat, (2,), [by_rows(t, 1) for t in terms],
        [
            by_rows(shape_of(2, 2 * rows, width, dtype=WIDE), 1),
            by_rows(shape_of(2, 2 * rows, width), 1),
        ],
    )
    kept = kept.reshape(4, rows, width)
    sent = send(sent, TO_ZH).reshape(4, rows, width)

    def share(flat_ref, kept_ref, sent_ref, *outs):
        for i in range(4):
            at = group_of(flat_ref[0]) ^ i
            outs[i][...] = (kept_ref[at] + sent_ref[at].astype(WIDE)).astype(LOW)

    slices = run(
        share, flat, (1,), [whole(kept), whole(sent)], [whole(shape_of(rows, width))] * 4
    )
    return [slices[0]] + [
        send(slices[i], pairs) for i, pairs in ((1, TO_ZL), (2, TO_CORE), (3, TO_FAR))
    ]


def finish(flat, slices, weight, gain, sizes):
    rows, width = slices[0].shape
    count, part, rest = sizes

    def body(flat_ref, *refs):
        w_ref, gain_ref, scaled_ref, gain_out, plain_ref, held = refs[4:]
        for i in range(4):
            held[group_of(flat_ref[0]) ^ i] = refs[i][...].astype(WIDE)
        total = jnp.zeros((rows, 1), WIDE)
        for s in range(4):
            for t in range(count):
                at = (4 * t + s) * part
                grad = held[s, :, t * part : (t + 1) * part]
                total += jnp.sum(
                    grad * w_ref[:, at : at + part].astype(WIDE), axis=1, keepdims=True
                )
                scaled_ref[:, at : at + part] = grad * gain_ref[...]
            plain_ref[:, s * rest : (s + 1) * rest] = held[s, :, count * part :]
        gain_out[...] = total

    return run(
        body, flat, (1,), [whole(a) for a in (*slices, weight, gain)],
        [
            whole(shape_of(*weight.shape, dtype=WIDE)),
            whole(shape_of(rows, 1, dtype=WIDE)),
            whole(shape_of(rows, 4 * rest, dtype=WIDE)),
        ],
        [pltpu.VMEM((4, rows, width), WIDE)],
    )


def quad_device(
    inputs,
    positions,
    attn_gain,
    qkv_weight,
    attn_out_weight,
    mlp_gain,
    up_weight,
    down_weight,
    cotangent,
):
    flat = lax.axis_index(FLAT).astype(jnp.int32).reshape(1)
    tokens, width = inputs.shape[1:]
    part, ff = width // 4, FF // 4
    gain_one, gain_two = attn_gain.astype(WIDE)[:, None], mlp_gain.astype(WIDE)[:, None]

    pos = positions[0]
    pos_row = jnp.concatenate([pos // 128, pos % 128]).astype(LOW)
    pos_row = jnp.pad(pos_row[None], ((0, 15), (0, width - 2 * tokens)))
    x, pos_all = enter_quad(flat, jnp.concatenate([inputs[0], pos_row]), tokens)
    w_qkv = split_qkv(flat, qkv_weight, gain_one)
    w_qkv = square_pieces(line_rows(flat, quad_rows(flat, w_qkv)), True)
    w_up, w_down = split_rest(flat, attn_out_weight, up_weight, down_weight, gain_two)
    w_down = square_pieces(line_rows(flat, quad_rows(flat, w_down)), True)
    w_up = square_pieces(line_rows(flat, quad_rows(flat, w_up)), False)
    w_out = quad_gather(jnp.concatenate([p[:, :part] for p in w_down]))
    (cot,) = enter_quad(flat, cotangent[0], tokens)

    pos_all = pos_all.reshape(4, 16, width)[:, 0, : 2 * tokens].astype(WIDE)
    pos_all = (pos_all[:, :tokens] * 128.0 + pos_all[:, tokens:]).reshape(4 * tokens)
    cos_table, sin_table = rope_lanes(pos_all)
    normed_one, mix = project(flat, x, w_qkv, cos_table, sin_table)
    attended, logs = attend(flat, mix)
    logs = logs[:, :8].T
    heads = quad_gather(attended)
    normed_two, resid = join_heads(flat, x, heads, w_out)
    hidden, d_up = feed(flat, normed_two, cot, w_up, w_down)
    terms = quad_sum(flat, [(d_up, 0)], w_up)
    d_low, d_resid = norm_pull(flat, resid, terms, cot, True)
    ff_pieces = feed_grads(flat, normed_two, cot, d_up, hidden)
    d_all = quad_gather(d_low)
    out_terms = quad_sum(flat, [(hidden, part)], w_down)
    output = resid + out_terms[0] + out_terms[1].astype(WIDE) + out_terms[2].astype(WIDE)
    output = send(output.astype(LOW), TO_HOME)
    d_attended, out_grad = heads_back(flat, d_all, heads, w_out)
    d_mixed = attend_back(flat, mix, attended, d_attended, logs, cos_table, sin_table)
    mixed_pieces = mixed_grads(flat, normed_one, d_mixed, out_grad)
    terms = quad_sum(flat, [(d, t * part) for t, d in enumerate(d_mixed)], w_qkv)
    (input_grad,) = norm_pull(flat, x, terms, d_resid, False)
    input_grad = send(input_grad, TO_HOME)
    up_grad, gain_two_grad, down_grad = finish(
        flat, owned_slices(flat, ff_pieces), up_weight, gain_two, (2, ff, ff)
    )
    qkv_grad, gain_one_grad, out_grad = finish(
        flat, owned_slices(flat, mixed_pieces), qkv_weight, gain_one, (3, part, part)
    )
    return (
        output[None],
        input_grad[None],
        gain_one_grad[:, 0],
        qkv_grad,
        out_grad,
        gain_two_grad[:, 0],
        up_grad,
        down_grad,
    )


def solution(mesh):
    return jax.shard_map(
        quad_device if tuple(mesh.shape.values()) == QUAD_MESH else per_device,
        mesh=mesh,
        in_specs=(
            P("dp", "seq", None),
            P("dp", "seq"),
            P(("dp", "seq")),
            P(("dp", "seq"), None),
            P(("dp", "seq"), None),
            P(("dp", "seq")),
            P(("dp", "seq"), None),
            P(("dp", "seq"), None),
            P("dp", "seq", None),
        ),
        out_specs=(
            P("dp", "seq", None),
            P("dp", "seq", None),
            P(("dp", "seq")),
            P(("dp", "seq"), None),
            P(("dp", "seq"), None),
            P(("dp", "seq")),
            P(("dp", "seq"), None),
            P(("dp", "seq"), None),
        ),
        check_vma=False,
    )
```

```python
import jax
import jax.numpy as jnp
from jax import lax
from jax.experimental import pallas as pl
from jax.experimental.pallas import tpu as pltpu
from jax.sharding import PartitionSpec as P

HEADS = 16
HEAD_DIM = 64
FF = 2624


norm_eps = 1e-05
rope_base = 160000.0
inv_root_two = 0.7071067811865476
inv_root_tau = 0.3989422804014327


def for_sending(array):
    return jax.tree.map(lambda a: a.astype(jnp.bfloat16) if a.dtype == jnp.float32 else a, array)


def normalize(values):
    centre = jnp.mean(values, axis=-1, keepdims=True)
    centred = values - centre
    spread = lax.rsqrt(jnp.mean(centred * centred, axis=-1, keepdims=True) + norm_eps)
    return (centred * spread, spread)


def norm_back(grad_in, normed, spread, gain):
    scaled = grad_in * gain
    gain_term = jnp.sum(grad_in * normed, axis=0)
    centred = (
        scaled
        - jnp.mean(scaled, axis=-1, keepdims=True)
        - normed * jnp.mean(scaled * normed, axis=-1, keepdims=True)
    )
    return (spread * centred, gain_term)


def rope_tables(seq_pos):
    exponent = jnp.arange(0, HEAD_DIM, 2).astype(jnp.float32) / HEAD_DIM
    frequency = rope_base ** (-exponent)
    angles = seq_pos.astype(jnp.float32)[:, None] * frequency[None, :]
    angles = jnp.concatenate([angles, angles], axis=-1)[:, None, :]
    return (jnp.cos(angles), jnp.sin(angles))


def rotate(values, cos_table, sin_table):
    half_dim = values.shape[-1] // 2
    turned = jnp.concatenate([-values[..., half_dim:], values[..., :half_dim]], axis=-1)
    return values * cos_table + turned * sin_table


def rotate_back(grads, cos_table, sin_table):
    half_dim = grads.shape[-1] // 2
    weighted = grads * sin_table
    turned = jnp.concatenate([weighted[..., half_dim:], -weighted[..., :half_dim]], axis=-1)
    return grads * cos_table + turned


def gelu_parts(inner_act):
    normal_cdf = 0.5 * (1.0 + jax.scipy.special.erf(inner_act * inv_root_two))
    slope = normal_cdf + inner_act * jnp.exp(-0.5 * inner_act * inner_act) * inv_root_tau
    return (inner_act * normal_cdf, slope)


def project_heads(attn_in, w_qkv, cos_table, sin_table):
    token_count, model_width = attn_in.shape
    mixed_rows = jnp.dot(attn_in, w_qkv, preferred_element_type=jnp.float32)
    shaped = (token_count, HEADS, HEAD_DIM)
    queries = rotate(mixed_rows[:, :model_width].reshape(shaped), cos_table, sin_table)
    key_rows = rotate(
        mixed_rows[:, model_width : 2 * model_width].reshape(shaped), cos_table, sin_table
    )
    queries = queries.reshape(token_count, model_width).astype(jnp.bfloat16)
    key_rows = key_rows.reshape(token_count, model_width).astype(jnp.bfloat16)
    values = mixed_rows[:, 2 * model_width :].astype(jnp.bfloat16)
    return (queries, key_rows, values)


def attend_forward(q_heads, k_heads, v_heads):
    seq_len, columns = q_heads.shape
    head_count = columns // HEAD_DIM
    block_rows = min(512, seq_len)
    block_count = seq_len // block_rows
    score_scale = HEAD_DIM ** (-0.5)
    k_all = k_heads.reshape(seq_len, head_count, HEAD_DIM)
    v_all = v_heads.reshape(seq_len, head_count, HEAD_DIM)

    def one_block(q_block):
        scores = (
            jnp.einsum("qhd,khd->hqk", q_block, k_all, preferred_element_type=jnp.float32)
            * score_scale
        )
        row_peak = jnp.max(scores, axis=-1, keepdims=True)
        exp_scores = jnp.exp(scores - row_peak)
        totals = jnp.sum(exp_scores, axis=-1, keepdims=True)
        prob_rows = (exp_scores / totals).astype(jnp.bfloat16)
        attended = jnp.einsum("hqk,khd->qhd", prob_rows, v_all, preferred_element_type=jnp.float32)
        return (attended.astype(jnp.bfloat16), row_peak[..., 0] + jnp.log(totals[..., 0]))

    attended, log_totals = lax.map(
        one_block, q_heads.reshape(block_count, block_rows, head_count, HEAD_DIM)
    )
    return (attended.reshape(seq_len, columns), log_totals)


def attend_backward(q_heads, k_heads, v_heads, d_heads, log_totals):
    seq_len, columns = q_heads.shape
    head_count = columns // HEAD_DIM
    block_rows = min(512, seq_len)
    block_count = seq_len // block_rows
    score_scale = HEAD_DIM ** (-0.5)
    k_all = k_heads.reshape(seq_len, head_count, HEAD_DIM)
    v_all = v_heads.reshape(seq_len, head_count, HEAD_DIM)
    q_blocks = q_heads.reshape(block_count, block_rows, head_count, HEAD_DIM)
    d_blocks = d_heads.reshape(block_count, block_rows, head_count, HEAD_DIM)

    def one_block(carry, item):
        key_acc, value_acc = carry
        q_block, d_block, lse_block = item
        scores = (
            jnp.einsum("qhd,khd->hqk", q_block, k_all, preferred_element_type=jnp.float32)
            * score_scale
        )
        prob_rows = jnp.exp(scores - lse_block[..., None])
        value_acc = value_acc + jnp.einsum(
            "hqk,qhd->khd",
            prob_rows.astype(jnp.bfloat16),
            d_block,
            preferred_element_type=jnp.float32,
        )
        d_probs = jnp.einsum("qhd,khd->hqk", d_block, v_all, preferred_element_type=jnp.float32)
        d_scores = (
            prob_rows * (d_probs - jnp.sum(prob_rows * d_probs, axis=-1, keepdims=True))
        ).astype(jnp.bfloat16)
        d_query = (
            jnp.einsum("hqk,khd->qhd", d_scores, k_all, preferred_element_type=jnp.float32)
            * score_scale
        )
        key_acc = (
            key_acc
            + jnp.einsum("hqk,qhd->khd", d_scores, q_block, preferred_element_type=jnp.float32)
            * score_scale
        )
        return ((key_acc, value_acc), d_query.astype(jnp.bfloat16))

    empty_acc = jnp.zeros((seq_len, head_count, HEAD_DIM), jnp.float32)
    (key_acc, value_acc), d_query = lax.scan(
        one_block, (empty_acc, empty_acc), (q_blocks, d_blocks, log_totals)
    )
    d_q = d_query.reshape(seq_len, columns)
    d_k = key_acc.astype(jnp.bfloat16).reshape(seq_len, columns)
    d_v = value_acc.astype(jnp.bfloat16).reshape(seq_len, columns)
    return (d_q, d_k, d_v)


def add_sources(received):
    return tuple((jnp.sum(piece, axis=0) for piece in received))


def per_device(
    inputs,
    positions,
    attn_gain,
    qkv_weight,
    attn_out_weight,
    mlp_gain,
    up_weight,
    down_weight,
    cotangent,
):
    layer = (
        lax.all_gather(attn_gain, ("dp", "seq"), axis=0, tiled=True),
        lax.all_gather(qkv_weight, ("dp", "seq"), axis=0, tiled=True),
        lax.all_gather(attn_out_weight, ("dp", "seq"), axis=0, tiled=True),
        lax.all_gather(mlp_gain, ("dp", "seq"), axis=0, tiled=True),
        lax.all_gather(up_weight, ("dp", "seq"), axis=0, tiled=True),
        lax.all_gather(down_weight, ("dp", "seq"), axis=0, tiled=True),
    )
    gain_one, w_qkv, w_out, gain_two, w_up, w_down = layer
    token_count = inputs.shape[1]
    resid_in = inputs[0].astype(jnp.float32)
    cos_table, sin_table = rope_tables(positions[0])
    normed_one, spread_one = normalize(resid_in)
    attn_in = (normed_one * gain_one.astype(jnp.float32)).astype(jnp.bfloat16)
    queries, key_rows, values = project_heads(attn_in, w_qkv, cos_table, sin_table)
    q_heads, k_heads, v_heads = (
        lax.all_to_all(queries, "seq", split_axis=1, concat_axis=0, tiled=True),
        lax.all_to_all(key_rows, "seq", split_axis=1, concat_axis=0, tiled=True),
        lax.all_to_all(values, "seq", split_axis=1, concat_axis=0, tiled=True),
    )
    attended_heads, log_totals = attend_forward(q_heads, k_heads, v_heads)
    attended = lax.all_to_all(attended_heads, "seq", split_axis=0, concat_axis=1, tiled=True)
    resid = resid_in + jnp.dot(attended, w_out, preferred_element_type=jnp.float32)
    normed_two, spread_two = normalize(resid)
    mlp_in = (normed_two * gain_two.astype(jnp.float32)).astype(jnp.bfloat16)
    up_rows = jnp.dot(mlp_in, w_up, preferred_element_type=jnp.float32)
    inner_act = up_rows[:, :FF]
    gate_act = up_rows[:, FF:]
    gelu_val, gelu_slope = gelu_parts(inner_act)
    hidden = (gelu_val * gate_act).astype(jnp.bfloat16)
    output = resid + jnp.einsum("tf,df->td", hidden, w_down, preferred_element_type=jnp.float32)
    layer_back = (
        lax.all_gather(attn_gain, ("dp", "seq"), axis=0, tiled=True),
        lax.all_gather(qkv_weight, ("dp", "seq"), axis=0, tiled=True),
        lax.all_gather(attn_out_weight, ("dp", "seq"), axis=0, tiled=True),
        lax.all_gather(mlp_gain, ("dp", "seq"), axis=0, tiled=True),
        lax.all_gather(up_weight, ("dp", "seq"), axis=0, tiled=True),
        lax.all_gather(down_weight, ("dp", "seq"), axis=0, tiled=True),
    )
    gain_one, w_qkv, w_out, gain_two, w_up, w_down = layer_back
    d_out = cotangent[0]
    down_grad = jnp.einsum("td,tf->df", d_out, hidden, preferred_element_type=jnp.float32)
    d_hidden = jnp.dot(d_out, w_down, preferred_element_type=jnp.float32)
    d_up = jnp.concatenate([d_hidden * gate_act * gelu_slope, d_hidden * gelu_val], axis=1).astype(
        jnp.bfloat16
    )
    up_grad = jnp.einsum("tk,tn->kn", mlp_in, d_up, preferred_element_type=jnp.float32)
    d_mlp_in = jnp.einsum("tn,kn->tk", d_up, w_up, preferred_element_type=jnp.float32)
    d_norm_two, gain_two_grad = norm_back(
        d_mlp_in, normed_two, spread_two, gain_two.astype(jnp.float32)
    )
    d_resid = d_out.astype(jnp.float32) + d_norm_two
    d_resid_low = d_resid.astype(jnp.bfloat16)
    out_grad = jnp.einsum("tk,tn->kn", attended, d_resid_low, preferred_element_type=jnp.float32)
    d_attended = jnp.einsum(
        "tn,kn->tk", d_resid_low, w_out, preferred_element_type=jnp.float32
    ).astype(jnp.bfloat16)
    d_heads = lax.all_to_all(d_attended, "seq", split_axis=1, concat_axis=0, tiled=True)
    queries, key_rows, values = project_heads(attn_in, w_qkv, cos_table, sin_table)
    head_inputs = (
        lax.all_to_all(queries, "seq", split_axis=1, concat_axis=0, tiled=True),
        lax.all_to_all(key_rows, "seq", split_axis=1, concat_axis=0, tiled=True),
        lax.all_to_all(values, "seq", split_axis=1, concat_axis=0, tiled=True),
    )
    d_q, d_k, d_v = attend_backward(
        head_inputs[0], head_inputs[1], head_inputs[2], d_heads, log_totals
    )
    dq_rows, dk_rows, dv_rows = (
        lax.all_to_all(d_q, "seq", split_axis=0, concat_axis=1, tiled=True),
        lax.all_to_all(d_k, "seq", split_axis=0, concat_axis=1, tiled=True),
        lax.all_to_all(d_v, "seq", split_axis=0, concat_axis=1, tiled=True),
    )
    shaped = (token_count, HEADS, HEAD_DIM)
    dq_pre = rotate_back(dq_rows.astype(jnp.float32).reshape(shaped), cos_table, sin_table).reshape(
        token_count, -1
    )
    dk_pre = rotate_back(dk_rows.astype(jnp.float32).reshape(shaped), cos_table, sin_table).reshape(
        token_count, -1
    )
    d_mixed = jnp.concatenate(
        [dq_pre.astype(jnp.bfloat16), dk_pre.astype(jnp.bfloat16), dv_rows], axis=1
    )
    qkv_grad = jnp.einsum("tk,tn->kn", attn_in, d_mixed, preferred_element_type=jnp.float32)
    d_attn_in = jnp.einsum("tn,kn->tk", d_mixed, w_qkv, preferred_element_type=jnp.float32)
    d_norm_one, gain_one_grad = norm_back(
        d_attn_in, normed_one, spread_one, gain_one.astype(jnp.float32)
    )
    input_grad = (d_resid + d_norm_one).astype(jnp.bfloat16)
    all_sent = (
        lax.all_to_all(
            gain_one_grad[None].astype(jnp.bfloat16), "dp", split_axis=1, concat_axis=0, tiled=True
        ).astype(jnp.float32),
        lax.all_to_all(
            qkv_grad[None].astype(jnp.bfloat16), "dp", split_axis=1, concat_axis=0, tiled=True
        ).astype(jnp.float32),
        lax.all_to_all(
            out_grad[None].astype(jnp.bfloat16), "dp", split_axis=1, concat_axis=0, tiled=True
        ).astype(jnp.float32),
        lax.all_to_all(
            gain_two_grad[None].astype(jnp.bfloat16), "dp", split_axis=1, concat_axis=0, tiled=True
        ).astype(jnp.float32),
        lax.all_to_all(
            up_grad[None].astype(jnp.bfloat16), "dp", split_axis=1, concat_axis=0, tiled=True
        ).astype(jnp.float32),
        lax.all_to_all(
            down_grad[None].astype(jnp.bfloat16), "dp", split_axis=1, concat_axis=0, tiled=True
        ).astype(jnp.float32),
    )
    grads = jax.tree.map(
        lambda part: part.astype(jnp.float32),
        lax.psum_scatter(
            for_sending(add_sources(all_sent)), "seq", scatter_dimension=0, tiled=True
        ),
    )
    return (
        output.astype(jnp.bfloat16)[None],
        input_grad[None],
        grads[0],
        grads[1],
        grads[2],
        grads[3],
        grads[4],
        grads[5],
    )


QUAD_MESH = (8, 4)
FLAT = ("y", "x", "c", "zh", "zl")
LOW, WIDE = jnp.bfloat16, jnp.float32


def pairs_of(step):
    found = []
    for dp in range(8):
        for seq in range(4):
            place = (dp // 4, dp // 2 % 2, dp % 2, seq // 2, seq % 2)
            target = step(*place)
            if target is not None:
                y, x, c, zh, zl = target
                found.append((dp * 4 + seq, (4 * y + 2 * x + c) * 4 + 2 * zh + zl))
    return found


TO_X = pairs_of(lambda y, x, c, zh, zl: (y, 1 - x, c, zh, zl))
TO_Y = pairs_of(lambda y, x, c, zh, zl: (1 - y, x, c, zh, zl))
TO_XY = pairs_of(lambda y, x, c, zh, zl: (1 - y, 1 - x, c, zh, zl))
TO_CORE = pairs_of(lambda y, x, c, zh, zl: (y, x, 1 - c, zh, zl))
TO_ZH = pairs_of(lambda y, x, c, zh, zl: (y, x, c, 1 - zh, zl))
TO_ZL = pairs_of(lambda y, x, c, zh, zl: (y, x, c, zh, 1 - zl))
TO_FAR = pairs_of(lambda y, x, c, zh, zl: (y, x, 1 - c, zh, 1 - zl))
TO_HOME = pairs_of(lambda y, x, c, zh, zl: (y, x, zh, c, zl))
ENTER = pairs_of(
    lambda y, x, c, zh, zl: (y, x, c, zh, 1 - zl) if c == zh else (y, x, zh, c, zl)
)
ENTER_MOVED = pairs_of(lambda y, x, c, zh, zl: None if c == zh else (y, x, c, zh, 1 - zl))


class Order(list):
    pass


def send(array, pairs):
    return lax.ppermute(array, FLAT, pairs)


def after(order, array):
    return lax.optimization_barrier((array, order[0]))[0]


def wait(order, *arrays):
    order[0] = lax.optimization_barrier((order[0], *arrays))[0]


def lanes(size):
    return -(-size // 128) * 128


def core_of(flat):
    return flat >> 2 & 1


def half_of(flat):
    return flat >> 1 & 1


def group_of(flat):
    return 2 * core_of(flat) + (flat & 1)


def square_of(flat):
    return flat >> 3


def mm(left, right):
    return lax.dot_general(left, right, (((1,), (0,)), ((), ())), preferred_element_type=WIDE)


def mm_t(left, right):
    return lax.dot_general(left, right, (((1,), (1,)), ((), ())), preferred_element_type=WIDE)


def t_mm(left, right):
    return lax.dot_general(left, right, (((0,), (0,)), ((), ())), preferred_element_type=WIDE)


def window(index, size):
    return pl.ds(pl.multiple_of(index * size, size), size)


def whole(array):
    rank = len(array.shape)
    return (array, array.shape, lambda *_: (0,) * rank)


def by_rows(array, rows, step=lambda b: b):
    return (array, (rows,) + array.shape[1:], lambda b, f: (step(b),) + (0,) * (len(array.shape) - 1))


def run(body, order, grid, ins, outs, scratch=(), flops=0):
    moved = sum(a.size * a.dtype.itemsize for a, _, _ in ins)
    moved += sum(a.size * a.dtype.itemsize for a, _, _ in outs)
    made = pl.pallas_call(
        body,
        grid_spec=pltpu.PrefetchScalarGridSpec(
            num_scalar_prefetch=1,
            grid=grid,
            in_specs=[pl.BlockSpec(block, index) for _, block, index in ins],
            out_specs=[pl.BlockSpec(block, index) for _, block, index in outs],
            scratch_shapes=list(scratch),
        ),
        out_shape=[a for a, _, _ in outs],
        cost_estimate=pl.CostEstimate(flops=flops // 100, bytes_accessed=moved // 100, transcendentals=0),
    )(order[0], *[a for a, _, _ in ins])
    order[0], _ = lax.optimization_barrier((order[0], made[0]))
    return made


def spans(pieces):
    rows = pieces[0].shape[0]
    return [(0, 0, rows), (1, 0, rows), (2, 0, rows), (3, 0, rows // 2), (3, rows // 2, rows // 2)]


def span_of(square, span, rows):
    index, first, count = span
    return pl.ds(pl.multiple_of((square ^ index) * rows + first, count), count)


def shape_of(*dims, dtype=LOW):
    return jax.ShapeDtypeStruct(dims, dtype)


def column_of(row):
    size = row.shape[1]
    down = lax.broadcasted_iota(jnp.int32, (size, size), 0)
    across = lax.broadcasted_iota(jnp.int32, (size, size), 1)
    return jnp.sum(jnp.where(down == across, row, 0.0), axis=1, keepdims=True)


def row_of(column):
    size = column.shape[0]
    down = lax.broadcasted_iota(jnp.int32, (size, size), 0)
    across = lax.broadcasted_iota(jnp.int32, (size, size), 1)
    return jnp.sum(jnp.where(down == across, column, 0.0), axis=0, keepdims=True)


def normed_of(x):
    centred = x - jnp.mean(x, axis=-1, keepdims=True)
    spread = lax.rsqrt(jnp.mean(centred * centred, axis=-1, keepdims=True) + norm_eps)
    return centred * spread, spread


def split_slices(order, scaled, plain, gain, parts):
    rows, part, rest = scaled.shape[0], scaled.shape[1] // (4 * parts), plain.shape[1] // 4
    out = shape_of(rows, lanes(parts * part + rest))

    def body(flat_ref, scaled_ref, plain_ref, gain_ref, *refs):
        held = refs[4]
        scale = column_of(gain_ref[...].astype(WIDE))
        for s in range(4):
            for t in range(parts):
                cols = scaled_ref[:, (4 * t + s) * part : (4 * t + s + 1) * part].astype(WIDE)
                held[s, :, t * part : (t + 1) * part] = (cols * scale).astype(LOW)
            held[s, :, parts * part : parts * part + rest] = plain_ref[
                :, s * rest : (s + 1) * rest
            ]
        for i in range(4):
            refs[i][...] = held[group_of(flat_ref[0]) ^ i]

    return run(
        body, order, (1,), [whole(a) for a in (scaled, plain, gain)], [whole(out)] * 4,
        [pltpu.VMEM((4, *out.shape), LOW)],
    )


def share_slices(slices):
    return [slices[0]] + [
        send(slices[i], pairs) for i, pairs in ((1, TO_ZL), (2, TO_CORE), (3, TO_FAR))
    ]


def quad_rows(order, parts):
    def body(flat_ref, *refs):
        for i in range(4):
            refs[4][group_of(flat_ref[0]) ^ i] = refs[i][...]

    out = shape_of(4, *parts[0].shape)
    return run(body, order, (1,), [whole(p) for p in parts], [whole(out)])[0]


def line_rows(order, near, far):
    _, rows, width = near.shape
    near = near.reshape(2, 2 * rows, width)
    far = far.reshape(2, 2 * rows, width)

    def body(flat_ref, near_ref, far_ref, out_ref):
        half = half_of(flat_ref[0])
        for c in range(2):
            out_ref[c, half] = near_ref[c]
            out_ref[c, 1 - half] = far_ref[c]

    out = run(
        body, order, (1,), [whole(near), whole(far)], [whole(shape_of(2, 2, 2 * rows, width))]
    )[0]
    return out.reshape(8 * rows, width)


def join_tokens(order, parts, rows):
    height, width = parts[0].shape
    extra = height - rows

    def body(flat_ref, block, first, second, core_block, core_first, core_second, *outs):
        home = core_of(flat_ref[0]) == half_of(flat_ref[0])
        here = (block, first, core_first, core_second)
        moved = (first, second, core_block, core_first)
        for k in range(4):
            for flag, source in ((home, here[k]), (jnp.logical_not(home), moved[k])):

                @pl.when(jnp.logical_and(pl.program_id(0) == k, flag))
                def _(source=source):
                    def step(r, carry):
                        outs[0][window(r, 32), :] = source[window(r, 32), :]
                        return carry

                    lax.fori_loop(0, rows // 32, step, 0)
                    if extra:
                        outs[1][...] = source[rows:, :]

    made = [shape_of(4 * rows, width)] + ([shape_of(4 * extra, width)] if extra else [])
    return run(
        body, order, (4,), [whole(a) for a in parts],
        [by_rows(m, m.shape[0] // 4) for m in made],
    )


def rope_lanes(seq_pos):
    exponent = jnp.arange(0, HEAD_DIM, 2).astype(WIDE) / HEAD_DIM
    angles = seq_pos[:, None] * (rope_base ** (-exponent))[None, :]
    cos_half, sin_half = jnp.cos(angles), jnp.sin(angles)
    return (
        jnp.concatenate([cos_half] * 4, axis=1),
        jnp.concatenate([-sin_half, sin_half] * 2, axis=1),
    )


def turned(v):
    half = HEAD_DIM // 2
    lane = lax.broadcasted_iota(jnp.int32, v.shape, 1)
    return jnp.where(
        lane % HEAD_DIM < half, pltpu.roll(v, 2 * HEAD_DIM - half, 1), pltpu.roll(v, half, 1)
    )


def project(order, x, pieces, cos_table, sin_table):
    tokens, width = x.shape
    piece, columns = pieces[0].shape[0], 3 * width // 4
    rows = tokens // 4

    def body(flat_ref, x_ref, *refs):
        weights, (cos_ref, sin_ref, n_ref, mix_ref) = refs[:5], refs[5:]
        n_ref[...] = normed_of(x_ref[...].astype(WIDE))[0].astype(LOW)
        square = square_of(flat_ref[0])
        mixed = sum(
            mm(n_ref[:, span_of(square, span, piece)], w[:, :columns])
            for span, w in zip(spans(pieces), weights)
        )
        turned_to = 2 * columns // 3
        for t in range(0, turned_to, 128):
            v = mixed[:, t : t + 128]
            mix_ref[:, t : t + 128] = (v * cos_ref[...] + turned(v) * sin_ref[...]).astype(LOW)
        mix_ref[:, turned_to:] = mixed[:, turned_to:].astype(LOW)

    return run(
        body, order, (4,),
        [by_rows(x, rows)] + [whole(p) for p in pieces]
        + [by_rows(cos_table, rows), by_rows(sin_table, rows)],
        [by_rows(shape_of(tokens, width), rows), by_rows(shape_of(tokens, columns), rows)],
        flops=2 * tokens * width * columns,
    )


def attend(order, mix):
    tokens, columns = mix.shape
    part = columns // 3
    rows = tokens // 4
    scale = HEAD_DIM ** (-0.5)

    def body(flat_ref, q_ref, k_ref, v_ref, out_ref, log_ref):
        lane = lax.broadcasted_iota(jnp.int32, (rows, part), 1) // HEAD_DIM
        log_lane = lax.broadcasted_iota(jnp.int32, (rows, 128), 1)
        total = jnp.zeros((rows, part), WIDE)
        logs = jnp.zeros((rows, 128), WIDE)
        queries = q_ref[...].astype(WIDE) * scale
        for h in range(part // HEAD_DIM):
            q_head = jnp.where(lane == h, queries, 0.0).astype(LOW)
            scores = mm_t(q_head, k_ref[...])
            peak = jnp.max(scores, axis=-1, keepdims=True)
            powers = jnp.exp(scores - peak)
            mass = jnp.sum(powers, axis=-1, keepdims=True)
            probs = (powers * (1.0 / mass)).astype(LOW)
            total = jnp.where(lane == h, mm(probs, v_ref[...]), total)
            logs = jnp.where(log_lane == h, peak + jnp.log(mass), logs)
        out_ref[...] = total.astype(LOW)
        log_ref[...] = logs

    return run(
        body, order, (4,),
        [
            (mix, (rows, part), lambda b, f: (b, 0)),
            (mix, (tokens, part), lambda b, f: (0, 1)),
            (mix, (tokens, part), lambda b, f: (0, 2)),
        ],
        [by_rows(shape_of(tokens, part), rows), by_rows(shape_of(tokens, 128, dtype=WIDE), rows)],
        flops=16 * tokens * tokens * part,
    )


def token_parts(arrays, rows):
    return [by_rows(a, rows, lambda b, i=i: b ^ i) for i, a in enumerate(arrays)]


def join_heads(order, x, heads, columns):
    tokens, width = x.shape
    rows, part = tokens // 4, width // 4

    def body(flat_ref, x_ref, *refs):
        parts, weights, (n_ref, own_ref, held) = refs[:4], refs[4:8], refs[8:]
        group, square = group_of(flat_ref[0]), square_of(flat_ref[0])
        for j in range(4):
            cols = window(group ^ j, part)
            held[:, cols] = x_ref[:, cols].astype(WIDE) + sum(
                mm(parts[i][...], weights[j][window(group ^ i ^ square, part), :])
                for i in range(4)
            )
        resid = held[...]
        n_ref[...] = normed_of(resid)[0].astype(LOW)

        @pl.when(pl.program_id(0) == 0)
        def _():
            own_ref[...] = held[...]

    return run(
        body, order, (4,),
        [by_rows(x, rows)] + token_parts(heads, rows) + [whole(w) for w in columns],
        [by_rows(shape_of(tokens, width), rows), whole(shape_of(rows, width, dtype=WIDE))],
        [pltpu.VMEM((rows, width), WIDE)],
        flops=2 * tokens * width * width,
    )


def feed(order, normed, cot, pieces):
    tokens, width = normed.shape
    piece, ff = pieces[0].shape[0], FF // 4
    rows = tokens // 4

    def body(flat_ref, n_ref, cot_ref, *refs):
        weights, (h_ref, d_ref) = refs[:5], refs[5:]
        square = square_of(flat_ref[0])
        cols = [span_of(square, span, piece) for span in spans(pieces)]
        wide = sum(mm(n_ref[:, at], w[:, : 2 * ff]) for at, w in zip(cols, weights))
        d_hidden = sum(mm(cot_ref[:, at], w[:, 2 * ff : 3 * ff]) for at, w in zip(cols, weights))
        inner, gate = wide[:, :ff], wide[:, ff:]
        cdf = 0.5 * (1.0 + lax.erf(inner * inv_root_two))
        slope = cdf + inner * jnp.exp(-0.5 * inner * inner) * inv_root_tau
        bent = inner * cdf
        h_ref[...] = (bent * gate).astype(LOW)
        d_ref[:, :ff] = (d_hidden * gate * slope).astype(LOW)
        d_ref[:, ff:] = (d_hidden * bent).astype(LOW)

    return run(
        body, order, (4,),
        [by_rows(normed, rows), by_rows(cot, rows)] + [whole(w) for w in pieces],
        [by_rows(shape_of(tokens, ff), rows), by_rows(shape_of(tokens, 2 * ff), rows)],
        flops=6 * tokens * width * ff,
    )


def back_half(order, grads, pieces, far):
    tokens = grads[0][0].shape[0]
    piece = pieces[0].shape[0]
    rows, width, count = tokens // 2, 4 * piece, len(grads)
    out = shape_of(rows, width, dtype=LOW if far else WIDE)

    def body(flat_ref, *refs):
        arrays, weights, out_ref = refs[:count], refs[count : count + 5], refs[count + 5]
        square = square_of(flat_ref[0])
        for span, w in zip(spans(pieces), weights):
            out_ref[:, span_of(square, span, piece)] = sum(
                mm_t(a[...], w[:, at : at + a.shape[1]]) for a, (_, at) in zip(arrays, grads)
            ).astype(out.dtype)

    return run(
        body, order, (1,),
        [by_rows(a, rows, lambda b: int(far)) for a, _ in grads] + [whole(p) for p in pieces],
        [whole(out)],
        flops=tokens * width * sum(a.shape[1] for a, _ in grads),
    )[0]


def norm_pull(order, x, terms, base, keep):
    rows, width = base.shape[0] // (4 if keep else 1), base.shape[1]
    step = rows // 4

    def body(flat_ref, x_ref, a_ref, b_ref, c_ref, base_ref, *outs):
        normed, spread = normed_of(x_ref[...].astype(WIDE))
        scaled = a_ref[...] + b_ref[...].astype(WIDE) + c_ref[...].astype(WIDE)
        grad = base_ref[...].astype(WIDE) + spread * (
            scaled
            - jnp.mean(scaled, axis=-1, keepdims=True)
            - normed * jnp.mean(scaled * normed, axis=-1, keepdims=True)
        )
        outs[0][...] = grad.astype(LOW)
        if keep:
            outs[1][...] = grad

    outs = [shape_of(rows, width)] + ([shape_of(rows, width, dtype=WIDE)] if keep else [])
    return run(
        body, order, (4,), [by_rows(a, step) for a in (x, *terms, base)],
        [by_rows(o, step) for o in outs],
    )


def feed_grads(order, normed, cot, d_up, hidden):
    tokens, width = normed.shape
    rows, piece = tokens // 4, width // 4
    ff = hidden.shape[1]
    out = shape_of(4, piece, lanes(3 * ff))

    def body(flat_ref, n_ref, cot_ref, d_ref, h_ref, out_ref, held):
        @pl.when(pl.program_id(0) == 0)
        def _():
            held[...] = jnp.zeros_like(held)

        for i in range(4):
            cols = slice(i * piece, (i + 1) * piece)
            held[i, :, : 2 * ff] += t_mm(n_ref[:, cols], d_ref[...])
            held[i, :, 2 * ff : 3 * ff] += t_mm(cot_ref[:, cols], h_ref[...])

        @pl.when(pl.program_id(0) == 3)
        def _():
            out_ref[...] = held[...].astype(LOW)

    return run(
        body, order, (4,), [by_rows(a, rows) for a in (normed, cot, d_up, hidden)],
        [whole(out)], [pltpu.VMEM(out.shape, WIDE)],
        flops=6 * tokens * width * ff,
    )[0]


def heads_back(order, d_all, heads, columns):
    rows, width = d_all[0].shape
    part = width // 4

    def body(flat_ref, *refs):
        blocks, parts, weights = refs[:4], refs[4:8], refs[8:12]
        d_ref, grad_ref, block, held, total = refs[12:]
        group, square = group_of(flat_ref[0]), square_of(flat_ref[0])
        at = pl.program_id(0)
        for k in range(4):

            @pl.when(at == k)
            def _(source=blocks[k]):
                def step(r, carry):
                    block[window(r, 32), :] = source[window(r, 32), :]
                    return carry

                lax.fori_loop(0, rows // 32, step, 0)

            held[k] = parts[k][...]

        @pl.when(at == 0)
        def _():
            total[...] = jnp.zeros_like(total)

        d_ref[...] = sum(
            mm_t(block[:, window(group ^ j, part)], weights[j][window(group ^ square, part), :])
            for j in range(4)
        ).astype(LOW)
        mine = block[:, window(group, part)]
        for i in range(4):
            total[i] += t_mm(held[group ^ square ^ i], mine)

        @pl.when(at == 3)
        def _():
            grad_ref[...] = total[...].astype(LOW)

    return run(
        body, order, (4,),
        [whole(d) for d in d_all] + token_parts(heads, rows) + [whole(w) for w in columns],
        [by_rows(shape_of(4 * rows, part), rows), whole(shape_of(4, part, part))],
        [
            pltpu.VMEM((rows, width), LOW),
            pltpu.VMEM((4, rows, part), LOW),
            pltpu.VMEM((4, part, part), WIDE),
        ],
        flops=4 * 4 * rows * width * part,
    )


def attend_back(order, mix, attended, d_attended, logs, cos_table, sin_table):
    tokens, columns = mix.shape
    part = columns // 3
    rows = tokens // 4
    scale = HEAD_DIM ** (-0.5)
    heads = part // HEAD_DIM

    def rotated(grad, cos, sin):
        halves = [grad[:, t : t + 128] for t in range(0, part, 128)]
        return jnp.concatenate([v * cos - turned(v) * sin for v in halves], axis=1).astype(LOW)

    def body(flat_ref, q_ref, k_ref, v_ref, o_ref, d_ref, log_ref, cos_ref, sin_ref, *refs):
        dq_ref, dk_ref, dv_ref, k_total, v_total = refs
        at = pl.program_id(0)

        @pl.when(at == 0)
        def _():
            k_total[...] = jnp.zeros_like(k_total)
            v_total[...] = jnp.zeros_like(v_total)

        lane = lax.broadcasted_iota(jnp.int32, (rows, part), 1) // HEAD_DIM
        queries = q_ref[...].astype(WIDE) * scale
        grads = d_ref[...].astype(WIDE)
        chosen = lax.broadcasted_iota(jnp.int32, (8, part), 0) == (
            lax.broadcasted_iota(jnp.int32, (8, part), 1) // HEAD_DIM
        )
        deltas = lax.dot_general(
            chosen.astype(WIDE), grads * o_ref[...].astype(WIDE), (((1,), (1,)), ((), ())),
            precision=lax.Precision.HIGHEST, preferred_element_type=WIDE,
        )
        d_query = jnp.zeros((rows, part), WIDE)
        for h in range(heads):
            q_head = jnp.where(lane == h, queries, 0.0).astype(LOW)
            d_head = jnp.where(lane == h, grads, 0.0).astype(LOW)
            probs = jnp.exp(mm_t(k_ref[...], q_head) - log_ref[h : h + 1, :])
            d_probs = mm_t(v_ref[...], d_head)
            d_scores = (probs * (d_probs - deltas[h : h + 1, :])).astype(LOW)
            v_total[...] += mm(probs.astype(LOW), d_head)
            k_total[...] += mm(d_scores, q_head)
            d_query = jnp.where(lane == h, t_mm(d_scores, k_ref[...]), d_query)
        here = window(at, rows)
        dq_ref[...] = rotated(d_query * scale, cos_ref[here, :], sin_ref[here, :])

        @pl.when(at == 3)
        def _():
            dk_ref[...] = rotated(k_total[...], cos_ref[...], sin_ref[...])
            dv_ref[...] = v_total[...].astype(LOW)

    out = shape_of(tokens, part)
    return run(
        body, order, (4,),
        [
            (mix, (rows, part), lambda b, f: (b, 0)),
            (mix, (tokens, part), lambda b, f: (0, 1)),
            (mix, (tokens, part), lambda b, f: (0, 2)),
            by_rows(attended, rows),
            by_rows(d_attended, rows),
            (logs, (8, rows), lambda b, f: (0, b)),
            whole(cos_table),
            whole(sin_table),
        ],
        [by_rows(out, rows), whole(out), whole(out)],
        [pltpu.VMEM((tokens, part), WIDE)] * 2,
        flops=40 * tokens * tokens * part,
    )


def mixed_grads(order, normed, d_mixed, out_grad):
    tokens, width = normed.shape
    rows, piece = tokens // 4, width // 4
    part = d_mixed[0].shape[1]

    def body(flat_ref, n_ref, *refs):
        grads, out_ref, outs, held = refs[:3], refs[3], refs[4:8], refs[8]
        square = square_of(flat_ref[0])

        @pl.when(pl.program_id(0) == 0)
        def _():
            held[...] = jnp.zeros_like(held)

        for i in range(4):
            cols = n_ref[:, window(square ^ i, piece)]
            for t in range(3):
                held[i, :, t * part : (t + 1) * part] += t_mm(cols, grads[t][...])

        @pl.when(pl.program_id(0) == 3)
        def _():
            for i in range(4):
                outs[i][:, : 3 * part] = held[i].astype(LOW)
                outs[i][:, 3 * part :] = out_ref[i]

    return run(
        body, order, (4,),
        [by_rows(normed, rows)] + [by_rows(d, rows) for d in d_mixed] + [whole(out_grad)],
        [whole(shape_of(piece, 4 * part))] * 4, [pltpu.VMEM((4, piece, 3 * part), WIDE)],
        flops=6 * tokens * width * part,
    )


def share_pieces(pieces):
    return [pieces[0]] + [
        send(pieces[i], pairs) for i, pairs in ((1, TO_X), (2, TO_Y), (3, TO_XY))
    ]


def fold(order, terms):
    high, width = terms[0].shape[1:]
    rows = high // 4
    terms = [t.reshape(-1, 2, 2, rows, width) for t in terms]

    def body(flat_ref, *refs):
        ins, (kept_ref, sent_ref) = refs[:-2], refs[-2:]
        half = half_of(flat_ref[0])

        def total(at):
            return sum(r[k, 0, at].astype(WIDE) for r in ins for k in range(r.shape[0]))

        kept_ref[0] = total(half)
        sent_ref[0] = total(1 - half).astype(LOW)

    return run(
        body, order, (2,),
        [
            (t, (t.shape[0], 1) + t.shape[2:], lambda b, f: (0, b, 0, 0, 0))
            for t in terms
        ],
        [by_rows(shape_of(2, rows, width, dtype=WIDE), 1), by_rows(shape_of(2, rows, width), 1)],
    )


def split_rows(order, kept, received):
    _, high, width = kept.shape
    rows = high // 2
    kept, received = kept.reshape(4, rows, width), received.reshape(4, rows, width)

    def body(flat_ref, kept_ref, received_ref, *outs):
        for i in range(4):
            at = group_of(flat_ref[0]) ^ i
            outs[i][...] = (kept_ref[at] + received_ref[at].astype(WIDE)).astype(LOW)

    return run(
        body, order, (1,), [whole(kept), whole(received)], [whole(shape_of(rows, width))] * 4
    )


def finish(order, slices, weight, gain, sizes):
    rows, width = slices[0].shape
    count, part, rest = sizes

    def body(flat_ref, *refs):
        w_ref, gain_ref, scaled_ref, gain_out, plain_ref, held = refs[4:]
        for i in range(4):
            held[group_of(flat_ref[0]) ^ i] = refs[i][...].astype(WIDE)
        total = jnp.zeros((rows, 1), WIDE)
        scale = column_of(gain_ref[...].astype(WIDE))
        for s in range(4):
            for t in range(count):
                at = (4 * t + s) * part
                grad = held[s, :, t * part : (t + 1) * part]
                total += jnp.sum(
                    grad * w_ref[:, at : at + part].astype(WIDE), axis=1, keepdims=True
                )
                scaled_ref[:, at : at + part] = grad * scale
            plain_ref[:, s * rest : (s + 1) * rest] = held[s, :, count * part : count * part + rest]
        gain_out[...] = row_of(total)

    return run(
        body, order, (1,), [whole(a) for a in (*slices, weight, gain)],
        [
            whole(shape_of(*weight.shape, dtype=WIDE)),
            whole(shape_of(1, rows, dtype=WIDE)),
            whole(shape_of(rows, 4 * rest, dtype=WIDE)),
        ],
        [pltpu.VMEM((4, rows, width), WIDE)],
    )


def quad_device(
    inputs,
    positions,
    attn_gain,
    qkv_weight,
    attn_out_weight,
    mlp_gain,
    up_weight,
    down_weight,
    cotangent,
):
    order = Order([lax.axis_index(FLAT).astype(jnp.int32).reshape(1)])
    tokens, width = inputs.shape[1:]
    part, ff = width // 4, FF // 4
    gain_one, gain_two = attn_gain[None], mlp_gain[None]

    one = share_slices(split_slices(order, qkv_weight, attn_out_weight, gain_one, 3))
    pos = positions[0]
    pos_row = jnp.concatenate([pos // 128, pos % 128]).astype(LOW)
    pos_row = jnp.pad(pos_row[None], ((0, 15), (0, width - 2 * tokens)))
    block = jnp.concatenate([inputs[0], pos_row])
    two = split_slices(order, up_weight, down_weight, gain_two, 2)
    first = send(after(order, block), ENTER)
    one = quad_rows(order, one)
    one_far = send(one, TO_ZH)
    two = share_slices([after(order, t) for t in two])
    one = line_rows(order, one, one_far)
    half = one.shape[0] // 2
    one_x, one_y = send(one, TO_X), send(one, TO_Y)
    two = quad_rows(order, two)
    two_far = send(two, TO_ZH)
    second = send(after(order, first), ENTER_MOVED)
    core_first = send(after(order, first), TO_CORE)
    wait(order, core_first, second)
    core_block = send(after(order, block), TO_CORE)
    core_second = send(after(order, second), TO_CORE)
    x, pos_all = join_tokens(
        order, [block, first, second, core_block, core_first, core_second], tokens
    )
    cot_first = send(after(order, cotangent[0]), ENTER)
    one_top = send(one_x[:half], TO_Y)
    one_low = send(one_y[half:], TO_X)
    pos_all = pos_all.reshape(4, 16, width)[:, 0, : 2 * tokens].astype(WIDE)
    pos_all = (pos_all[:, :tokens] * 128.0 + pos_all[:, tokens:]).reshape(4 * tokens)
    cos_table, sin_table = rope_lanes(pos_all)
    one = [one, one_x, one_y, one_top, one_low]

    normed_one, mix = project(order, x, one, cos_table, sin_table)
    w_out = after(order, jnp.concatenate([p[:, 3 * part :] for p in one]))
    w_side = send(w_out, TO_ZL)
    w_core = send(w_out, TO_CORE)
    two = line_rows(order, two, two_far)
    two_x, two_y = send(two, TO_X), send(two, TO_Y)
    attended, logs = attend(order, mix)
    att_side = send(attended, TO_ZL)
    att_core = send(attended, TO_CORE)
    w_far = send(after(order, w_side), TO_CORE)
    w_out = [w_out, w_side, w_core, w_far]
    wait(order, w_far, cot_first)
    cot_second = send(after(order, cot_first), ENTER_MOVED)
    logs = logs[:, :8].T
    wait(order, att_side, logs)
    heads = [attended, att_side, att_core, send(att_side, TO_CORE)]
    normed_two, resid = join_heads(order, x, heads, w_out)

    two_top = send(two_x[:half], TO_Y)
    two_low = send(two_y[half:], TO_X)
    core_block = send(after(order, cotangent[0]), TO_CORE)
    core_first = send(after(order, cot_first), TO_CORE)
    core_second = send(after(order, cot_second), TO_CORE)
    (cot,) = join_tokens(
        order,
        [cotangent[0], cot_first, cot_second, core_block, core_first, core_second],
        tokens,
    )
    two = [two, two_x, two_y, two_top, two_low]
    hidden, d_up = feed(order, normed_two, cot, two)

    def crossed(far):
        return send(far, TO_CORE)

    def side_of(near, far):
        return send((near[tokens:] + far[tokens:].astype(WIDE)).astype(LOW), TO_ZL)

    grads = [(d_up, 0)]
    far = crossed(back_half(order, grads, two, True))
    near = back_half(order, grads, two, False)
    side = side_of(near, far)
    ff_terms = feed_grads(order, normed_two, cot, d_up, hidden)
    d_low, d_resid = norm_pull(order, resid, (near, far, side), cot, True)
    ff_terms = lax.all_to_all(
        after(order, ff_terms), ("y", "x"), split_axis=0, concat_axis=0, tiled=True
    )
    d_side = send(d_low, TO_ZL)
    d_core = send(d_low, TO_CORE)
    grads = [(hidden, 2 * ff)]
    out_far = back_half(order, grads, two, True)
    out_near = back_half(order, grads, two, False)
    d_all = [d_low, d_side, d_core, send(after(order, d_side), TO_CORE)]
    d_attended, out_grad = heads_back(order, d_all, heads, w_out)
    out_far = crossed(after(order, out_far))
    out_side = side_of(out_near, out_far)
    d_mixed = attend_back(order, mix, attended, d_attended, logs, cos_table, sin_table)
    output = resid + out_near[:tokens] + out_far[:tokens].astype(WIDE) + out_side.astype(WIDE)
    output = output.astype(LOW)
    wait(order, output)
    output = send(output, TO_HOME)
    mixed_terms = share_pieces(mixed_grads(order, normed_one, d_mixed, out_grad))
    grads = [(d, t * part) for t, d in enumerate(d_mixed)]
    far = crossed(back_half(order, grads, one, True))
    near = back_half(order, grads, one, False)
    side = side_of(near, far)
    ff_kept, ff_sent = fold(order, [ff_terms])
    wait(order, output)
    ff_sent = send(after(order, ff_sent), TO_ZH)
    (input_grad,) = norm_pull(order, x, (near, far, side), d_resid, False)
    input_grad = send(input_grad, TO_HOME)
    mixed_kept, mixed_sent = fold(order, [t[None] for t in mixed_terms])
    mixed_sent = send(mixed_sent, TO_ZH)
    ff_slices = share_slices(split_rows(order, ff_kept, ff_sent))
    mixed_slices = share_slices(split_rows(order, mixed_kept, mixed_sent))
    up_grad, gain_two_grad, down_grad = finish(
        order, ff_slices, up_weight, gain_two, (2, ff, ff)
    )
    qkv_grad, gain_one_grad, out_grad = finish(
        order, mixed_slices, qkv_weight, gain_one, (3, part, part)
    )
    return (
        output[None],
        input_grad[None],
        gain_one_grad[0],
        qkv_grad,
        out_grad,
        gain_two_grad[0],
        up_grad,
        down_grad,
    )


def solution(mesh):
    dp, seq = "dp", "seq"
    step = per_device
    if tuple(mesh.shape.values()) == QUAD_MESH:
        dp, seq, step = ("y", "x", "c"), ("zh", "zl"), quad_device
        mesh = jax.sharding.Mesh(mesh.devices.reshape(2, 2, 2, 2, 2), FLAT)
        every = FLAT
    else:
        every = (dp, seq)
    rows = P(every, None)
    return jax.shard_map(
        step,
        mesh=mesh,
        in_specs=(
            P(dp, seq, None),
            P(dp, seq),
            P(every),
            rows,
            rows,
            P(every),
            rows,
            rows,
            P(dp, seq, None),
        ),
        out_specs=(
            P(dp, seq, None),
            P(dp, seq, None),
            P(every),
            rows,
            rows,
            P(every),
            rows,
            rows,
        ),
        check_vma=False,
    )
```

```python
import math

import jax
import jax.numpy as jnp
from jax import lax
from jax.experimental import pallas as pl
from jax.experimental.pallas import tpu as pltpu
from jax.sharding import PartitionSpec as P

HEADS = 16
HEAD_DIM = 64
FF = 2624


norm_eps = 1e-05
rope_base = 160000.0
inv_root_two = 0.7071067811865476
inv_root_tau = 0.3989422804014327


def for_sending(array):
    return jax.tree.map(lambda a: a.astype(jnp.bfloat16) if a.dtype == jnp.float32 else a, array)


def normalize(values):
    centre = jnp.mean(values, axis=-1, keepdims=True)
    centred = values - centre
    spread = lax.rsqrt(jnp.mean(centred * centred, axis=-1, keepdims=True) + norm_eps)
    return (centred * spread, spread)


def norm_back(grad_in, normed, spread, gain):
    scaled = grad_in * gain
    gain_term = jnp.sum(grad_in * normed, axis=0)
    centred = (
        scaled
        - jnp.mean(scaled, axis=-1, keepdims=True)
        - normed * jnp.mean(scaled * normed, axis=-1, keepdims=True)
    )
    return (spread * centred, gain_term)


def rope_tables(seq_pos):
    exponent = jnp.arange(0, HEAD_DIM, 2).astype(jnp.float32) / HEAD_DIM
    frequency = rope_base ** (-exponent)
    angles = seq_pos.astype(jnp.float32)[:, None] * frequency[None, :]
    angles = jnp.concatenate([angles, angles], axis=-1)[:, None, :]
    return (jnp.cos(angles), jnp.sin(angles))


def rotate(values, cos_table, sin_table):
    half_dim = values.shape[-1] // 2
    turned = jnp.concatenate([-values[..., half_dim:], values[..., :half_dim]], axis=-1)
    return values * cos_table + turned * sin_table


def rotate_back(grads, cos_table, sin_table):
    half_dim = grads.shape[-1] // 2
    weighted = grads * sin_table
    turned = jnp.concatenate([weighted[..., half_dim:], -weighted[..., :half_dim]], axis=-1)
    return grads * cos_table + turned


def gelu_parts(inner_act):
    normal_cdf = 0.5 * (1.0 + jax.scipy.special.erf(inner_act * inv_root_two))
    slope = normal_cdf + inner_act * jnp.exp(-0.5 * inner_act * inner_act) * inv_root_tau
    return (inner_act * normal_cdf, slope)


def project_heads(attn_in, w_qkv, cos_table, sin_table):
    token_count, model_width = attn_in.shape
    mixed_rows = jnp.dot(attn_in, w_qkv, preferred_element_type=jnp.float32)
    shaped = (token_count, HEADS, HEAD_DIM)
    queries = rotate(mixed_rows[:, :model_width].reshape(shaped), cos_table, sin_table)
    key_rows = rotate(
        mixed_rows[:, model_width : 2 * model_width].reshape(shaped), cos_table, sin_table
    )
    queries = queries.reshape(token_count, model_width).astype(jnp.bfloat16)
    key_rows = key_rows.reshape(token_count, model_width).astype(jnp.bfloat16)
    values = mixed_rows[:, 2 * model_width :].astype(jnp.bfloat16)
    return (queries, key_rows, values)


def attend_forward(q_heads, k_heads, v_heads):
    seq_len, columns = q_heads.shape
    head_count = columns // HEAD_DIM
    block_rows = min(512, seq_len)
    block_count = seq_len // block_rows
    score_scale = HEAD_DIM ** (-0.5)
    k_all = k_heads.reshape(seq_len, head_count, HEAD_DIM)
    v_all = v_heads.reshape(seq_len, head_count, HEAD_DIM)

    def one_block(q_block):
        scores = (
            jnp.einsum("qhd,khd->hqk", q_block, k_all, preferred_element_type=jnp.float32)
            * score_scale
        )
        row_peak = jnp.max(scores, axis=-1, keepdims=True)
        exp_scores = jnp.exp(scores - row_peak)
        totals = jnp.sum(exp_scores, axis=-1, keepdims=True)
        prob_rows = (exp_scores / totals).astype(jnp.bfloat16)
        attended = jnp.einsum("hqk,khd->qhd", prob_rows, v_all, preferred_element_type=jnp.float32)
        return (attended.astype(jnp.bfloat16), row_peak[..., 0] + jnp.log(totals[..., 0]))

    attended, log_totals = lax.map(
        one_block, q_heads.reshape(block_count, block_rows, head_count, HEAD_DIM)
    )
    return (attended.reshape(seq_len, columns), log_totals)


def attend_backward(q_heads, k_heads, v_heads, d_heads, log_totals):
    seq_len, columns = q_heads.shape
    head_count = columns // HEAD_DIM
    block_rows = min(512, seq_len)
    block_count = seq_len // block_rows
    score_scale = HEAD_DIM ** (-0.5)
    k_all = k_heads.reshape(seq_len, head_count, HEAD_DIM)
    v_all = v_heads.reshape(seq_len, head_count, HEAD_DIM)
    q_blocks = q_heads.reshape(block_count, block_rows, head_count, HEAD_DIM)
    d_blocks = d_heads.reshape(block_count, block_rows, head_count, HEAD_DIM)

    def one_block(carry, item):
        key_acc, value_acc = carry
        q_block, d_block, lse_block = item
        scores = (
            jnp.einsum("qhd,khd->hqk", q_block, k_all, preferred_element_type=jnp.float32)
            * score_scale
        )
        prob_rows = jnp.exp(scores - lse_block[..., None])
        value_acc = value_acc + jnp.einsum(
            "hqk,qhd->khd",
            prob_rows.astype(jnp.bfloat16),
            d_block,
            preferred_element_type=jnp.float32,
        )
        d_probs = jnp.einsum("qhd,khd->hqk", d_block, v_all, preferred_element_type=jnp.float32)
        d_scores = (
            prob_rows * (d_probs - jnp.sum(prob_rows * d_probs, axis=-1, keepdims=True))
        ).astype(jnp.bfloat16)
        d_query = (
            jnp.einsum("hqk,khd->qhd", d_scores, k_all, preferred_element_type=jnp.float32)
            * score_scale
        )
        key_acc = (
            key_acc
            + jnp.einsum("hqk,qhd->khd", d_scores, q_block, preferred_element_type=jnp.float32)
            * score_scale
        )
        return ((key_acc, value_acc), d_query.astype(jnp.bfloat16))

    empty_acc = jnp.zeros((seq_len, head_count, HEAD_DIM), jnp.float32)
    (key_acc, value_acc), d_query = lax.scan(
        one_block, (empty_acc, empty_acc), (q_blocks, d_blocks, log_totals)
    )
    d_q = d_query.reshape(seq_len, columns)
    d_k = key_acc.astype(jnp.bfloat16).reshape(seq_len, columns)
    d_v = value_acc.astype(jnp.bfloat16).reshape(seq_len, columns)
    return (d_q, d_k, d_v)


def add_sources(received):
    return tuple((jnp.sum(piece, axis=0) for piece in received))


def per_device(
    inputs,
    positions,
    attn_gain,
    qkv_weight,
    attn_out_weight,
    mlp_gain,
    up_weight,
    down_weight,
    cotangent,
):
    layer = (
        lax.all_gather(attn_gain, ("dp", "seq"), axis=0, tiled=True),
        lax.all_gather(qkv_weight, ("dp", "seq"), axis=0, tiled=True),
        lax.all_gather(attn_out_weight, ("dp", "seq"), axis=0, tiled=True),
        lax.all_gather(mlp_gain, ("dp", "seq"), axis=0, tiled=True),
        lax.all_gather(up_weight, ("dp", "seq"), axis=0, tiled=True),
        lax.all_gather(down_weight, ("dp", "seq"), axis=0, tiled=True),
    )
    gain_one, w_qkv, w_out, gain_two, w_up, w_down = layer
    token_count = inputs.shape[1]
    resid_in = inputs[0].astype(jnp.float32)
    cos_table, sin_table = rope_tables(positions[0])
    normed_one, spread_one = normalize(resid_in)
    attn_in = (normed_one * gain_one.astype(jnp.float32)).astype(jnp.bfloat16)
    queries, key_rows, values = project_heads(attn_in, w_qkv, cos_table, sin_table)
    q_heads, k_heads, v_heads = (
        lax.all_to_all(queries, "seq", split_axis=1, concat_axis=0, tiled=True),
        lax.all_to_all(key_rows, "seq", split_axis=1, concat_axis=0, tiled=True),
        lax.all_to_all(values, "seq", split_axis=1, concat_axis=0, tiled=True),
    )
    attended_heads, log_totals = attend_forward(q_heads, k_heads, v_heads)
    attended = lax.all_to_all(attended_heads, "seq", split_axis=0, concat_axis=1, tiled=True)
    resid = resid_in + jnp.dot(attended, w_out, preferred_element_type=jnp.float32)
    normed_two, spread_two = normalize(resid)
    mlp_in = (normed_two * gain_two.astype(jnp.float32)).astype(jnp.bfloat16)
    up_rows = jnp.dot(mlp_in, w_up, preferred_element_type=jnp.float32)
    inner_act = up_rows[:, :FF]
    gate_act = up_rows[:, FF:]
    gelu_val, gelu_slope = gelu_parts(inner_act)
    hidden = (gelu_val * gate_act).astype(jnp.bfloat16)
    output = resid + jnp.einsum("tf,df->td", hidden, w_down, preferred_element_type=jnp.float32)
    layer_back = (
        lax.all_gather(attn_gain, ("dp", "seq"), axis=0, tiled=True),
        lax.all_gather(qkv_weight, ("dp", "seq"), axis=0, tiled=True),
        lax.all_gather(attn_out_weight, ("dp", "seq"), axis=0, tiled=True),
        lax.all_gather(mlp_gain, ("dp", "seq"), axis=0, tiled=True),
        lax.all_gather(up_weight, ("dp", "seq"), axis=0, tiled=True),
        lax.all_gather(down_weight, ("dp", "seq"), axis=0, tiled=True),
    )
    gain_one, w_qkv, w_out, gain_two, w_up, w_down = layer_back
    d_out = cotangent[0]
    down_grad = jnp.einsum("td,tf->df", d_out, hidden, preferred_element_type=jnp.float32)
    d_hidden = jnp.dot(d_out, w_down, preferred_element_type=jnp.float32)
    d_up = jnp.concatenate([d_hidden * gate_act * gelu_slope, d_hidden * gelu_val], axis=1).astype(
        jnp.bfloat16
    )
    up_grad = jnp.einsum("tk,tn->kn", mlp_in, d_up, preferred_element_type=jnp.float32)
    d_mlp_in = jnp.einsum("tn,kn->tk", d_up, w_up, preferred_element_type=jnp.float32)
    d_norm_two, gain_two_grad = norm_back(
        d_mlp_in, normed_two, spread_two, gain_two.astype(jnp.float32)
    )
    d_resid = d_out.astype(jnp.float32) + d_norm_two
    d_resid_low = d_resid.astype(jnp.bfloat16)
    out_grad = jnp.einsum("tk,tn->kn", attended, d_resid_low, preferred_element_type=jnp.float32)
    d_attended = jnp.einsum(
        "tn,kn->tk", d_resid_low, w_out, preferred_element_type=jnp.float32
    ).astype(jnp.bfloat16)
    d_heads = lax.all_to_all(d_attended, "seq", split_axis=1, concat_axis=0, tiled=True)
    queries, key_rows, values = project_heads(attn_in, w_qkv, cos_table, sin_table)
    head_inputs = (
        lax.all_to_all(queries, "seq", split_axis=1, concat_axis=0, tiled=True),
        lax.all_to_all(key_rows, "seq", split_axis=1, concat_axis=0, tiled=True),
        lax.all_to_all(values, "seq", split_axis=1, concat_axis=0, tiled=True),
    )
    d_q, d_k, d_v = attend_backward(
        head_inputs[0], head_inputs[1], head_inputs[2], d_heads, log_totals
    )
    dq_rows, dk_rows, dv_rows = (
        lax.all_to_all(d_q, "seq", split_axis=0, concat_axis=1, tiled=True),
        lax.all_to_all(d_k, "seq", split_axis=0, concat_axis=1, tiled=True),
        lax.all_to_all(d_v, "seq", split_axis=0, concat_axis=1, tiled=True),
    )
    shaped = (token_count, HEADS, HEAD_DIM)
    dq_pre = rotate_back(dq_rows.astype(jnp.float32).reshape(shaped), cos_table, sin_table).reshape(
        token_count, -1
    )
    dk_pre = rotate_back(dk_rows.astype(jnp.float32).reshape(shaped), cos_table, sin_table).reshape(
        token_count, -1
    )
    d_mixed = jnp.concatenate(
        [dq_pre.astype(jnp.bfloat16), dk_pre.astype(jnp.bfloat16), dv_rows], axis=1
    )
    qkv_grad = jnp.einsum("tk,tn->kn", attn_in, d_mixed, preferred_element_type=jnp.float32)
    d_attn_in = jnp.einsum("tn,kn->tk", d_mixed, w_qkv, preferred_element_type=jnp.float32)
    d_norm_one, gain_one_grad = norm_back(
        d_attn_in, normed_one, spread_one, gain_one.astype(jnp.float32)
    )
    input_grad = (d_resid + d_norm_one).astype(jnp.bfloat16)
    all_sent = (
        lax.all_to_all(
            gain_one_grad[None].astype(jnp.bfloat16), "dp", split_axis=1, concat_axis=0, tiled=True
        ).astype(jnp.float32),
        lax.all_to_all(
            qkv_grad[None].astype(jnp.bfloat16), "dp", split_axis=1, concat_axis=0, tiled=True
        ).astype(jnp.float32),
        lax.all_to_all(
            out_grad[None].astype(jnp.bfloat16), "dp", split_axis=1, concat_axis=0, tiled=True
        ).astype(jnp.float32),
        lax.all_to_all(
            gain_two_grad[None].astype(jnp.bfloat16), "dp", split_axis=1, concat_axis=0, tiled=True
        ).astype(jnp.float32),
        lax.all_to_all(
            up_grad[None].astype(jnp.bfloat16), "dp", split_axis=1, concat_axis=0, tiled=True
        ).astype(jnp.float32),
        lax.all_to_all(
            down_grad[None].astype(jnp.bfloat16), "dp", split_axis=1, concat_axis=0, tiled=True
        ).astype(jnp.float32),
    )
    grads = jax.tree.map(
        lambda part: part.astype(jnp.float32),
        lax.psum_scatter(
            for_sending(add_sources(all_sent)), "seq", scatter_dimension=0, tiled=True
        ),
    )
    return (
        output.astype(jnp.bfloat16)[None],
        input_grad[None],
        grads[0],
        grads[1],
        grads[2],
        grads[3],
        grads[4],
        grads[5],
    )


QUAD_MESH = (8, 4)
FLAT = ("y", "x", "c", "zh", "zl")
LOW, WIDE = jnp.bfloat16, jnp.float32


def pairs_of(step):
    found = []
    for dp in range(8):
        for seq in range(4):
            place = (dp // 4, dp // 2 % 2, dp % 2, seq // 2, seq % 2)
            target = step(*place)
            if target is not None:
                y, x, c, zh, zl = target
                found.append((dp * 4 + seq, (4 * y + 2 * x + c) * 4 + 2 * zh + zl))
    return found


TO_X = pairs_of(lambda y, x, c, zh, zl: (y, 1 - x, c, zh, zl))
TO_Y = pairs_of(lambda y, x, c, zh, zl: (1 - y, x, c, zh, zl))
TO_XY = pairs_of(lambda y, x, c, zh, zl: (1 - y, 1 - x, c, zh, zl))
TO_CORE = pairs_of(lambda y, x, c, zh, zl: (y, x, 1 - c, zh, zl))
TO_ZH = pairs_of(lambda y, x, c, zh, zl: (y, x, c, 1 - zh, zl))
TO_ZL = pairs_of(lambda y, x, c, zh, zl: (y, x, c, zh, 1 - zl))
TO_FAR = pairs_of(lambda y, x, c, zh, zl: (y, x, 1 - c, zh, 1 - zl))
TO_HOME = pairs_of(lambda y, x, c, zh, zl: (y, x, zh, c, zl))
ENTER = pairs_of(
    lambda y, x, c, zh, zl: (y, x, c, zh, 1 - zl) if c == zh else (y, x, zh, c, zl)
)
ENTER_MOVED = pairs_of(lambda y, x, c, zh, zl: None if c == zh else (y, x, c, zh, 1 - zl))


class Order(list):
    pass


def send(array, pairs):
    return lax.ppermute(array, FLAT, pairs)


def after(order, array):
    return lax.optimization_barrier((array, order[0]))[0]


def wait(order, *arrays):
    order[0] = lax.optimization_barrier((order[0], *arrays))[0]


def lanes(size):
    return -(-size // 128) * 128


def core_of(flat):
    return flat >> 2 & 1


def half_of(flat):
    return flat >> 1 & 1


def group_of(flat):
    return 2 * core_of(flat) + (flat & 1)


def square_of(flat):
    return flat >> 3


def mm(left, right):
    return lax.dot_general(left, right, (((1,), (0,)), ((), ())), preferred_element_type=WIDE)


def mm_t(left, right):
    return lax.dot_general(left, right, (((1,), (1,)), ((), ())), preferred_element_type=WIDE)


def t_mm(left, right):
    return lax.dot_general(left, right, (((0,), (0,)), ((), ())), preferred_element_type=WIDE)


def window(index, size):
    return pl.ds(pl.multiple_of(index * size, size), size)


def whole(array):
    rank = len(array.shape)
    return (array, array.shape, lambda *_: (0,) * rank)


def by_rows(array, rows, step=lambda b: b):
    return (array, (rows,) + array.shape[1:], lambda b, f: (step(b),) + (0,) * (len(array.shape) - 1))


def run(body, order, grid, ins, outs, scratch=(), flops=0, spare=6 * 2**20):
    moved = sum(a.size * a.dtype.itemsize for a, _, _ in ins)
    moved += sum(a.size * a.dtype.itemsize for a, _, _ in outs)
    def held(block, dtype, count):
        return count * math.prod(block) * jnp.dtype(dtype).itemsize

    count = 1 if grid == (1,) else 2
    grant = sum(held(block, a.dtype, count) for a, block, _ in (*ins, *outs))
    grant += sum(held(m.shape, m.dtype, 1) for m in scratch) + spare
    made = pl.pallas_call(
        body,
        grid_spec=pltpu.PrefetchScalarGridSpec(
            num_scalar_prefetch=1,
            grid=grid,
            in_specs=[pl.BlockSpec(block, index) for _, block, index in ins],
            out_specs=[pl.BlockSpec(block, index) for _, block, index in outs],
            scratch_shapes=list(scratch),
        ),
        out_shape=[a for a, _, _ in outs],
        compiler_params=pltpu.CompilerParams(vmem_limit_bytes=grant),
        cost_estimate=pl.CostEstimate(flops=flops // 100, bytes_accessed=moved // 100, transcendentals=0),
    )(order[0], *[a for a, _, _ in ins])
    order[0], _ = lax.optimization_barrier((order[0], made[0]))
    return made


def spans(pieces):
    rows = pieces[0].shape[0]
    return [(0, 0, rows), (1, 0, rows), (2, 0, rows), (3, 0, rows // 2), (3, rows // 2, rows // 2)]


def span_of(square, span, rows):
    index, first, count = span
    return pl.ds(pl.multiple_of((square ^ index) * rows + first, count), count)


def shape_of(*dims, dtype=LOW):
    return jax.ShapeDtypeStruct(dims, dtype)


def column_of(row):
    size = row.shape[1]
    down = lax.broadcasted_iota(jnp.int32, (size, size), 0)
    across = lax.broadcasted_iota(jnp.int32, (size, size), 1)
    return jnp.sum(jnp.where(down == across, row, 0.0), axis=1, keepdims=True)


def row_of(column):
    size = column.shape[0]
    down = lax.broadcasted_iota(jnp.int32, (size, size), 0)
    across = lax.broadcasted_iota(jnp.int32, (size, size), 1)
    return jnp.sum(jnp.where(down == across, column, 0.0), axis=0, keepdims=True)


def normed_of(x):
    centred = x - jnp.mean(x, axis=-1, keepdims=True)
    spread = lax.rsqrt(jnp.mean(centred * centred, axis=-1, keepdims=True) + norm_eps)
    return centred * spread, spread


def split_slices(order, scaled, plain, gain, parts):
    rows, part, rest = scaled.shape[0], scaled.shape[1] // (4 * parts), plain.shape[1] // 4
    out = shape_of(2, rows, lanes(parts * part + rest))

    def body(flat_ref, scaled_ref, plain_ref, gain_ref, own_ref, sent_ref, held):
        scale = column_of(gain_ref[...].astype(WIDE))
        for s in range(4):
            for t in range(parts):
                cols = scaled_ref[:, (4 * t + s) * part : (4 * t + s + 1) * part].astype(WIDE)
                held[s, :, t * part : (t + 1) * part] = (cols * scale).astype(LOW)
            held[s, :, parts * part : parts * part + rest] = plain_ref[
                :, s * rest : (s + 1) * rest
            ]
        core = core_of(flat_ref[0])
        for zl in range(2):
            own_ref[zl] = held[2 * core + zl]
            sent_ref[zl] = held[2 * (1 - core) + zl]

    return run(
        body, order, (1,), [whole(a) for a in (scaled, plain, gain)], [whole(out)] * 2,
        [pltpu.VMEM((4, *out.shape[1:]), LOW)],
    )


def chip_rows(order, own, received):
    def body(flat_ref, own_ref, received_ref, kept_ref, sent_ref):
        core, chip = core_of(flat_ref[0]), flat_ref[0] & 1
        kept_ref[core] = own_ref[chip]
        kept_ref[1 - core] = received_ref[chip]
        sent_ref[core] = own_ref[1 - chip]
        sent_ref[1 - core] = received_ref[1 - chip]

    return run(
        body, order, (1,), [whole(own), whole(received)], [whole(shape_of(*own.shape))] * 2
    )


def quad_rows(order, own, received):
    _, rows, width = own.shape

    def body(flat_ref, own_ref, received_ref, out_ref):
        chip = flat_ref[0] & 1
        for c in range(2):
            out_ref[2 * c + chip] = own_ref[c]
            out_ref[2 * c + 1 - chip] = received_ref[c]

    return run(
        body, order, (1,), [whole(own), whole(received)], [whole(shape_of(4, rows, width))]
    )[0]


def line_rows(order, near, far):
    _, rows, width = near.shape
    near = near.reshape(2, 2 * rows, width)
    far = far.reshape(2, 2 * rows, width)

    def body(flat_ref, near_ref, far_ref, out_ref):
        half = half_of(flat_ref[0])
        for c in range(2):
            out_ref[c, half] = near_ref[c]
            out_ref[c, 1 - half] = far_ref[c]

    out = run(
        body, order, (1,), [whole(near), whole(far)], [whole(shape_of(2, 2, 2 * rows, width))]
    )[0]
    return out.reshape(8 * rows, width)


def join_tokens(order, parts, rows):
    height, width = parts[0].shape
    extra = height - rows

    def body(flat_ref, block, first, second, core_block, core_first, core_second, *outs):
        home = core_of(flat_ref[0]) == half_of(flat_ref[0])
        here = (block, first, core_first, core_second)
        moved = (first, second, core_block, core_first)
        for k in range(4):
            for flag, source in ((home, here[k]), (jnp.logical_not(home), moved[k])):

                @pl.when(jnp.logical_and(pl.program_id(0) == k, flag))
                def _(source=source):
                    def step(r, carry):
                        outs[0][window(r, 32), :] = source[window(r, 32), :]
                        return carry

                    lax.fori_loop(0, rows // 32, step, 0)
                    if extra:
                        outs[1][...] = source[rows:, :]

    made = [shape_of(4 * rows, width)] + ([shape_of(4 * extra, width)] if extra else [])
    return run(
        body, order, (4,), [whole(a) for a in parts],
        [by_rows(m, m.shape[0] // 4) for m in made],
    )


def rope_lanes(seq_pos):
    exponent = jnp.arange(0, HEAD_DIM, 2).astype(WIDE) / HEAD_DIM
    angles = seq_pos[:, None] * (rope_base ** (-exponent))[None, :]
    cos_half, sin_half = jnp.cos(angles), jnp.sin(angles)
    return (
        jnp.concatenate([cos_half] * 4, axis=1),
        jnp.concatenate([-sin_half, sin_half] * 2, axis=1),
    )


def turned(v):
    half = HEAD_DIM // 2
    lane = lax.broadcasted_iota(jnp.int32, v.shape, 1)
    return jnp.where(
        lane % HEAD_DIM < half, pltpu.roll(v, 2 * HEAD_DIM - half, 1), pltpu.roll(v, half, 1)
    )


def project(order, x, pieces, cos_table, sin_table):
    tokens, width = x.shape
    piece, columns = pieces[0].shape[0], 3 * width // 4
    rows = tokens // 4

    def body(flat_ref, x_ref, *refs):
        weights, (cos_ref, sin_ref, n_ref, mix_ref) = refs[:5], refs[5:]
        n_ref[...] = normed_of(x_ref[...].astype(WIDE))[0].astype(LOW)
        square = square_of(flat_ref[0])
        mixed = sum(
            mm(n_ref[:, span_of(square, span, piece)], w[:, :columns])
            for span, w in zip(spans(pieces), weights)
        )
        turned_to = 2 * columns // 3
        for t in range(0, turned_to, 128):
            v = mixed[:, t : t + 128]
            mix_ref[:, t : t + 128] = (v * cos_ref[...] + turned(v) * sin_ref[...]).astype(LOW)
        mix_ref[:, turned_to:] = mixed[:, turned_to:].astype(LOW)

    return run(
        body, order, (4,),
        [by_rows(x, rows)] + [whole(p) for p in pieces]
        + [by_rows(cos_table, rows), by_rows(sin_table, rows)],
        [by_rows(shape_of(tokens, width), rows), by_rows(shape_of(tokens, columns), rows)],
        flops=2 * tokens * width * columns,
    )


def attend(order, mix):
    tokens, columns = mix.shape
    part = columns // 3
    rows = tokens // 4
    scale = HEAD_DIM ** (-0.5)

    def body(flat_ref, q_ref, k_ref, v_ref, out_ref, log_ref):
        lane = lax.broadcasted_iota(jnp.int32, (rows, part), 1) // HEAD_DIM
        total = jnp.zeros((rows, part), WIDE)
        queries = q_ref[...].astype(WIDE) * scale
        for h in range(part // HEAD_DIM):
            q_head = jnp.where(lane == h, queries, 0.0).astype(LOW)
            scores = mm_t(q_head, k_ref[...])
            peak = jnp.max(scores, axis=-1, keepdims=True)
            powers = jnp.exp(scores - peak)
            mass = jnp.sum(powers, axis=-1, keepdims=True)
            probs = (powers * (1.0 / mass)).astype(LOW)
            total = jnp.where(lane == h, mm(probs, v_ref[...]), total)
            log_ref[h : h + 1, :] = row_of(peak + jnp.log(mass))
        out_ref[...] = total.astype(LOW)

    return run(
        body, order, (4,),
        [
            (mix, (rows, part), lambda b, f: (b, 0)),
            (mix, (tokens, part), lambda b, f: (0, 1)),
            (mix, (tokens, part), lambda b, f: (0, 2)),
        ],
        [
            by_rows(shape_of(tokens, part), rows),
            (shape_of(8, tokens, dtype=WIDE), (8, rows), lambda b, f: (0, b)),
        ],
        flops=16 * tokens * tokens * part,
    )


def token_parts(arrays, rows):
    return [by_rows(a, rows, lambda b, i=i: b ^ i) for i, a in enumerate(arrays)]


def join_heads(order, x, heads, columns):
    tokens, width = x.shape
    rows, part = tokens // 4, width // 4

    def body(flat_ref, x_ref, *refs):
        parts, weights, (n_ref, own_ref, held) = refs[:4], refs[4:8], refs[8:]
        group, square = group_of(flat_ref[0]), square_of(flat_ref[0])
        for j in range(4):
            cols = window(group ^ j, part)
            held[:, cols] = x_ref[:, cols].astype(WIDE) + sum(
                mm(parts[i][...], weights[j][window(group ^ i ^ square, part), :])
                for i in range(4)
            )
        resid = held[...]
        n_ref[...] = normed_of(resid)[0].astype(LOW)

        @pl.when(pl.program_id(0) == 0)
        def _():
            own_ref[...] = held[...]

    return run(
        body, order, (4,),
        [by_rows(x, rows)] + token_parts(heads, rows) + [whole(w) for w in columns],
        [by_rows(shape_of(tokens, width), rows), whole(shape_of(rows, width, dtype=WIDE))],
        [pltpu.VMEM((rows, width), WIDE)],
        flops=2 * tokens * width * width,
    )


def feed(order, normed, cot, pieces):
    tokens, width = normed.shape
    piece, ff = pieces[0].shape[0], FF // 4
    rows = tokens // 4

    def body(flat_ref, n_ref, cot_ref, *refs):
        weights, (h_ref, d_ref) = refs[:5], refs[5:]
        square = square_of(flat_ref[0])
        cols = [span_of(square, span, piece) for span in spans(pieces)]
        wide = sum(mm(n_ref[:, at], w[:, : 2 * ff]) for at, w in zip(cols, weights))
        d_hidden = sum(mm(cot_ref[:, at], w[:, 2 * ff : 3 * ff]) for at, w in zip(cols, weights))
        inner, gate = wide[:, :ff], wide[:, ff:]
        cdf = 0.5 * (1.0 + lax.erf(inner * inv_root_two))
        slope = cdf + inner * jnp.exp(-0.5 * inner * inner) * inv_root_tau
        bent = inner * cdf
        h_ref[...] = (bent * gate).astype(LOW)
        d_ref[:, :ff] = (d_hidden * gate * slope).astype(LOW)
        d_ref[:, ff:] = (d_hidden * bent).astype(LOW)

    return run(
        body, order, (4,),
        [by_rows(normed, rows), by_rows(cot, rows)] + [whole(w) for w in pieces],
        [by_rows(shape_of(tokens, ff), rows), by_rows(shape_of(tokens, 2 * ff), rows)],
        flops=6 * tokens * width * ff,
    )


def back_half(order, grads, pieces, far):
    tokens = grads[0][0].shape[0]
    piece = pieces[0].shape[0]
    rows, width, count = tokens // 2, 4 * piece, len(grads)
    out = shape_of(rows, width, dtype=LOW if far else WIDE)

    def body(flat_ref, *refs):
        arrays, weights, out_ref = refs[:count], refs[count : count + 5], refs[count + 5]
        square = square_of(flat_ref[0])
        for span, w in zip(spans(pieces), weights):
            out_ref[:, span_of(square, span, piece)] = sum(
                mm_t(a[...], w[:, at : at + a.shape[1]]) for a, (_, at) in zip(arrays, grads)
            ).astype(out.dtype)

    return run(
        body, order, (1,),
        [by_rows(a, rows, lambda b: int(far)) for a, _ in grads] + [whole(p) for p in pieces],
        [whole(out)],
        flops=tokens * width * sum(a.shape[1] for a, _ in grads),
    )[0]


def norm_pull(order, x, terms, base, keep):
    rows, width = base.shape[0] // (4 if keep else 1), base.shape[1]
    step = rows // 4

    def body(flat_ref, x_ref, a_ref, b_ref, c_ref, base_ref, *outs):
        normed, spread = normed_of(x_ref[...].astype(WIDE))
        scaled = a_ref[...] + b_ref[...].astype(WIDE) + c_ref[...].astype(WIDE)
        grad = base_ref[...].astype(WIDE) + spread * (
            scaled
            - jnp.mean(scaled, axis=-1, keepdims=True)
            - normed * jnp.mean(scaled * normed, axis=-1, keepdims=True)
        )
        outs[0][...] = grad.astype(LOW)
        if keep:
            outs[1][...] = grad

    outs = [shape_of(rows, width)] + ([shape_of(rows, width, dtype=WIDE)] if keep else [])
    return run(
        body, order, (4,), [by_rows(a, step) for a in (x, *terms, base)],
        [by_rows(o, step) for o in outs],
    )


def feed_grads(order, normed, cot, d_up, hidden):
    tokens, width = normed.shape
    rows, piece = tokens // 4, width // 4
    ff = hidden.shape[1]
    out = shape_of(4, piece, lanes(3 * ff))

    def body(flat_ref, n_ref, cot_ref, d_ref, h_ref, out_ref, held):
        @pl.when(pl.program_id(0) == 0)
        def _():
            held[...] = jnp.zeros_like(held)

        for i in range(4):
            cols = slice(i * piece, (i + 1) * piece)
            held[i, :, : 2 * ff] += t_mm(n_ref[:, cols], d_ref[...])
            held[i, :, 2 * ff : 3 * ff] += t_mm(cot_ref[:, cols], h_ref[...])

        @pl.when(pl.program_id(0) == 3)
        def _():
            out_ref[...] = held[...].astype(LOW)

    return run(
        body, order, (4,), [by_rows(a, rows) for a in (normed, cot, d_up, hidden)],
        [whole(out)], [pltpu.VMEM(out.shape, WIDE)],
        flops=6 * tokens * width * ff,
    )[0]


def heads_back(order, d_all, heads, columns):
    rows, width = d_all[0].shape
    part = width // 4

    def body(flat_ref, *refs):
        blocks, parts, weights = refs[:4], refs[4:8], refs[8:12]
        d_ref, grad_ref, block, held, total = refs[12:]
        group, square = group_of(flat_ref[0]), square_of(flat_ref[0])
        at = pl.program_id(0)
        for k in range(4):

            @pl.when(at == k)
            def _(source=blocks[k]):
                def step(r, carry):
                    block[window(r, 32), :] = source[window(r, 32), :]
                    return carry

                lax.fori_loop(0, rows // 32, step, 0)

            held[k] = parts[k][...]

        @pl.when(at == 0)
        def _():
            total[...] = jnp.zeros_like(total)

        d_ref[...] = sum(
            mm_t(block[:, window(group ^ j, part)], weights[j][window(group ^ square, part), :])
            for j in range(4)
        ).astype(LOW)
        mine = block[:, window(group, part)]
        for i in range(4):
            total[i] += t_mm(held[group ^ square ^ i], mine)

        @pl.when(at == 3)
        def _():
            grad_ref[...] = total[...].astype(LOW)

    return run(
        body, order, (4,),
        [whole(d) for d in d_all] + token_parts(heads, rows) + [whole(w) for w in columns],
        [by_rows(shape_of(4 * rows, part), rows), whole(shape_of(4, part, part))],
        [
            pltpu.VMEM((rows, width), LOW),
            pltpu.VMEM((4, rows, part), LOW),
            pltpu.VMEM((4, part, part), WIDE),
        ],
        flops=4 * 4 * rows * width * part,
    )


def attend_back(order, mix, attended, d_attended, logs, cos_table, sin_table):
    tokens, columns = mix.shape
    part = columns // 3
    rows = tokens // 4
    scale = HEAD_DIM ** (-0.5)
    heads = part // HEAD_DIM

    def rotated(grad, cos, sin):
        halves = [grad[:, t : t + 128] for t in range(0, part, 128)]
        return jnp.concatenate([v * cos - turned(v) * sin for v in halves], axis=1).astype(LOW)

    def body(flat_ref, q_ref, k_ref, v_ref, o_ref, d_ref, log_ref, cos_ref, sin_ref, *refs):
        dq_ref, dk_ref, dv_ref, k_total, v_total = refs
        at = pl.program_id(0)

        @pl.when(at == 0)
        def _():
            k_total[...] = jnp.zeros_like(k_total)
            v_total[...] = jnp.zeros_like(v_total)

        lane = lax.broadcasted_iota(jnp.int32, (rows, part), 1) // HEAD_DIM
        queries = q_ref[...].astype(WIDE) * scale
        grads = d_ref[...].astype(WIDE)
        chosen = lax.broadcasted_iota(jnp.int32, (8, part), 0) == (
            lax.broadcasted_iota(jnp.int32, (8, part), 1) // HEAD_DIM
        )
        deltas = lax.dot_general(
            chosen.astype(WIDE), grads * o_ref[...].astype(WIDE), (((1,), (1,)), ((), ())),
            precision=lax.Precision.HIGHEST, preferred_element_type=WIDE,
        )
        d_query = jnp.zeros((rows, part), WIDE)
        for h in range(heads):
            q_head = jnp.where(lane == h, queries, 0.0).astype(LOW)
            d_head = jnp.where(lane == h, grads, 0.0).astype(LOW)
            probs = jnp.exp(mm_t(k_ref[...], q_head) - log_ref[h : h + 1, :])
            d_probs = mm_t(v_ref[...], d_head)
            d_scores = (probs * (d_probs - deltas[h : h + 1, :])).astype(LOW)
            v_total[...] += mm(probs.astype(LOW), d_head)
            k_total[...] += mm(d_scores, q_head)
            d_query = jnp.where(lane == h, t_mm(d_scores, k_ref[...]), d_query)
        here = window(at, rows)
        dq_ref[...] = rotated(d_query * scale, cos_ref[here, :], sin_ref[here, :])

        @pl.when(at == 3)
        def _():
            dk_ref[...] = rotated(k_total[...], cos_ref[...], sin_ref[...])
            dv_ref[...] = v_total[...].astype(LOW)

    out = shape_of(tokens, part)
    return run(
        body, order, (4,),
        [
            (mix, (rows, part), lambda b, f: (b, 0)),
            (mix, (tokens, part), lambda b, f: (0, 1)),
            (mix, (tokens, part), lambda b, f: (0, 2)),
            by_rows(attended, rows),
            by_rows(d_attended, rows),
            (logs, (8, rows), lambda b, f: (0, b)),
            whole(cos_table),
            whole(sin_table),
        ],
        [by_rows(out, rows), whole(out), whole(out)],
        [pltpu.VMEM((tokens, part), WIDE)] * 2,
        flops=40 * tokens * tokens * part,
    )


def mixed_grads(order, normed, d_mixed, out_grad):
    tokens, width = normed.shape
    rows, piece = tokens // 4, width // 4
    part = d_mixed[0].shape[1]

    def body(flat_ref, n_ref, *refs):
        grads, out_ref, outs, held = refs[:3], refs[3], refs[4:8], refs[8]
        square = square_of(flat_ref[0])

        @pl.when(pl.program_id(0) == 0)
        def _():
            held[...] = jnp.zeros_like(held)

        for i in range(4):
            cols = n_ref[:, window(square ^ i, piece)]
            for t in range(3):
                held[i, :, t * part : (t + 1) * part] += t_mm(cols, grads[t][...])

        @pl.when(pl.program_id(0) == 3)
        def _():
            for i in range(4):
                outs[i][:, : 3 * part] = held[i].astype(LOW)
                outs[i][:, 3 * part :] = out_ref[i]

    return run(
        body, order, (4,),
        [by_rows(normed, rows)] + [by_rows(d, rows) for d in d_mixed] + [whole(out_grad)],
        [whole(shape_of(piece, 4 * part))] * 4, [pltpu.VMEM((4, piece, 3 * part), WIDE)],
        flops=6 * tokens * width * part,
    )


def share_slices(slices):
    return [slices[0]] + [
        send(slices[i], pairs) for i, pairs in ((1, TO_ZL), (2, TO_CORE), (3, TO_FAR))
    ]


def share_pieces(pieces):
    return [pieces[0]] + [
        send(pieces[i], pairs) for i, pairs in ((1, TO_X), (2, TO_Y), (3, TO_XY))
    ]


def fold(order, terms):
    high, width = terms[0].shape[1:]
    rows = high // 4
    terms = [t.reshape(-1, 2, 2, rows, width) for t in terms]

    def body(flat_ref, *refs):
        ins, (kept_ref, sent_ref) = refs[:-2], refs[-2:]
        half = half_of(flat_ref[0])

        def total(at):
            return sum(r[k, 0, at].astype(WIDE) for r in ins for k in range(r.shape[0]))

        kept_ref[0] = total(half)
        sent_ref[0] = total(1 - half).astype(LOW)

    return run(
        body, order, (2,),
        [
            (t, (t.shape[0], 1) + t.shape[2:], lambda b, f: (0, b, 0, 0, 0))
            for t in terms
        ],
        [by_rows(shape_of(2, rows, width, dtype=WIDE), 1), by_rows(shape_of(2, rows, width), 1)],
    )


def split_rows(order, kept, received):
    _, high, width = kept.shape
    rows = high // 2
    kept, received = kept.reshape(4, rows, width), received.reshape(4, rows, width)

    def body(flat_ref, kept_ref, received_ref, *outs):
        for i in range(4):
            at = group_of(flat_ref[0]) ^ i
            outs[i][...] = (kept_ref[at] + received_ref[at].astype(WIDE)).astype(LOW)

    return run(
        body, order, (1,), [whole(kept), whole(received)], [whole(shape_of(rows, width))] * 4
    )


def finish(order, slices, weight, gain, sizes):
    rows, width = slices[0].shape
    count, part, rest = sizes

    def body(flat_ref, *refs):
        w_ref, gain_ref, scaled_ref, gain_out, plain_ref, held = refs[4:]
        for i in range(4):
            held[group_of(flat_ref[0]) ^ i] = refs[i][...].astype(WIDE)
        total = jnp.zeros((rows, 1), WIDE)
        scale = column_of(gain_ref[...].astype(WIDE))
        for s in range(4):
            for t in range(count):
                at = (4 * t + s) * part
                grad = held[s, :, t * part : (t + 1) * part]
                total += jnp.sum(
                    grad * w_ref[:, at : at + part].astype(WIDE), axis=1, keepdims=True
                )
                scaled_ref[:, at : at + part] = grad * scale
            plain_ref[:, s * rest : (s + 1) * rest] = held[s, :, count * part : count * part + rest]
        gain_out[...] = row_of(total)

    return run(
        body, order, (1,), [whole(a) for a in (*slices, weight, gain)],
        [
            whole(shape_of(*weight.shape, dtype=WIDE)),
            whole(shape_of(1, rows, dtype=WIDE)),
            whole(shape_of(rows, 4 * rest, dtype=WIDE)),
        ],
        [pltpu.VMEM((4, rows, width), WIDE)],
    )


def quad_device(
    inputs,
    positions,
    attn_gain,
    qkv_weight,
    attn_out_weight,
    mlp_gain,
    up_weight,
    down_weight,
    cotangent,
):
    order = Order([lax.axis_index(FLAT).astype(jnp.int32).reshape(1)])
    tokens, width = inputs.shape[1:]
    part, ff = width // 4, FF // 4
    gain_one, gain_two = attn_gain[None], mlp_gain[None]

    own, sent = split_slices(order, qkv_weight, attn_out_weight, gain_one, 3)
    received = send(sent, TO_CORE)
    own_two, sent = split_slices(order, up_weight, down_weight, gain_two, 2)
    received_two = send(sent, TO_CORE)
    own, sent = chip_rows(order, own, received)
    received = send(sent, TO_ZL)
    own_two, sent = chip_rows(order, own_two, received_two)
    pos = positions[0]
    pos_row = jnp.concatenate([pos // 128, pos % 128]).astype(LOW)
    pos_row = jnp.pad(pos_row[None], ((0, 15), (0, width - 2 * tokens)))
    block = jnp.concatenate([inputs[0], pos_row])
    wait(order, block)
    one = quad_rows(order, own, received)
    one_far = send(one, TO_ZH)
    first = send(after(order, block), ENTER)
    received_two = send(after(order, sent), TO_ZL)
    one = line_rows(order, one, one_far)
    half = one.shape[0] // 2
    one_x, one_y = send(one, TO_X), send(one, TO_Y)
    two = quad_rows(order, own_two, received_two)
    two_far = send(two, TO_ZH)
    second = send(after(order, first), ENTER_MOVED)
    core_first = send(after(order, first), TO_CORE)
    wait(order, core_first, second)
    core_block = send(after(order, block), TO_CORE)
    core_second = send(after(order, second), TO_CORE)
    x, pos_all = join_tokens(
        order, [block, first, second, core_block, core_first, core_second], tokens
    )
    cot_first = send(after(order, cotangent[0]), ENTER)
    one_top = send(one_x[:half], TO_Y)
    one_low = send(one_y[half:], TO_X)
    pos_all = pos_all.reshape(4, 16, width)[:, 0, : 2 * tokens].astype(WIDE)
    pos_all = (pos_all[:, :tokens] * 128.0 + pos_all[:, tokens:]).reshape(4 * tokens)
    cos_table, sin_table = rope_lanes(pos_all)
    one = [one, one_x, one_y, one_top, one_low]

    w_out = jnp.concatenate([p[:, 3 * part :] for p in one])
    wait(order, w_out, cos_table, sin_table)
    w_side = send(after(order, w_out), TO_ZL)
    w_core = send(after(order, w_out), TO_CORE)
    normed_one, mix = project(order, x, one, cos_table, sin_table)
    two = line_rows(order, two, two_far)
    two_x, two_y = send(two, TO_X), send(two, TO_Y)
    wait(order, w_core, cot_first)
    attended, logs = attend(order, mix)
    att_side = send(attended, TO_ZL)
    att_core = send(attended, TO_CORE)
    wait(order, att_core, w_side)
    w_far = send(after(order, w_side), TO_CORE)
    cot_second = send(after(order, cot_first), ENTER_MOVED)
    w_out = [w_out, w_side, w_core, w_far]
    heads = [attended, att_side, att_core, send(att_side, TO_CORE)]
    normed_two, resid = join_heads(order, x, heads, w_out)

    two_top = send(two_x[:half], TO_Y)
    two_low = send(two_y[half:], TO_X)
    core_block = send(after(order, cotangent[0]), TO_CORE)
    core_first = send(after(order, cot_first), TO_CORE)
    core_second = send(after(order, cot_second), TO_CORE)
    (cot,) = join_tokens(
        order,
        [cotangent[0], cot_first, cot_second, core_block, core_first, core_second],
        tokens,
    )
    two = [two, two_x, two_y, two_top, two_low]
    hidden, d_up = feed(order, normed_two, cot, two)

    def crossed(far):
        return send(far, TO_CORE)

    def side_of(near, far):
        return send((near[tokens:] + far[tokens:].astype(WIDE)).astype(LOW), TO_ZL)

    grads = [(d_up, 0)]
    far = crossed(back_half(order, grads, two, True))
    near = back_half(order, grads, two, False)
    side = side_of(near, far)
    ff_terms = feed_grads(order, normed_two, cot, d_up, hidden)
    d_low, d_resid = norm_pull(order, resid, (near, far, side), cot, True)
    ff_terms = lax.all_to_all(
        after(order, ff_terms), ("y", "x"), split_axis=0, concat_axis=0, tiled=True
    )
    d_side = send(d_low, TO_ZL)
    d_core = send(d_low, TO_CORE)
    grads = [(hidden, 2 * ff)]
    out_far = back_half(order, grads, two, True)
    out_near = back_half(order, grads, two, False)
    d_all = [d_low, d_side, d_core, send(after(order, d_side), TO_CORE)]
    d_attended, out_grad = heads_back(order, d_all, heads, w_out)
    out_far = crossed(after(order, out_far))
    out_side = side_of(out_near, out_far)
    d_mixed = attend_back(order, mix, attended, d_attended, logs, cos_table, sin_table)
    output = resid + out_near[:tokens] + out_far[:tokens].astype(WIDE) + out_side.astype(WIDE)
    output = output.astype(LOW)
    wait(order, output)
    output = send(output, TO_HOME)
    mixed_terms = share_pieces(mixed_grads(order, normed_one, d_mixed, out_grad))
    grads = [(d, t * part) for t, d in enumerate(d_mixed)]
    far = crossed(back_half(order, grads, one, True))
    near = back_half(order, grads, one, False)
    side = side_of(near, far)
    ff_kept, ff_sent = fold(order, [ff_terms])
    wait(order, output)
    ff_sent = send(after(order, ff_sent), TO_ZH)
    mixed_kept, mixed_sent = fold(order, [t[None] for t in mixed_terms])
    mixed_sent = send(mixed_sent, TO_ZH)
    (input_grad,) = norm_pull(order, x, (near, far, side), d_resid, False)
    input_grad = send(input_grad, TO_HOME)
    ff_slices = share_slices(split_rows(order, ff_kept, ff_sent))
    mixed_slices = share_slices(split_rows(order, mixed_kept, mixed_sent))
    up_grad, gain_two_grad, down_grad = finish(
        order, ff_slices, up_weight, gain_two, (2, ff, ff)
    )
    qkv_grad, gain_one_grad, out_grad = finish(
        order, mixed_slices, qkv_weight, gain_one, (3, part, part)
    )
    return (
        output[None],
        input_grad[None],
        gain_one_grad[0],
        qkv_grad,
        out_grad,
        gain_two_grad[0],
        up_grad,
        down_grad,
    )


def solution(mesh):
    dp, seq = "dp", "seq"
    step = per_device
    if tuple(mesh.shape.values()) == QUAD_MESH:
        dp, seq, step = ("y", "x", "c"), ("zh", "zl"), quad_device
        mesh = jax.sharding.Mesh(mesh.devices.reshape(2, 2, 2, 2, 2), FLAT)
        every = FLAT
    else:
        every = (dp, seq)
    rows = P(every, None)
    return jax.shard_map(
        step,
        mesh=mesh,
        in_specs=(
            P(dp, seq, None),
            P(dp, seq),
            P(every),
            rows,
            rows,
            P(every),
            rows,
            rows,
            P(dp, seq, None),
        ),
        out_specs=(
            P(dp, seq, None),
            P(dp, seq, None),
            P(every),
            rows,
            rows,
            P(every),
            rows,
            rows,
        ),
        check_vma=False,
    )
```

```python
import math

import jax
import jax.numpy as jnp
from jax import lax
from jax.experimental import pallas as pl
from jax.experimental.pallas import tpu as pltpu
from jax.sharding import PartitionSpec as P

HEADS = 16
HEAD_DIM = 64
FF = 2624


norm_eps = 1e-05
rope_base = 160000.0
inv_root_two = 0.7071067811865476
inv_root_tau = 0.3989422804014327


def for_sending(array):
    return jax.tree.map(lambda a: a.astype(jnp.bfloat16) if a.dtype == jnp.float32 else a, array)


def normalize(values):
    centre = jnp.mean(values, axis=-1, keepdims=True)
    centred = values - centre
    spread = lax.rsqrt(jnp.mean(centred * centred, axis=-1, keepdims=True) + norm_eps)
    return (centred * spread, spread)


def norm_back(grad_in, normed, spread, gain):
    scaled = grad_in * gain
    gain_term = jnp.sum(grad_in * normed, axis=0)
    centred = (
        scaled
        - jnp.mean(scaled, axis=-1, keepdims=True)
        - normed * jnp.mean(scaled * normed, axis=-1, keepdims=True)
    )
    return (spread * centred, gain_term)


def rope_tables(seq_pos):
    exponent = jnp.arange(0, HEAD_DIM, 2).astype(jnp.float32) / HEAD_DIM
    frequency = rope_base ** (-exponent)
    angles = seq_pos.astype(jnp.float32)[:, None] * frequency[None, :]
    angles = jnp.concatenate([angles, angles], axis=-1)[:, None, :]
    return (jnp.cos(angles), jnp.sin(angles))


def rotate(values, cos_table, sin_table):
    half_dim = values.shape[-1] // 2
    turned = jnp.concatenate([-values[..., half_dim:], values[..., :half_dim]], axis=-1)
    return values * cos_table + turned * sin_table


def rotate_back(grads, cos_table, sin_table):
    half_dim = grads.shape[-1] // 2
    weighted = grads * sin_table
    turned = jnp.concatenate([weighted[..., half_dim:], -weighted[..., :half_dim]], axis=-1)
    return grads * cos_table + turned


def gelu_parts(inner_act):
    normal_cdf = 0.5 * (1.0 + jax.scipy.special.erf(inner_act * inv_root_two))
    slope = normal_cdf + inner_act * jnp.exp(-0.5 * inner_act * inner_act) * inv_root_tau
    return (inner_act * normal_cdf, slope)


def project_heads(attn_in, w_qkv, cos_table, sin_table):
    token_count, model_width = attn_in.shape
    mixed_rows = jnp.dot(attn_in, w_qkv, preferred_element_type=jnp.float32)
    shaped = (token_count, HEADS, HEAD_DIM)
    queries = rotate(mixed_rows[:, :model_width].reshape(shaped), cos_table, sin_table)
    key_rows = rotate(
        mixed_rows[:, model_width : 2 * model_width].reshape(shaped), cos_table, sin_table
    )
    queries = queries.reshape(token_count, model_width).astype(jnp.bfloat16)
    key_rows = key_rows.reshape(token_count, model_width).astype(jnp.bfloat16)
    values = mixed_rows[:, 2 * model_width :].astype(jnp.bfloat16)
    return (queries, key_rows, values)


def attend_forward(q_heads, k_heads, v_heads):
    seq_len, columns = q_heads.shape
    head_count = columns // HEAD_DIM
    block_rows = min(512, seq_len)
    block_count = seq_len // block_rows
    score_scale = HEAD_DIM ** (-0.5)
    k_all = k_heads.reshape(seq_len, head_count, HEAD_DIM)
    v_all = v_heads.reshape(seq_len, head_count, HEAD_DIM)

    def one_block(q_block):
        scores = (
            jnp.einsum("qhd,khd->hqk", q_block, k_all, preferred_element_type=jnp.float32)
            * score_scale
        )
        row_peak = jnp.max(scores, axis=-1, keepdims=True)
        exp_scores = jnp.exp(scores - row_peak)
        totals = jnp.sum(exp_scores, axis=-1, keepdims=True)
        prob_rows = (exp_scores / totals).astype(jnp.bfloat16)
        attended = jnp.einsum("hqk,khd->qhd", prob_rows, v_all, preferred_element_type=jnp.float32)
        return (attended.astype(jnp.bfloat16), row_peak[..., 0] + jnp.log(totals[..., 0]))

    attended, log_totals = lax.map(
        one_block, q_heads.reshape(block_count, block_rows, head_count, HEAD_DIM)
    )
    return (attended.reshape(seq_len, columns), log_totals)


def attend_backward(q_heads, k_heads, v_heads, d_heads, log_totals):
    seq_len, columns = q_heads.shape
    head_count = columns // HEAD_DIM
    block_rows = min(512, seq_len)
    block_count = seq_len // block_rows
    score_scale = HEAD_DIM ** (-0.5)
    k_all = k_heads.reshape(seq_len, head_count, HEAD_DIM)
    v_all = v_heads.reshape(seq_len, head_count, HEAD_DIM)
    q_blocks = q_heads.reshape(block_count, block_rows, head_count, HEAD_DIM)
    d_blocks = d_heads.reshape(block_count, block_rows, head_count, HEAD_DIM)

    def one_block(carry, item):
        key_acc, value_acc = carry
        q_block, d_block, lse_block = item
        scores = (
            jnp.einsum("qhd,khd->hqk", q_block, k_all, preferred_element_type=jnp.float32)
            * score_scale
        )
        prob_rows = jnp.exp(scores - lse_block[..., None])
        value_acc = value_acc + jnp.einsum(
            "hqk,qhd->khd",
            prob_rows.astype(jnp.bfloat16),
            d_block,
            preferred_element_type=jnp.float32,
        )
        d_probs = jnp.einsum("qhd,khd->hqk", d_block, v_all, preferred_element_type=jnp.float32)
        d_scores = (
            prob_rows * (d_probs - jnp.sum(prob_rows * d_probs, axis=-1, keepdims=True))
        ).astype(jnp.bfloat16)
        d_query = (
            jnp.einsum("hqk,khd->qhd", d_scores, k_all, preferred_element_type=jnp.float32)
            * score_scale
        )
        key_acc = (
            key_acc
            + jnp.einsum("hqk,qhd->khd", d_scores, q_block, preferred_element_type=jnp.float32)
            * score_scale
        )
        return ((key_acc, value_acc), d_query.astype(jnp.bfloat16))

    empty_acc = jnp.zeros((seq_len, head_count, HEAD_DIM), jnp.float32)
    (key_acc, value_acc), d_query = lax.scan(
        one_block, (empty_acc, empty_acc), (q_blocks, d_blocks, log_totals)
    )
    d_q = d_query.reshape(seq_len, columns)
    d_k = key_acc.astype(jnp.bfloat16).reshape(seq_len, columns)
    d_v = value_acc.astype(jnp.bfloat16).reshape(seq_len, columns)
    return (d_q, d_k, d_v)


def add_sources(received):
    return tuple((jnp.sum(piece, axis=0) for piece in received))


def per_device(
    inputs,
    positions,
    attn_gain,
    qkv_weight,
    attn_out_weight,
    mlp_gain,
    up_weight,
    down_weight,
    cotangent,
):
    layer = (
        lax.all_gather(attn_gain, ("dp", "seq"), axis=0, tiled=True),
        lax.all_gather(qkv_weight, ("dp", "seq"), axis=0, tiled=True),
        lax.all_gather(attn_out_weight, ("dp", "seq"), axis=0, tiled=True),
        lax.all_gather(mlp_gain, ("dp", "seq"), axis=0, tiled=True),
        lax.all_gather(up_weight, ("dp", "seq"), axis=0, tiled=True),
        lax.all_gather(down_weight, ("dp", "seq"), axis=0, tiled=True),
    )
    gain_one, w_qkv, w_out, gain_two, w_up, w_down = layer
    token_count = inputs.shape[1]
    resid_in = inputs[0].astype(jnp.float32)
    cos_table, sin_table = rope_tables(positions[0])
    normed_one, spread_one = normalize(resid_in)
    attn_in = (normed_one * gain_one.astype(jnp.float32)).astype(jnp.bfloat16)
    queries, key_rows, values = project_heads(attn_in, w_qkv, cos_table, sin_table)
    q_heads, k_heads, v_heads = (
        lax.all_to_all(queries, "seq", split_axis=1, concat_axis=0, tiled=True),
        lax.all_to_all(key_rows, "seq", split_axis=1, concat_axis=0, tiled=True),
        lax.all_to_all(values, "seq", split_axis=1, concat_axis=0, tiled=True),
    )
    attended_heads, log_totals = attend_forward(q_heads, k_heads, v_heads)
    attended = lax.all_to_all(attended_heads, "seq", split_axis=0, concat_axis=1, tiled=True)
    resid = resid_in + jnp.dot(attended, w_out, preferred_element_type=jnp.float32)
    normed_two, spread_two = normalize(resid)
    mlp_in = (normed_two * gain_two.astype(jnp.float32)).astype(jnp.bfloat16)
    up_rows = jnp.dot(mlp_in, w_up, preferred_element_type=jnp.float32)
    inner_act = up_rows[:, :FF]
    gate_act = up_rows[:, FF:]
    gelu_val, gelu_slope = gelu_parts(inner_act)
    hidden = (gelu_val * gate_act).astype(jnp.bfloat16)
    output = resid + jnp.einsum("tf,df->td", hidden, w_down, preferred_element_type=jnp.float32)
    layer_back = (
        lax.all_gather(attn_gain, ("dp", "seq"), axis=0, tiled=True),
        lax.all_gather(qkv_weight, ("dp", "seq"), axis=0, tiled=True),
        lax.all_gather(attn_out_weight, ("dp", "seq"), axis=0, tiled=True),
        lax.all_gather(mlp_gain, ("dp", "seq"), axis=0, tiled=True),
        lax.all_gather(up_weight, ("dp", "seq"), axis=0, tiled=True),
        lax.all_gather(down_weight, ("dp", "seq"), axis=0, tiled=True),
    )
    gain_one, w_qkv, w_out, gain_two, w_up, w_down = layer_back
    d_out = cotangent[0]
    down_grad = jnp.einsum("td,tf->df", d_out, hidden, preferred_element_type=jnp.float32)
    d_hidden = jnp.dot(d_out, w_down, preferred_element_type=jnp.float32)
    d_up = jnp.concatenate([d_hidden * gate_act * gelu_slope, d_hidden * gelu_val], axis=1).astype(
        jnp.bfloat16
    )
    up_grad = jnp.einsum("tk,tn->kn", mlp_in, d_up, preferred_element_type=jnp.float32)
    d_mlp_in = jnp.einsum("tn,kn->tk", d_up, w_up, preferred_element_type=jnp.float32)
    d_norm_two, gain_two_grad = norm_back(
        d_mlp_in, normed_two, spread_two, gain_two.astype(jnp.float32)
    )
    d_resid = d_out.astype(jnp.float32) + d_norm_two
    d_resid_low = d_resid.astype(jnp.bfloat16)
    out_grad = jnp.einsum("tk,tn->kn", attended, d_resid_low, preferred_element_type=jnp.float32)
    d_attended = jnp.einsum(
        "tn,kn->tk", d_resid_low, w_out, preferred_element_type=jnp.float32
    ).astype(jnp.bfloat16)
    d_heads = lax.all_to_all(d_attended, "seq", split_axis=1, concat_axis=0, tiled=True)
    queries, key_rows, values = project_heads(attn_in, w_qkv, cos_table, sin_table)
    head_inputs = (
        lax.all_to_all(queries, "seq", split_axis=1, concat_axis=0, tiled=True),
        lax.all_to_all(key_rows, "seq", split_axis=1, concat_axis=0, tiled=True),
        lax.all_to_all(values, "seq", split_axis=1, concat_axis=0, tiled=True),
    )
    d_q, d_k, d_v = attend_backward(
        head_inputs[0], head_inputs[1], head_inputs[2], d_heads, log_totals
    )
    dq_rows, dk_rows, dv_rows = (
        lax.all_to_all(d_q, "seq", split_axis=0, concat_axis=1, tiled=True),
        lax.all_to_all(d_k, "seq", split_axis=0, concat_axis=1, tiled=True),
        lax.all_to_all(d_v, "seq", split_axis=0, concat_axis=1, tiled=True),
    )
    shaped = (token_count, HEADS, HEAD_DIM)
    dq_pre = rotate_back(dq_rows.astype(jnp.float32).reshape(shaped), cos_table, sin_table).reshape(
        token_count, -1
    )
    dk_pre = rotate_back(dk_rows.astype(jnp.float32).reshape(shaped), cos_table, sin_table).reshape(
        token_count, -1
    )
    d_mixed = jnp.concatenate(
        [dq_pre.astype(jnp.bfloat16), dk_pre.astype(jnp.bfloat16), dv_rows], axis=1
    )
    qkv_grad = jnp.einsum("tk,tn->kn", attn_in, d_mixed, preferred_element_type=jnp.float32)
    d_attn_in = jnp.einsum("tn,kn->tk", d_mixed, w_qkv, preferred_element_type=jnp.float32)
    d_norm_one, gain_one_grad = norm_back(
        d_attn_in, normed_one, spread_one, gain_one.astype(jnp.float32)
    )
    input_grad = (d_resid + d_norm_one).astype(jnp.bfloat16)
    all_sent = (
        lax.all_to_all(
            gain_one_grad[None].astype(jnp.bfloat16), "dp", split_axis=1, concat_axis=0, tiled=True
        ).astype(jnp.float32),
        lax.all_to_all(
            qkv_grad[None].astype(jnp.bfloat16), "dp", split_axis=1, concat_axis=0, tiled=True
        ).astype(jnp.float32),
        lax.all_to_all(
            out_grad[None].astype(jnp.bfloat16), "dp", split_axis=1, concat_axis=0, tiled=True
        ).astype(jnp.float32),
        lax.all_to_all(
            gain_two_grad[None].astype(jnp.bfloat16), "dp", split_axis=1, concat_axis=0, tiled=True
        ).astype(jnp.float32),
        lax.all_to_all(
            up_grad[None].astype(jnp.bfloat16), "dp", split_axis=1, concat_axis=0, tiled=True
        ).astype(jnp.float32),
        lax.all_to_all(
            down_grad[None].astype(jnp.bfloat16), "dp", split_axis=1, concat_axis=0, tiled=True
        ).astype(jnp.float32),
    )
    grads = jax.tree.map(
        lambda part: part.astype(jnp.float32),
        lax.psum_scatter(
            for_sending(add_sources(all_sent)), "seq", scatter_dimension=0, tiled=True
        ),
    )
    return (
        output.astype(jnp.bfloat16)[None],
        input_grad[None],
        grads[0],
        grads[1],
        grads[2],
        grads[3],
        grads[4],
        grads[5],
    )


QUAD_MESH = (8, 4)
FLAT = ("y", "x", "c", "zh", "zl")
LOW, WIDE = jnp.bfloat16, jnp.float32


def pairs_of(step):
    found = []
    for dp in range(8):
        for seq in range(4):
            place = (dp // 4, dp // 2 % 2, dp % 2, seq // 2, seq % 2)
            target = step(*place)
            if target is not None:
                y, x, c, zh, zl = target
                found.append((dp * 4 + seq, (4 * y + 2 * x + c) * 4 + 2 * zh + zl))
    return found


TO_X = pairs_of(lambda y, x, c, zh, zl: (y, 1 - x, c, zh, zl))
TO_Y = pairs_of(lambda y, x, c, zh, zl: (1 - y, x, c, zh, zl))
TO_XY = pairs_of(lambda y, x, c, zh, zl: (1 - y, 1 - x, c, zh, zl))
TO_CORE = pairs_of(lambda y, x, c, zh, zl: (y, x, 1 - c, zh, zl))
TO_ZH = pairs_of(lambda y, x, c, zh, zl: (y, x, c, 1 - zh, zl))
TO_ZL = pairs_of(lambda y, x, c, zh, zl: (y, x, c, zh, 1 - zl))
TO_FAR = pairs_of(lambda y, x, c, zh, zl: (y, x, 1 - c, zh, 1 - zl))
TO_HOME = pairs_of(lambda y, x, c, zh, zl: (y, x, zh, c, zl))
ENTER = pairs_of(
    lambda y, x, c, zh, zl: (y, x, c, zh, 1 - zl) if c == zh else (y, x, zh, c, zl)
)
ENTER_MOVED = pairs_of(lambda y, x, c, zh, zl: None if c == zh else (y, x, c, zh, 1 - zl))


class Order(list):
    pass


def send(array, pairs):
    return lax.ppermute(array, FLAT, pairs)


def after(order, array):
    return lax.optimization_barrier((array, order[0]))[0]


def wait(order, *arrays):
    order[0] = lax.optimization_barrier((order[0], *arrays))[0]


def lanes(size):
    return -(-size // 128) * 128


def core_of(flat):
    return flat >> 2 & 1


def half_of(flat):
    return flat >> 1 & 1


def group_of(flat):
    return 2 * core_of(flat) + (flat & 1)


def square_of(flat):
    return flat >> 3


def mm(left, right):
    return lax.dot_general(left, right, (((1,), (0,)), ((), ())), preferred_element_type=WIDE)


def mm_t(left, right):
    return lax.dot_general(left, right, (((1,), (1,)), ((), ())), preferred_element_type=WIDE)


def t_mm(left, right):
    return lax.dot_general(left, right, (((0,), (0,)), ((), ())), preferred_element_type=WIDE)


def window(index, size):
    return pl.ds(pl.multiple_of(index * size, size), size)


def whole(array):
    rank = len(array.shape)
    return (array, array.shape, lambda *_: (0,) * rank)


def by_rows(array, rows, step=lambda b: b):
    return (array, (rows,) + array.shape[1:], lambda b, f: (step(b),) + (0,) * (len(array.shape) - 1))


def run(body, order, grid, ins, outs, scratch=(), flops=0, spare=6 * 2**20):
    moved = sum(a.size * a.dtype.itemsize for a, _, _ in ins)
    moved += sum(a.size * a.dtype.itemsize for a, _, _ in outs)
    def held(block, dtype, count):
        return count * math.prod(block) * jnp.dtype(dtype).itemsize

    grant = sum(
        held(block, a.dtype, 1 if tuple(block) == tuple(a.shape) else 2)
        for a, block, _ in (*ins, *outs)
    )
    grant += sum(held(m.shape, m.dtype, 1) for m in scratch) + spare
    made = pl.pallas_call(
        body,
        grid_spec=pltpu.PrefetchScalarGridSpec(
            num_scalar_prefetch=1,
            grid=grid,
            in_specs=[pl.BlockSpec(block, index) for _, block, index in ins],
            out_specs=[pl.BlockSpec(block, index) for _, block, index in outs],
            scratch_shapes=list(scratch),
        ),
        out_shape=[a for a, _, _ in outs],
        compiler_params=pltpu.CompilerParams(vmem_limit_bytes=grant),
        cost_estimate=pl.CostEstimate(flops=flops // 100, bytes_accessed=moved // 100, transcendentals=0),
    )(order[0], *[a for a, _, _ in ins])
    order[0], _ = lax.optimization_barrier((order[0], made[0]))
    return made


def spans(pieces):
    rows = pieces[0].shape[0]
    return [(0, 0, rows), (1, 0, rows), (2, 0, rows), (3, 0, rows // 2), (3, rows // 2, rows // 2)]


def rows_of(ref, span):
    count = span[2]
    return slice(ref.shape[0] - count, None) if span[1] else slice(0, count)


def span_of(square, span, rows):
    index, first, count = span
    return pl.ds(pl.multiple_of((square ^ index) * rows + first, count), count)


def shape_of(*dims, dtype=LOW):
    return jax.ShapeDtypeStruct(dims, dtype)


def column_of(row):
    size = row.shape[1]
    down = lax.broadcasted_iota(jnp.int32, (size, size), 0)
    across = lax.broadcasted_iota(jnp.int32, (size, size), 1)
    return jnp.sum(jnp.where(down == across, row, 0.0), axis=1, keepdims=True)


def row_of(column):
    size = column.shape[0]
    down = lax.broadcasted_iota(jnp.int32, (size, size), 0)
    across = lax.broadcasted_iota(jnp.int32, (size, size), 1)
    return jnp.sum(jnp.where(down == across, column, 0.0), axis=0, keepdims=True)


def normed_of(x):
    centred = x - jnp.mean(x, axis=-1, keepdims=True)
    spread = lax.rsqrt(jnp.mean(centred * centred, axis=-1, keepdims=True) + norm_eps)
    return centred * spread, spread


def split_slices(order, scaled, plain, gain, parts):
    rows, part, rest = scaled.shape[0], scaled.shape[1] // (4 * parts), plain.shape[1] // 4
    out = shape_of(2, rows, lanes(parts * part + rest))

    def body(flat_ref, scaled_ref, plain_ref, gain_ref, own_ref, sent_ref, held):
        scale = column_of(gain_ref[...].astype(WIDE))
        for s in range(4):
            for t in range(parts):
                cols = scaled_ref[:, (4 * t + s) * part : (4 * t + s + 1) * part].astype(WIDE)
                held[s, :, t * part : (t + 1) * part] = (cols * scale).astype(LOW)
            held[s, :, parts * part : parts * part + rest] = plain_ref[
                :, s * rest : (s + 1) * rest
            ]
        core = core_of(flat_ref[0])
        for zl in range(2):
            own_ref[zl] = held[2 * core + zl]
            sent_ref[zl] = held[2 * (1 - core) + zl]

    return run(
        body, order, (1,), [whole(a) for a in (scaled, plain, gain)], [whole(out)] * 2,
        [pltpu.VMEM((4, *out.shape[1:]), LOW)],
    )


def chip_rows(order, own, received):
    def body(flat_ref, own_ref, received_ref, kept_ref, sent_ref):
        core, chip = core_of(flat_ref[0]), flat_ref[0] & 1
        kept_ref[core] = own_ref[chip]
        kept_ref[1 - core] = received_ref[chip]
        sent_ref[core] = own_ref[1 - chip]
        sent_ref[1 - core] = received_ref[1 - chip]

    return run(
        body, order, (1,), [whole(own), whole(received)], [whole(shape_of(*own.shape))] * 2
    )


def quad_rows(order, own, received):
    _, rows, width = own.shape

    def body(flat_ref, own_ref, received_ref, out_ref):
        chip = flat_ref[0] & 1
        for c in range(2):
            out_ref[2 * c + chip] = own_ref[c]
            out_ref[2 * c + 1 - chip] = received_ref[c]

    return run(
        body, order, (1,), [whole(own), whole(received)], [whole(shape_of(4, rows, width))]
    )[0]


def line_rows(order, near, far):
    _, rows, width = near.shape
    near = near.reshape(2, 2 * rows, width)
    far = far.reshape(2, 2 * rows, width)

    def body(flat_ref, near_ref, far_ref, out_ref):
        half = half_of(flat_ref[0])
        for c in range(2):
            out_ref[c, half] = near_ref[c]
            out_ref[c, 1 - half] = far_ref[c]

    out = run(
        body, order, (1,), [whole(near), whole(far)], [whole(shape_of(2, 2, 2 * rows, width))]
    )[0]
    return out.reshape(8 * rows, width)


def join_tokens(order, parts, rows, extra=0):
    width = parts[0].shape[1]

    def body(flat_ref, block, first, second, core_block, core_first, core_second, *outs):
        home = core_of(flat_ref[0]) == half_of(flat_ref[0])
        here = (block, first, core_first, core_second)
        moved = (first, second, core_block, core_first)
        for k in range(4):
            for flag, source in ((home, here[k]), (jnp.logical_not(home), moved[k])):

                @pl.when(jnp.logical_and(pl.program_id(0) == k, flag))
                def _(source=source):
                    def step(r, carry):
                        outs[0][window(r, 32), :] = source[window(r, 32), :]
                        return carry

                    lax.fori_loop(0, rows // 32, step, 0)
                    if extra:
                        outs[1][...] = source[rows : rows + extra, :]

    made = [shape_of(4 * rows, width)] + ([shape_of(4 * extra, width)] if extra else [])
    return run(
        body, order, (4,), [whole(a) for a in parts],
        [by_rows(m, m.shape[0] // 4) for m in made],
    )


def rope_lanes(seq_pos):
    exponent = jnp.arange(0, HEAD_DIM, 2).astype(WIDE) / HEAD_DIM
    angles = seq_pos[:, None] * (rope_base ** (-exponent))[None, :]
    cos_half, sin_half = jnp.cos(angles), jnp.sin(angles)
    return (
        jnp.concatenate([cos_half] * 4, axis=1),
        jnp.concatenate([-sin_half, sin_half] * 2, axis=1),
    )


def turned(v):
    half = HEAD_DIM // 2
    lane = lax.broadcasted_iota(jnp.int32, v.shape, 1)
    return jnp.where(
        lane % HEAD_DIM < half, pltpu.roll(v, 2 * HEAD_DIM - half, 1), pltpu.roll(v, half, 1)
    )


def project(order, x, pieces, cos_table, sin_table):
    tokens, width = x.shape
    piece, columns = pieces[0].shape[0], 3 * width // 4
    rows = tokens // 4

    def body(flat_ref, x_ref, *refs):
        weights, (cos_ref, sin_ref, n_ref, mix_ref) = refs[:5], refs[5:]
        n_ref[...] = normed_of(x_ref[...].astype(WIDE))[0].astype(LOW)
        square = square_of(flat_ref[0])
        mixed = sum(
            mm(n_ref[:, span_of(square, span, piece)], w[rows_of(w, span), :columns])
            for span, w in zip(spans(pieces), weights)
        )
        turned_to = 2 * columns // 3
        for t in range(0, turned_to, 128):
            v = mixed[:, t : t + 128]
            mix_ref[:, t : t + 128] = (v * cos_ref[...] + turned(v) * sin_ref[...]).astype(LOW)
        mix_ref[:, turned_to:] = mixed[:, turned_to:].astype(LOW)

    return run(
        body, order, (4,),
        [by_rows(x, rows)] + [whole(p) for p in pieces]
        + [by_rows(cos_table, rows), by_rows(sin_table, rows)],
        [by_rows(shape_of(tokens, width), rows), by_rows(shape_of(tokens, columns), rows)],
        flops=2 * tokens * width * columns,
    )


def attend(order, mix):
    tokens, columns = mix.shape
    part = columns // 3
    rows = tokens // 4
    scale = HEAD_DIM ** (-0.5)

    def body(flat_ref, q_ref, k_ref, v_ref, out_ref, log_ref):
        lane = lax.broadcasted_iota(jnp.int32, (rows, part), 1) // HEAD_DIM
        total = jnp.zeros((rows, part), WIDE)
        queries = q_ref[...].astype(WIDE) * scale
        for h in range(part // HEAD_DIM):
            q_head = jnp.where(lane == h, queries, 0.0).astype(LOW)
            scores = mm_t(q_head, k_ref[...])
            peak = jnp.max(scores, axis=-1, keepdims=True)
            powers = jnp.exp(scores - peak)
            mass = jnp.sum(powers, axis=-1, keepdims=True)
            probs = (powers * (1.0 / mass)).astype(LOW)
            total = jnp.where(lane == h, mm(probs, v_ref[...]), total)
            log_ref[h : h + 1, :] = row_of(peak + jnp.log(mass))
        out_ref[...] = total.astype(LOW)

    return run(
        body, order, (4,),
        [
            (mix, (rows, part), lambda b, f: (b, 0)),
            (mix, (tokens, part), lambda b, f: (0, 1)),
            (mix, (tokens, part), lambda b, f: (0, 2)),
        ],
        [
            by_rows(shape_of(tokens, part), rows),
            (shape_of(8, tokens, dtype=WIDE), (8, rows), lambda b, f: (0, b)),
        ],
        flops=16 * tokens * tokens * part,
    )


def token_parts(arrays, rows):
    return [by_rows(a, rows, lambda b, i=i: b ^ i) for i, a in enumerate(arrays)]


def join_heads(order, x, heads, columns):
    tokens, width = x.shape
    rows, part = tokens // 4, width // 4

    def body(flat_ref, x_ref, *refs):
        parts, weights, (n_ref, own_ref, held) = refs[:4], refs[4:8], refs[8:]
        group, square = group_of(flat_ref[0]), square_of(flat_ref[0])
        for j in range(4):
            cols = window(group ^ j, part)
            held[:, cols] = x_ref[:, cols].astype(WIDE) + sum(
                mm(parts[i][...], weights[j][window(group ^ i ^ square, part), :])
                for i in range(4)
            )
        resid = held[...]
        n_ref[...] = normed_of(resid)[0].astype(LOW)

        @pl.when(pl.program_id(0) == 0)
        def _():
            own_ref[...] = held[...]

    return run(
        body, order, (4,),
        [by_rows(x, rows)] + token_parts(heads, rows) + [whole(w) for w in columns],
        [by_rows(shape_of(tokens, width), rows), whole(shape_of(rows, width, dtype=WIDE))],
        [pltpu.VMEM((rows, width), WIDE)],
        flops=2 * tokens * width * width,
    )


def feed(order, normed, cot, pieces):
    tokens, width = normed.shape
    piece, ff = pieces[0].shape[0], FF // 4
    rows = tokens // 4

    def body(flat_ref, n_ref, cot_ref, *refs):
        weights, (h_ref, d_ref) = refs[:5], refs[5:]
        square = square_of(flat_ref[0])
        cut = [
            (span_of(square, span, piece), rows_of(w, span), w)
            for span, w in zip(spans(pieces), weights)
        ]
        wide = sum(mm(n_ref[:, at], w[of, : 2 * ff]) for at, of, w in cut)
        d_hidden = sum(mm(cot_ref[:, at], w[of, 2 * ff : 3 * ff]) for at, of, w in cut)
        inner, gate = wide[:, :ff], wide[:, ff:]
        cdf = 0.5 * (1.0 + lax.erf(inner * inv_root_two))
        slope = cdf + inner * jnp.exp(-0.5 * inner * inner) * inv_root_tau
        bent = inner * cdf
        h_ref[...] = (bent * gate).astype(LOW)
        d_ref[:, :ff] = (d_hidden * gate * slope).astype(LOW)
        d_ref[:, ff:] = (d_hidden * bent).astype(LOW)

    return run(
        body, order, (4,),
        [by_rows(normed, rows), by_rows(cot, rows)] + [whole(w) for w in pieces],
        [by_rows(shape_of(tokens, ff), rows), by_rows(shape_of(tokens, 2 * ff), rows)],
        flops=6 * tokens * width * ff,
    )


def back_half(order, grads, pieces, far):
    tokens = grads[0][0].shape[0]
    piece = pieces[0].shape[0]
    rows, width, count = tokens // 2, 4 * piece, len(grads)
    out = shape_of(rows, width, dtype=LOW if far else WIDE)

    def body(flat_ref, *refs):
        arrays, weights, out_ref = refs[:count], refs[count : count + 5], refs[count + 5]
        square = square_of(flat_ref[0])
        for span, w in zip(spans(pieces), weights):
            out_ref[:, span_of(square, span, piece)] = sum(
                mm_t(a[...], w[rows_of(w, span), at : at + a.shape[1]])
                for a, (_, at) in zip(arrays, grads)
            ).astype(out.dtype)

    return run(
        body, order, (1,),
        [by_rows(a, rows, lambda b: int(far)) for a, _ in grads] + [whole(p) for p in pieces],
        [whole(out)],
        flops=tokens * width * sum(a.shape[1] for a, _ in grads),
    )[0]


def back_both(order, grad, first, pieces):
    tokens = grad.shape[0]
    piece = pieces[0].shape[0]
    rows, width, columns = tokens // 2, 4 * piece, grad.shape[1]

    def body(flat_ref, grad_ref, *refs):
        weights, (far_ref, near_ref) = refs[:5], refs[5:]
        square = square_of(flat_ref[0])
        for span, w in zip(spans(pieces), weights):
            total = mm_t(grad_ref[...], w[rows_of(w, span), first : first + columns])
            near_ref[:, span_of(square, span, piece)] = total[:rows]
            far_ref[:, span_of(square, span, piece)] = total[rows:].astype(LOW)

    return run(
        body, order, (1,), [whole(grad)] + [whole(p) for p in pieces],
        [whole(shape_of(rows, width)), whole(shape_of(rows, width, dtype=WIDE))],
        flops=2 * tokens * width * columns,
    )


def norm_pull(order, x, terms, base, keep):
    rows, width = base.shape[0] // (4 if keep else 1), base.shape[1]
    step = rows // 4

    def body(flat_ref, x_ref, a_ref, b_ref, c_ref, base_ref, *outs):
        normed, spread = normed_of(x_ref[...].astype(WIDE))
        scaled = a_ref[...] + b_ref[...].astype(WIDE) + c_ref[...].astype(WIDE)
        grad = base_ref[...].astype(WIDE) + spread * (
            scaled
            - jnp.mean(scaled, axis=-1, keepdims=True)
            - normed * jnp.mean(scaled * normed, axis=-1, keepdims=True)
        )
        outs[0][...] = grad.astype(LOW)
        if keep:
            outs[1][...] = grad

    low = shape_of(rows + 16 if keep else rows, width)
    outs = [low] + ([shape_of(rows, width, dtype=WIDE)] if keep else [])
    return run(
        body, order, (4,), [by_rows(a, step) for a in (x, *terms, base)],
        [by_rows(o, step) for o in outs],
    )


def feed_grads(order, normed, cot, d_up, hidden):
    tokens, width = normed.shape
    piece, ff = width // 4, hidden.shape[1]
    out = shape_of(4, piece, lanes(3 * ff))

    def body(flat_ref, n_ref, cot_ref, d_ref, h_ref, out_ref):
        out_ref[0, :, : 2 * ff] = t_mm(n_ref[...], d_ref[...]).astype(LOW)
        out_ref[0, :, 2 * ff : 3 * ff] = t_mm(cot_ref[...], h_ref[...]).astype(LOW)

    return run(
        body, order, (4,),
        [(a, (tokens, piece), lambda b, f: (0, b)) for a in (normed, cot)]
        + [whole(d_up), whole(hidden)],
        [by_rows(out, 1)],
        flops=6 * tokens * width * ff,
    )[0]


def heads_back(order, d_all, heads, columns):
    rows, width = heads[0].shape[0] // 4, d_all[0].shape[1]
    part = width // 4

    def body(flat_ref, *refs):
        blocks, parts, weights = refs[:4], refs[4:8], refs[8:12]
        d_ref, grad_ref, block, held, total = refs[12:]
        group, square = group_of(flat_ref[0]), square_of(flat_ref[0])
        at = pl.program_id(0)
        for k in range(4):

            @pl.when(at == k)
            def _(source=blocks[k]):
                def step(r, carry):
                    block[window(r, 32), :] = source[window(r, 32), :]
                    return carry

                lax.fori_loop(0, rows // 32, step, 0)

            held[k] = parts[k][...]

        @pl.when(at == 0)
        def _():
            total[...] = jnp.zeros_like(total)

        d_ref[...] = sum(
            mm_t(block[:, window(group ^ j, part)], weights[j][window(group ^ square, part), :])
            for j in range(4)
        ).astype(LOW)
        mine = block[:, window(group, part)]
        for i in range(4):
            total[i] += t_mm(held[group ^ square ^ i], mine)

        @pl.when(at == 3)
        def _():
            grad_ref[...] = total[...].astype(LOW)

    return run(
        body, order, (4,),
        [whole(d) for d in d_all] + token_parts(heads, rows) + [whole(w) for w in columns],
        [by_rows(shape_of(4 * rows, part), rows), whole(shape_of(4, part, part))],
        [
            pltpu.VMEM((rows, width), LOW),
            pltpu.VMEM((4, rows, part), LOW),
            pltpu.VMEM((4, part, part), WIDE),
        ],
        flops=4 * 4 * rows * width * part,
    )


def attend_back(order, mix, attended, d_attended, logs, cos_table, sin_table):
    tokens, columns = mix.shape
    part = columns // 3
    rows = tokens // 4
    scale = HEAD_DIM ** (-0.5)
    heads = part // HEAD_DIM

    def rotated(grad, cos, sin):
        halves = [grad[:, t : t + 128] for t in range(0, part, 128)]
        return jnp.concatenate([v * cos - turned(v) * sin for v in halves], axis=1).astype(LOW)

    def body(flat_ref, q_ref, k_ref, v_ref, o_ref, d_ref, log_ref, cos_ref, sin_ref, *refs):
        dq_ref, dk_ref, dv_ref, k_total, v_total = refs
        at = pl.program_id(0)

        @pl.when(at == 0)
        def _():
            k_total[...] = jnp.zeros_like(k_total)
            v_total[...] = jnp.zeros_like(v_total)

        lane = lax.broadcasted_iota(jnp.int32, (rows, part), 1) // HEAD_DIM
        queries = q_ref[...].astype(WIDE) * scale
        grads = d_ref[...].astype(WIDE)
        chosen = lax.broadcasted_iota(jnp.int32, (8, part), 0) == (
            lax.broadcasted_iota(jnp.int32, (8, part), 1) // HEAD_DIM
        )
        deltas = lax.dot_general(
            chosen.astype(WIDE), grads * o_ref[...].astype(WIDE), (((1,), (1,)), ((), ())),
            precision=lax.Precision.HIGHEST, preferred_element_type=WIDE,
        )
        d_query = jnp.zeros((rows, part), WIDE)
        for h in range(heads):
            q_head = jnp.where(lane == h, queries, 0.0).astype(LOW)
            d_head = jnp.where(lane == h, grads, 0.0).astype(LOW)
            probs = jnp.exp(mm_t(k_ref[...], q_head) - log_ref[h : h + 1, :])
            d_probs = mm_t(v_ref[...], d_head)
            d_scores = (probs * (d_probs - deltas[h : h + 1, :])).astype(LOW)
            v_total[...] += mm(probs.astype(LOW), d_head)
            k_total[...] += mm(d_scores, q_head)
            d_query = jnp.where(lane == h, t_mm(d_scores, k_ref[...]), d_query)
        here = window(at, rows)
        dq_ref[...] = rotated(d_query * scale, cos_ref[here, :], sin_ref[here, :])

        @pl.when(at == 3)
        def _():
            dk_ref[...] = rotated(k_total[...], cos_ref[...], sin_ref[...])
            dv_ref[...] = v_total[...].astype(LOW)

    out = shape_of(tokens, part)
    return run(
        body, order, (4,),
        [
            (mix, (rows, part), lambda b, f: (b, 0)),
            (mix, (tokens, part), lambda b, f: (0, 1)),
            (mix, (tokens, part), lambda b, f: (0, 2)),
            by_rows(attended, rows),
            by_rows(d_attended, rows),
            (logs, (8, rows), lambda b, f: (0, b)),
            whole(cos_table),
            whole(sin_table),
        ],
        [by_rows(out, rows), whole(out), whole(out)],
        [pltpu.VMEM((tokens, part), WIDE)] * 2,
        flops=40 * tokens * tokens * part,
    )


def mixed_grads(order, normed, d_mixed, out_grad):
    tokens, width = normed.shape
    rows, piece = tokens // 4, width // 4
    part = d_mixed[0].shape[1]

    def body(flat_ref, n_ref, *refs):
        grads, out_ref, outs, held = refs[:3], refs[3], refs[4:8], refs[8]
        square = square_of(flat_ref[0])

        @pl.when(pl.program_id(0) == 0)
        def _():
            held[...] = jnp.zeros_like(held)

        for i in range(4):
            cols = n_ref[:, window(square ^ i, piece)]
            for t in range(3):
                held[i, :, t * part : (t + 1) * part] += t_mm(cols, grads[t][...])

        @pl.when(pl.program_id(0) == 3)
        def _():
            for i in range(4):
                outs[i][:, : 3 * part] = held[i].astype(LOW)
                outs[i][:, 3 * part :] = out_ref[i]

    return run(
        body, order, (4,),
        [by_rows(normed, rows)] + [by_rows(d, rows) for d in d_mixed] + [whole(out_grad)],
        [whole(shape_of(piece, 4 * part))] * 4, [pltpu.VMEM((4, piece, 3 * part), WIDE)],
        flops=6 * tokens * width * part,
    )


def share_slices(slices):
    return [slices[0]] + [
        send(slices[i], pairs) for i, pairs in ((1, TO_ZL), (2, TO_CORE), (3, TO_FAR))
    ]


def share_pieces(pieces):
    return [pieces[0]] + [
        send(pieces[i], pairs) for i, pairs in ((1, TO_X), (2, TO_Y), (3, TO_XY))
    ]


def fold(order, terms, margin=0):
    high, width = terms[0].shape[1:]
    rows = high // 4
    terms = [t.reshape(-1, 2, 2, rows, width) for t in terms]

    def body(flat_ref, *refs):
        ins, (kept_ref, sent_ref) = refs[:-2], refs[-2:]
        half = half_of(flat_ref[0])

        def total(at):
            return sum(r[k, 0, at].astype(WIDE) for r in ins for k in range(r.shape[0]))

        kept_ref[0] = total(half)
        sent_ref[0, :, :width] = total(1 - half).astype(LOW)

    return run(
        body, order, (2,),
        [
            (t, (t.shape[0], 1) + t.shape[2:], lambda b, f: (0, b, 0, 0, 0))
            for t in terms
        ],
        [
            by_rows(shape_of(2, rows, width, dtype=WIDE), 1),
            by_rows(shape_of(2, rows, width + margin), 1),
        ],
    )


def split_rows(order, kept, received):
    _, high, width = kept.shape
    rows = high // 2
    kept, received = kept.reshape(4, rows, width), received.reshape(4, rows, -1)

    def body(flat_ref, kept_ref, received_ref, *outs):
        for i in range(4):
            at = group_of(flat_ref[0]) ^ i
            outs[i][...] = (
                kept_ref[at] + received_ref[at, :, :width].astype(WIDE)
            ).astype(LOW)

    return run(
        body, order, (1,), [whole(kept), whole(received)], [whole(shape_of(rows, width))] * 4
    )


def finish(order, slices, weight, gain, sizes):
    rows, width = slices[0].shape
    count, part, rest = sizes

    def body(flat_ref, *refs):
        w_ref, gain_ref, scaled_ref, gain_out, plain_ref, held = refs[4:]
        for i in range(4):
            held[group_of(flat_ref[0]) ^ i] = refs[i][...].astype(WIDE)
        total = jnp.zeros((rows, 1), WIDE)
        scale = column_of(gain_ref[...].astype(WIDE))
        for s in range(4):
            for t in range(count):
                at = (4 * t + s) * part
                grad = held[s, :, t * part : (t + 1) * part]
                total += jnp.sum(
                    grad * w_ref[:, at : at + part].astype(WIDE), axis=1, keepdims=True
                )
                scaled_ref[:, at : at + part] = grad * scale
            plain_ref[:, s * rest : (s + 1) * rest] = held[s, :, count * part : count * part + rest]
        gain_out[...] = row_of(total)

    return run(
        body, order, (1,), [whole(a) for a in (*slices, weight, gain)],
        [
            whole(shape_of(*weight.shape, dtype=WIDE)),
            whole(shape_of(1, rows, dtype=WIDE)),
            whole(shape_of(rows, 4 * rest, dtype=WIDE)),
        ],
        [pltpu.VMEM((4, rows, width), WIDE)],
    )


def quad_device(
    inputs,
    positions,
    attn_gain,
    qkv_weight,
    attn_out_weight,
    mlp_gain,
    up_weight,
    down_weight,
    cotangent,
):
    order = Order([lax.axis_index(FLAT).astype(jnp.int32).reshape(1)])
    tokens, width = inputs.shape[1:]
    part, ff = width // 4, FF // 4
    gain_one, gain_two = attn_gain[None], mlp_gain[None]

    pos = positions[0]
    pos_row = jnp.concatenate([pos // 128, pos % 128]).astype(LOW)
    pos_row = jnp.pad(pos_row[None], ((0, 15), (0, width - 2 * tokens)))
    block = jnp.concatenate([inputs[0], pos_row])
    first = send(block, ENTER)
    wait(order, block)
    own, sent = split_slices(order, qkv_weight, attn_out_weight, gain_one, 3)
    received = send(sent, TO_CORE)
    own_two, sent = split_slices(order, up_weight, down_weight, gain_two, 2)
    received_two = send(sent, TO_CORE)
    core_block = send(block, TO_CORE)
    cot_own = jnp.concatenate([cotangent[0], pos_row])
    cot_block = send(cot_own, TO_CORE)
    own, sent = chip_rows(order, own, received)
    received = send(sent, TO_ZL)
    own_two, sent = chip_rows(order, own_two, received_two)
    wait(order, core_block, cot_block)
    one = quad_rows(order, own, received)
    one_far = send(one, TO_ZH)
    received_two = send(after(order, sent), TO_ZL)
    second = send(after(order, first), ENTER_MOVED)
    core_first = send(after(order, first), TO_CORE)
    two = quad_rows(order, own_two, received_two)
    two_far = send(two, TO_ZH)
    one = line_rows(order, one, one_far)
    half = one.shape[0] // 2
    one_x, one_y = send(one, TO_X), send(one, TO_Y)
    wait(order, core_first, second)
    core_second = send(after(order, second), TO_CORE)
    cot_first = send(after(order, cot_own), ENTER)
    one_top = send(one_x[:half], TO_Y)
    one_low = send(one_y[half:], TO_X)
    x, pos_all = join_tokens(
        order, [block, first, second, core_block, core_first, core_second], tokens, 16
    )
    pos_all = pos_all.reshape(4, 16, width)[:, 0, : 2 * tokens].astype(WIDE)
    pos_all = (pos_all[:, :tokens] * 128.0 + pos_all[:, tokens:]).reshape(4 * tokens)
    cos_table, sin_table = rope_lanes(pos_all)
    one = [one, one_x, one_y, one_top, one_low]

    w_out = jnp.concatenate([p[:, 3 * part :] for p in one])
    w_side = send(w_out, TO_ZL)
    w_core = send(w_out, TO_CORE)
    normed_one, mix = project(order, x, one, cos_table, sin_table)
    two = line_rows(order, two, two_far)
    two_x, two_y = send(two, TO_X), send(two, TO_Y)
    wait(order, w_core, w_side)
    w_far = send(w_side, TO_CORE)
    attended, logs = attend(order, mix)
    att_side = send(attended, TO_ZL)
    wait(order, two_x, two_y)
    two_top = send(after(order, two_x[: half + 16]), TO_Y)
    two_low = send(after(order, two_y[half - 16 :]), TO_X)
    att_core = send(after(order, attended), TO_CORE)
    wait(order, w_far, att_side)
    cot_second = send(after(order, cot_first), ENTER_MOVED)
    w_out = [w_out, w_side, w_core, w_far]
    heads = [attended, att_side, att_core, send(after(order, att_side), TO_CORE)]
    normed_two, resid = join_heads(order, x, heads, w_out)

    core_first = send(cot_first, TO_CORE)
    core_second = send(cot_second, TO_CORE)
    (cot,) = join_tokens(
        order,
        [cot_own, cot_first, cot_second, cot_block, core_first, core_second],
        tokens,
    )
    two = [two, two_x, two_y, two_top, two_low]
    hidden, d_up = feed(order, normed_two, cot, two)

    def crossed(far):
        return send(far, TO_CORE)

    def side_of(near, far):
        return send((near[tokens:] + far[tokens:].astype(WIDE)).astype(LOW), TO_ZL)

    grads = [(d_up, 0)]
    far = crossed(back_half(order, grads, two, True))
    near = back_half(order, grads, two, False)
    side = side_of(near, far)
    ff_terms = feed_grads(order, normed_two, cot, d_up, hidden)
    d_low, d_resid = norm_pull(order, resid, (near, far, side), cot, True)
    ff_terms = lax.all_to_all(
        after(order, ff_terms), ("y", "x"), split_axis=0, concat_axis=0, tiled=True
    )
    d_side = send(d_low, TO_ZL)
    d_core = send(d_low, TO_CORE)
    out_far, out_near = back_both(order, hidden, 2 * ff, two)
    out_far = [crossed(out_far[:tokens]), crossed(out_far[tokens:])]
    out_side = (out_near[tokens:] + out_far[1].astype(WIDE)).astype(LOW)
    out_side = send(out_side, TO_ZL)
    d_all = [d_low, d_side, d_core, send(after(order, d_side), TO_CORE)]
    d_attended, out_grad = heads_back(order, d_all, heads, w_out)
    d_mixed = attend_back(order, mix, attended, d_attended, logs, cos_table, sin_table)
    wait(order, out_side)
    grads = [(d, t * part) for t, d in enumerate(d_mixed)]
    far = crossed(back_half(order, grads, one, True))
    output = resid + out_near[:tokens] + out_far[0].astype(WIDE) + out_side.astype(WIDE)
    output = output.astype(LOW)
    wait(order, output)
    output = send(output, TO_HOME)
    near = back_half(order, grads, one, False)
    side = (near[tokens:] + far[tokens:].astype(WIDE)).astype(LOW)
    wait(order, side)
    side = send(side, TO_ZL)
    mixed_terms = share_pieces(mixed_grads(order, normed_one, d_mixed, out_grad))
    ff_kept, ff_sent = fold(order, [ff_terms])
    ff_sent = send(ff_sent, TO_ZH)
    (input_grad,) = norm_pull(order, x, (near, far, side), d_resid, False)
    wait(order, output)
    mixed_kept, mixed_sent = fold(order, [t[None] for t in mixed_terms], 128)
    mixed_sent = send(mixed_sent, TO_ZH)
    ff_slices = share_slices(split_rows(order, ff_kept, ff_sent))
    input_grad = jnp.concatenate(
        [send(input_grad[: tokens // 2], TO_HOME), send(input_grad[tokens // 2 :], TO_HOME)]
    )
    mixed_slices = share_slices(split_rows(order, mixed_kept, mixed_sent))
    up_grad, gain_two_grad, down_grad = finish(
        order, ff_slices, up_weight, gain_two, (2, ff, ff)
    )
    qkv_grad, gain_one_grad, out_grad = finish(
        order, mixed_slices, qkv_weight, gain_one, (3, part, part)
    )
    return (
        output[None],
        input_grad[None],
        gain_one_grad[0],
        qkv_grad,
        out_grad,
        gain_two_grad[0],
        up_grad,
        down_grad,
    )


def solution(mesh):
    dp, seq = "dp", "seq"
    step = per_device
    if tuple(mesh.shape.values()) == QUAD_MESH:
        dp, seq, step = ("y", "x", "c"), ("zh", "zl"), quad_device
        mesh = jax.sharding.Mesh(mesh.devices.reshape(2, 2, 2, 2, 2), FLAT)
        every = FLAT
    else:
        every = (dp, seq)
    rows = P(every, None)
    return jax.shard_map(
        step,
        mesh=mesh,
        in_specs=(
            P(dp, seq, None),
            P(dp, seq),
            P(every),
            rows,
            rows,
            P(every),
            rows,
            rows,
            P(dp, seq, None),
        ),
        out_specs=(
            P(dp, seq, None),
            P(dp, seq, None),
            P(every),
            rows,
            rows,
            P(every),
            rows,
            rows,
        ),
        check_vma=False,
    )
```

```python
import math

import jax
import jax.numpy as jnp
from jax import lax
from jax.experimental import pallas as pl
from jax.experimental.pallas import tpu as pltpu
from jax.sharding import PartitionSpec as P

HEADS = 16
HEAD_DIM = 64
FF = 2624


norm_eps = 1e-05
rope_base = 160000.0
inv_root_two = 0.7071067811865476
inv_root_tau = 0.3989422804014327


def for_sending(array):
    return jax.tree.map(lambda a: a.astype(jnp.bfloat16) if a.dtype == jnp.float32 else a, array)


def normalize(values):
    centre = jnp.mean(values, axis=-1, keepdims=True)
    centred = values - centre
    spread = lax.rsqrt(jnp.mean(centred * centred, axis=-1, keepdims=True) + norm_eps)
    return (centred * spread, spread)


def norm_back(grad_in, normed, spread, gain):
    scaled = grad_in * gain
    gain_term = jnp.sum(grad_in * normed, axis=0)
    centred = (
        scaled
        - jnp.mean(scaled, axis=-1, keepdims=True)
        - normed * jnp.mean(scaled * normed, axis=-1, keepdims=True)
    )
    return (spread * centred, gain_term)


def rope_tables(seq_pos):
    exponent = jnp.arange(0, HEAD_DIM, 2).astype(jnp.float32) / HEAD_DIM
    frequency = rope_base ** (-exponent)
    angles = seq_pos.astype(jnp.float32)[:, None] * frequency[None, :]
    angles = jnp.concatenate([angles, angles], axis=-1)[:, None, :]
    return (jnp.cos(angles), jnp.sin(angles))


def rotate(values, cos_table, sin_table):
    half_dim = values.shape[-1] // 2
    turned = jnp.concatenate([-values[..., half_dim:], values[..., :half_dim]], axis=-1)
    return values * cos_table + turned * sin_table


def rotate_back(grads, cos_table, sin_table):
    half_dim = grads.shape[-1] // 2
    weighted = grads * sin_table
    turned = jnp.concatenate([weighted[..., half_dim:], -weighted[..., :half_dim]], axis=-1)
    return grads * cos_table + turned


def gelu_parts(inner_act):
    normal_cdf = 0.5 * (1.0 + jax.scipy.special.erf(inner_act * inv_root_two))
    slope = normal_cdf + inner_act * jnp.exp(-0.5 * inner_act * inner_act) * inv_root_tau
    return (inner_act * normal_cdf, slope)


def project_heads(attn_in, w_qkv, cos_table, sin_table):
    token_count, model_width = attn_in.shape
    mixed_rows = jnp.dot(attn_in, w_qkv, preferred_element_type=jnp.float32)
    shaped = (token_count, HEADS, HEAD_DIM)
    queries = rotate(mixed_rows[:, :model_width].reshape(shaped), cos_table, sin_table)
    key_rows = rotate(
        mixed_rows[:, model_width : 2 * model_width].reshape(shaped), cos_table, sin_table
    )
    queries = queries.reshape(token_count, model_width).astype(jnp.bfloat16)
    key_rows = key_rows.reshape(token_count, model_width).astype(jnp.bfloat16)
    values = mixed_rows[:, 2 * model_width :].astype(jnp.bfloat16)
    return (queries, key_rows, values)


def attend_forward(q_heads, k_heads, v_heads):
    seq_len, columns = q_heads.shape
    head_count = columns // HEAD_DIM
    block_rows = min(512, seq_len)
    block_count = seq_len // block_rows
    score_scale = HEAD_DIM ** (-0.5)
    k_all = k_heads.reshape(seq_len, head_count, HEAD_DIM)
    v_all = v_heads.reshape(seq_len, head_count, HEAD_DIM)

    def one_block(q_block):
        scores = (
            jnp.einsum("qhd,khd->hqk", q_block, k_all, preferred_element_type=jnp.float32)
            * score_scale
        )
        row_peak = jnp.max(scores, axis=-1, keepdims=True)
        exp_scores = jnp.exp(scores - row_peak)
        totals = jnp.sum(exp_scores, axis=-1, keepdims=True)
        prob_rows = (exp_scores / totals).astype(jnp.bfloat16)
        attended = jnp.einsum("hqk,khd->qhd", prob_rows, v_all, preferred_element_type=jnp.float32)
        return (attended.astype(jnp.bfloat16), row_peak[..., 0] + jnp.log(totals[..., 0]))

    attended, log_totals = lax.map(
        one_block, q_heads.reshape(block_count, block_rows, head_count, HEAD_DIM)
    )
    return (attended.reshape(seq_len, columns), log_totals)


def attend_backward(q_heads, k_heads, v_heads, d_heads, log_totals):
    seq_len, columns = q_heads.shape
    head_count = columns // HEAD_DIM
    block_rows = min(512, seq_len)
    block_count = seq_len // block_rows
    score_scale = HEAD_DIM ** (-0.5)
    k_all = k_heads.reshape(seq_len, head_count, HEAD_DIM)
    v_all = v_heads.reshape(seq_len, head_count, HEAD_DIM)
    q_blocks = q_heads.reshape(block_count, block_rows, head_count, HEAD_DIM)
    d_blocks = d_heads.reshape(block_count, block_rows, head_count, HEAD_DIM)

    def one_block(carry, item):
        key_acc, value_acc = carry
        q_block, d_block, lse_block = item
        scores = (
            jnp.einsum("qhd,khd->hqk", q_block, k_all, preferred_element_type=jnp.float32)
            * score_scale
        )
        prob_rows = jnp.exp(scores - lse_block[..., None])
        value_acc = value_acc + jnp.einsum(
            "hqk,qhd->khd",
            prob_rows.astype(jnp.bfloat16),
            d_block,
            preferred_element_type=jnp.float32,
        )
        d_probs = jnp.einsum("qhd,khd->hqk", d_block, v_all, preferred_element_type=jnp.float32)
        d_scores = (
            prob_rows * (d_probs - jnp.sum(prob_rows * d_probs, axis=-1, keepdims=True))
        ).astype(jnp.bfloat16)
        d_query = (
            jnp.einsum("hqk,khd->qhd", d_scores, k_all, preferred_element_type=jnp.float32)
            * score_scale
        )
        key_acc = (
            key_acc
            + jnp.einsum("hqk,qhd->khd", d_scores, q_block, preferred_element_type=jnp.float32)
            * score_scale
        )
        return ((key_acc, value_acc), d_query.astype(jnp.bfloat16))

    empty_acc = jnp.zeros((seq_len, head_count, HEAD_DIM), jnp.float32)
    (key_acc, value_acc), d_query = lax.scan(
        one_block, (empty_acc, empty_acc), (q_blocks, d_blocks, log_totals)
    )
    d_q = d_query.reshape(seq_len, columns)
    d_k = key_acc.astype(jnp.bfloat16).reshape(seq_len, columns)
    d_v = value_acc.astype(jnp.bfloat16).reshape(seq_len, columns)
    return (d_q, d_k, d_v)


def add_sources(received):
    return tuple((jnp.sum(piece, axis=0) for piece in received))


def per_device(
    inputs,
    positions,
    attn_gain,
    qkv_weight,
    attn_out_weight,
    mlp_gain,
    up_weight,
    down_weight,
    cotangent,
):
    layer = (
        lax.all_gather(attn_gain, ("dp", "seq"), axis=0, tiled=True),
        lax.all_gather(qkv_weight, ("dp", "seq"), axis=0, tiled=True),
        lax.all_gather(attn_out_weight, ("dp", "seq"), axis=0, tiled=True),
        lax.all_gather(mlp_gain, ("dp", "seq"), axis=0, tiled=True),
        lax.all_gather(up_weight, ("dp", "seq"), axis=0, tiled=True),
        lax.all_gather(down_weight, ("dp", "seq"), axis=0, tiled=True),
    )
    gain_one, w_qkv, w_out, gain_two, w_up, w_down = layer
    token_count = inputs.shape[1]
    resid_in = inputs[0].astype(jnp.float32)
    cos_table, sin_table = rope_tables(positions[0])
    normed_one, spread_one = normalize(resid_in)
    attn_in = (normed_one * gain_one.astype(jnp.float32)).astype(jnp.bfloat16)
    queries, key_rows, values = project_heads(attn_in, w_qkv, cos_table, sin_table)
    q_heads, k_heads, v_heads = (
        lax.all_to_all(queries, "seq", split_axis=1, concat_axis=0, tiled=True),
        lax.all_to_all(key_rows, "seq", split_axis=1, concat_axis=0, tiled=True),
        lax.all_to_all(values, "seq", split_axis=1, concat_axis=0, tiled=True),
    )
    attended_heads, log_totals = attend_forward(q_heads, k_heads, v_heads)
    attended = lax.all_to_all(attended_heads, "seq", split_axis=0, concat_axis=1, tiled=True)
    resid = resid_in + jnp.dot(attended, w_out, preferred_element_type=jnp.float32)
    normed_two, spread_two = normalize(resid)
    mlp_in = (normed_two * gain_two.astype(jnp.float32)).astype(jnp.bfloat16)
    up_rows = jnp.dot(mlp_in, w_up, preferred_element_type=jnp.float32)
    inner_act = up_rows[:, :FF]
    gate_act = up_rows[:, FF:]
    gelu_val, gelu_slope = gelu_parts(inner_act)
    hidden = (gelu_val * gate_act).astype(jnp.bfloat16)
    output = resid + jnp.einsum("tf,df->td", hidden, w_down, preferred_element_type=jnp.float32)
    layer_back = (
        lax.all_gather(attn_gain, ("dp", "seq"), axis=0, tiled=True),
        lax.all_gather(qkv_weight, ("dp", "seq"), axis=0, tiled=True),
        lax.all_gather(attn_out_weight, ("dp", "seq"), axis=0, tiled=True),
        lax.all_gather(mlp_gain, ("dp", "seq"), axis=0, tiled=True),
        lax.all_gather(up_weight, ("dp", "seq"), axis=0, tiled=True),
        lax.all_gather(down_weight, ("dp", "seq"), axis=0, tiled=True),
    )
    gain_one, w_qkv, w_out, gain_two, w_up, w_down = layer_back
    d_out = cotangent[0]
    down_grad = jnp.einsum("td,tf->df", d_out, hidden, preferred_element_type=jnp.float32)
    d_hidden = jnp.dot(d_out, w_down, preferred_element_type=jnp.float32)
    d_up = jnp.concatenate([d_hidden * gate_act * gelu_slope, d_hidden * gelu_val], axis=1).astype(
        jnp.bfloat16
    )
    up_grad = jnp.einsum("tk,tn->kn", mlp_in, d_up, preferred_element_type=jnp.float32)
    d_mlp_in = jnp.einsum("tn,kn->tk", d_up, w_up, preferred_element_type=jnp.float32)
    d_norm_two, gain_two_grad = norm_back(
        d_mlp_in, normed_two, spread_two, gain_two.astype(jnp.float32)
    )
    d_resid = d_out.astype(jnp.float32) + d_norm_two
    d_resid_low = d_resid.astype(jnp.bfloat16)
    out_grad = jnp.einsum("tk,tn->kn", attended, d_resid_low, preferred_element_type=jnp.float32)
    d_attended = jnp.einsum(
        "tn,kn->tk", d_resid_low, w_out, preferred_element_type=jnp.float32
    ).astype(jnp.bfloat16)
    d_heads = lax.all_to_all(d_attended, "seq", split_axis=1, concat_axis=0, tiled=True)
    queries, key_rows, values = project_heads(attn_in, w_qkv, cos_table, sin_table)
    head_inputs = (
        lax.all_to_all(queries, "seq", split_axis=1, concat_axis=0, tiled=True),
        lax.all_to_all(key_rows, "seq", split_axis=1, concat_axis=0, tiled=True),
        lax.all_to_all(values, "seq", split_axis=1, concat_axis=0, tiled=True),
    )
    d_q, d_k, d_v = attend_backward(
        head_inputs[0], head_inputs[1], head_inputs[2], d_heads, log_totals
    )
    dq_rows, dk_rows, dv_rows = (
        lax.all_to_all(d_q, "seq", split_axis=0, concat_axis=1, tiled=True),
        lax.all_to_all(d_k, "seq", split_axis=0, concat_axis=1, tiled=True),
        lax.all_to_all(d_v, "seq", split_axis=0, concat_axis=1, tiled=True),
    )
    shaped = (token_count, HEADS, HEAD_DIM)
    dq_pre = rotate_back(dq_rows.astype(jnp.float32).reshape(shaped), cos_table, sin_table).reshape(
        token_count, -1
    )
    dk_pre = rotate_back(dk_rows.astype(jnp.float32).reshape(shaped), cos_table, sin_table).reshape(
        token_count, -1
    )
    d_mixed = jnp.concatenate(
        [dq_pre.astype(jnp.bfloat16), dk_pre.astype(jnp.bfloat16), dv_rows], axis=1
    )
    qkv_grad = jnp.einsum("tk,tn->kn", attn_in, d_mixed, preferred_element_type=jnp.float32)
    d_attn_in = jnp.einsum("tn,kn->tk", d_mixed, w_qkv, preferred_element_type=jnp.float32)
    d_norm_one, gain_one_grad = norm_back(
        d_attn_in, normed_one, spread_one, gain_one.astype(jnp.float32)
    )
    input_grad = (d_resid + d_norm_one).astype(jnp.bfloat16)
    all_sent = (
        lax.all_to_all(
            gain_one_grad[None].astype(jnp.bfloat16), "dp", split_axis=1, concat_axis=0, tiled=True
        ).astype(jnp.float32),
        lax.all_to_all(
            qkv_grad[None].astype(jnp.bfloat16), "dp", split_axis=1, concat_axis=0, tiled=True
        ).astype(jnp.float32),
        lax.all_to_all(
            out_grad[None].astype(jnp.bfloat16), "dp", split_axis=1, concat_axis=0, tiled=True
        ).astype(jnp.float32),
        lax.all_to_all(
            gain_two_grad[None].astype(jnp.bfloat16), "dp", split_axis=1, concat_axis=0, tiled=True
        ).astype(jnp.float32),
        lax.all_to_all(
            up_grad[None].astype(jnp.bfloat16), "dp", split_axis=1, concat_axis=0, tiled=True
        ).astype(jnp.float32),
        lax.all_to_all(
            down_grad[None].astype(jnp.bfloat16), "dp", split_axis=1, concat_axis=0, tiled=True
        ).astype(jnp.float32),
    )
    grads = jax.tree.map(
        lambda part: part.astype(jnp.float32),
        lax.psum_scatter(
            for_sending(add_sources(all_sent)), "seq", scatter_dimension=0, tiled=True
        ),
    )
    return (
        output.astype(jnp.bfloat16)[None],
        input_grad[None],
        grads[0],
        grads[1],
        grads[2],
        grads[3],
        grads[4],
        grads[5],
    )


QUAD_MESH = (8, 4)
FLAT = ("y", "x", "c", "zh", "zl")
LOW, WIDE = jnp.bfloat16, jnp.float32


def pairs_of(step):
    found = []
    for dp in range(8):
        for seq in range(4):
            place = (dp // 4, dp // 2 % 2, dp % 2, seq // 2, seq % 2)
            target = step(*place)
            if target is not None:
                y, x, c, zh, zl = target
                found.append((dp * 4 + seq, (4 * y + 2 * x + c) * 4 + 2 * zh + zl))
    return found


TO_X = pairs_of(lambda y, x, c, zh, zl: (y, 1 - x, c, zh, zl))
TO_Y = pairs_of(lambda y, x, c, zh, zl: (1 - y, x, c, zh, zl))
TO_XY = pairs_of(lambda y, x, c, zh, zl: (1 - y, 1 - x, c, zh, zl))
TO_CORE = pairs_of(lambda y, x, c, zh, zl: (y, x, 1 - c, zh, zl))
TO_ZH = pairs_of(lambda y, x, c, zh, zl: (y, x, c, 1 - zh, zl))
TO_ZL = pairs_of(lambda y, x, c, zh, zl: (y, x, c, zh, 1 - zl))
TO_FAR = pairs_of(lambda y, x, c, zh, zl: (y, x, 1 - c, zh, 1 - zl))
TO_HOME = pairs_of(lambda y, x, c, zh, zl: (y, x, zh, c, zl))
ENTER = pairs_of(
    lambda y, x, c, zh, zl: (y, x, c, zh, 1 - zl) if c == zh else (y, x, zh, c, zl)
)
ENTER_MOVED = pairs_of(lambda y, x, c, zh, zl: None if c == zh else (y, x, c, zh, 1 - zl))


class Order(list):
    pass


def send(array, pairs):
    return lax.ppermute(array, FLAT, pairs)


def after(order, array):
    return lax.optimization_barrier((array, order[0]))[0]


def wait(order, *arrays):
    order[0] = lax.optimization_barrier((order[0], *arrays))[0]


def lanes(size):
    return -(-size // 128) * 128


def core_of(flat):
    return flat >> 2 & 1


def half_of(flat):
    return flat >> 1 & 1


def group_of(flat):
    return 2 * core_of(flat) + (flat & 1)


def square_of(flat):
    return flat >> 3


def mm(left, right):
    return lax.dot_general(left, right, (((1,), (0,)), ((), ())), preferred_element_type=WIDE)


def mm_t(left, right):
    return lax.dot_general(left, right, (((1,), (1,)), ((), ())), preferred_element_type=WIDE)


def t_mm(left, right):
    return lax.dot_general(left, right, (((0,), (0,)), ((), ())), preferred_element_type=WIDE)


def window(index, size):
    return pl.ds(pl.multiple_of(index * size, size), size)


def whole(array):
    rank = len(array.shape)
    return (array, array.shape, lambda *_: (0,) * rank)


def by_rows(array, rows, step=lambda b: b):
    return (array, (rows,) + array.shape[1:], lambda b, f: (step(b),) + (0,) * (len(array.shape) - 1))


def run(body, order, grid, ins, outs, scratch=(), flops=0, spare=6 * 2**20):
    moved = sum(a.size * a.dtype.itemsize for a, _, _ in ins)
    moved += sum(a.size * a.dtype.itemsize for a, _, _ in outs)
    def held(block, dtype, count):
        return count * math.prod(block) * jnp.dtype(dtype).itemsize

    grant = sum(
        held(block, a.dtype, 1 if tuple(block) == tuple(a.shape) else 2)
        for a, block, _ in (*ins, *outs)
    )
    grant += sum(held(m.shape, m.dtype, 1) for m in scratch) + spare
    made = pl.pallas_call(
        body,
        grid_spec=pltpu.PrefetchScalarGridSpec(
            num_scalar_prefetch=1,
            grid=grid,
            in_specs=[pl.BlockSpec(block, index) for _, block, index in ins],
            out_specs=[pl.BlockSpec(block, index) for _, block, index in outs],
            scratch_shapes=list(scratch),
        ),
        out_shape=[a for a, _, _ in outs],
        compiler_params=pltpu.CompilerParams(vmem_limit_bytes=grant),
        cost_estimate=pl.CostEstimate(flops=flops // 100, bytes_accessed=moved // 100, transcendentals=0),
    )(order[0], *[a for a, _, _ in ins])
    order[0], _ = lax.optimization_barrier((order[0], made[0]))
    return made


def spans(pieces):
    rows = pieces[0].shape[0]
    return [(0, 0, rows), (1, 0, rows), (2, 0, rows), (3, 0, rows // 2), (3, rows // 2, rows // 2)]


def rows_of(ref, span):
    count = span[2]
    return slice(ref.shape[0] - count, None) if span[1] else slice(0, count)


def span_of(square, span, rows):
    index, first, count = span
    return pl.ds(pl.multiple_of((square ^ index) * rows + first, count), count)


def shape_of(*dims, dtype=LOW):
    return jax.ShapeDtypeStruct(dims, dtype)


def column_of(row):
    size = row.shape[1]
    down = lax.broadcasted_iota(jnp.int32, (size, size), 0)
    across = lax.broadcasted_iota(jnp.int32, (size, size), 1)
    return jnp.sum(jnp.where(down == across, row, 0.0), axis=1, keepdims=True)


def row_of(column):
    size = column.shape[0]
    down = lax.broadcasted_iota(jnp.int32, (size, size), 0)
    across = lax.broadcasted_iota(jnp.int32, (size, size), 1)
    return jnp.sum(jnp.where(down == across, column, 0.0), axis=0, keepdims=True)


def normed_of(x):
    centred = x - jnp.mean(x, axis=-1, keepdims=True)
    spread = lax.rsqrt(jnp.mean(centred * centred, axis=-1, keepdims=True) + norm_eps)
    return centred * spread, spread


def split_slices(order, scaled, plain, gain, parts):
    rows, part, rest = scaled.shape[0], scaled.shape[1] // (4 * parts), plain.shape[1] // 4
    out = shape_of(2, rows, lanes(parts * part + rest))

    def body(flat_ref, scaled_ref, plain_ref, gain_ref, own_ref, sent_ref, held):
        scale = column_of(gain_ref[...].astype(WIDE))
        for s in range(4):
            for t in range(parts):
                cols = scaled_ref[:, (4 * t + s) * part : (4 * t + s + 1) * part].astype(WIDE)
                held[s, :, t * part : (t + 1) * part] = (cols * scale).astype(LOW)
            held[s, :, parts * part : parts * part + rest] = plain_ref[
                :, s * rest : (s + 1) * rest
            ]
        core = core_of(flat_ref[0])
        for zl in range(2):
            own_ref[zl] = held[2 * core + zl]
            sent_ref[zl] = held[2 * (1 - core) + zl]

    return run(
        body, order, (1,), [whole(a) for a in (scaled, plain, gain)], [whole(out)] * 2,
        [pltpu.VMEM((4, *out.shape[1:]), LOW)],
    )


def chip_rows(order, own, received):
    def body(flat_ref, own_ref, received_ref, kept_ref, sent_ref):
        core, chip = core_of(flat_ref[0]), flat_ref[0] & 1
        kept_ref[core] = own_ref[chip]
        kept_ref[1 - core] = received_ref[chip]
        sent_ref[core] = own_ref[1 - chip]
        sent_ref[1 - core] = received_ref[1 - chip]

    return run(
        body, order, (1,), [whole(own), whole(received)], [whole(shape_of(*own.shape))] * 2
    )


def quad_rows(order, own, received):
    _, rows, width = own.shape

    def body(flat_ref, own_ref, received_ref, out_ref):
        chip = flat_ref[0] & 1
        for c in range(2):
            out_ref[2 * c + chip] = own_ref[c]
            out_ref[2 * c + 1 - chip] = received_ref[c]

    return run(
        body, order, (1,), [whole(own), whole(received)], [whole(shape_of(4, rows, width))]
    )[0]


def line_rows(order, near, far):
    _, rows, width = near.shape
    near = near.reshape(2, 2 * rows, width)
    far = far.reshape(2, 2 * rows, width)

    def body(flat_ref, near_ref, far_ref, out_ref):
        half = half_of(flat_ref[0])
        for c in range(2):
            out_ref[c, half] = near_ref[c]
            out_ref[c, 1 - half] = far_ref[c]

    out = run(
        body, order, (1,), [whole(near), whole(far)], [whole(shape_of(2, 2, 2 * rows, width))]
    )[0]
    return out.reshape(8 * rows, width)


def join_tokens(order, parts, rows, extra=0):
    width = parts[0].shape[1]

    def body(flat_ref, block, first, second, core_block, core_first, core_second, *outs):
        home = core_of(flat_ref[0]) == half_of(flat_ref[0])
        here = (block, first, core_first, core_second)
        moved = (first, second, core_block, core_first)
        for k in range(4):
            for flag, source in ((home, here[k]), (jnp.logical_not(home), moved[k])):

                @pl.when(jnp.logical_and(pl.program_id(0) == k, flag))
                def _(source=source):
                    def step(r, carry):
                        outs[0][window(r, 32), :] = source[window(r, 32), :]
                        return carry

                    lax.fori_loop(0, rows // 32, step, 0)
                    if extra:
                        outs[1][...] = source[rows : rows + extra, :]

    made = [shape_of(4 * rows, width)] + ([shape_of(4 * extra, width)] if extra else [])
    return run(
        body, order, (4,), [whole(a) for a in parts],
        [by_rows(m, m.shape[0] // 4) for m in made],
    )


def rope_lanes(seq_pos):
    exponent = jnp.arange(0, HEAD_DIM, 2).astype(WIDE) / HEAD_DIM
    angles = seq_pos[:, None] * (rope_base ** (-exponent))[None, :]
    cos_half, sin_half = jnp.cos(angles), jnp.sin(angles)
    return (
        jnp.concatenate([cos_half] * 4, axis=1),
        jnp.concatenate([-sin_half, sin_half] * 2, axis=1),
    )


def turned(v):
    half = HEAD_DIM // 2
    lane = lax.broadcasted_iota(jnp.int32, v.shape, 1)
    return jnp.where(
        lane % HEAD_DIM < half, pltpu.roll(v, 2 * HEAD_DIM - half, 1), pltpu.roll(v, half, 1)
    )


def project(order, x, pieces, cos_table, sin_table):
    tokens, width = x.shape
    piece, columns = pieces[0].shape[0], 3 * width // 4
    rows = tokens // 4

    def body(flat_ref, x_ref, *refs):
        weights, (cos_ref, sin_ref, n_ref, mix_ref) = refs[:5], refs[5:]
        n_ref[...] = normed_of(x_ref[...].astype(WIDE))[0].astype(LOW)
        square = square_of(flat_ref[0])
        mixed = sum(
            mm(n_ref[:, span_of(square, span, piece)], w[rows_of(w, span), :columns])
            for span, w in zip(spans(pieces), weights)
        )
        turned_to = 2 * columns // 3
        for t in range(0, turned_to, 128):
            v = mixed[:, t : t + 128]
            mix_ref[:, t : t + 128] = (v * cos_ref[...] + turned(v) * sin_ref[...]).astype(LOW)
        mix_ref[:, turned_to:] = mixed[:, turned_to:].astype(LOW)

    return run(
        body, order, (4,),
        [by_rows(x, rows)] + [whole(p) for p in pieces]
        + [by_rows(cos_table, rows), by_rows(sin_table, rows)],
        [by_rows(shape_of(tokens, width), rows), by_rows(shape_of(tokens, columns), rows)],
        flops=2 * tokens * width * columns,
    )


def attend(order, mix):
    tokens, columns = mix.shape
    part = columns // 3
    rows = tokens // 4
    scale = HEAD_DIM ** (-0.5)

    def body(flat_ref, q_ref, k_ref, v_ref, out_ref, log_ref):
        lane = lax.broadcasted_iota(jnp.int32, (rows, part), 1) // HEAD_DIM
        total = jnp.zeros((rows, part), WIDE)
        queries = q_ref[...].astype(WIDE) * scale
        for h in range(part // HEAD_DIM):
            q_head = jnp.where(lane == h, queries, 0.0).astype(LOW)
            scores = mm_t(q_head, k_ref[...])
            peak = jnp.max(scores, axis=-1, keepdims=True)
            powers = jnp.exp(scores - peak)
            mass = jnp.sum(powers, axis=-1, keepdims=True)
            probs = (powers * (1.0 / mass)).astype(LOW)
            total = jnp.where(lane == h, mm(probs, v_ref[...]), total)
            log_ref[h : h + 1, :] = row_of(peak + jnp.log(mass))
        out_ref[...] = total.astype(LOW)

    return run(
        body, order, (4,),
        [
            (mix, (rows, part), lambda b, f: (b, 0)),
            (mix, (tokens, part), lambda b, f: (0, 1)),
            (mix, (tokens, part), lambda b, f: (0, 2)),
        ],
        [
            by_rows(shape_of(tokens, part), rows),
            (shape_of(8, tokens, dtype=WIDE), (8, rows), lambda b, f: (0, b)),
        ],
        flops=16 * tokens * tokens * part,
    )


def token_parts(arrays, rows):
    return [by_rows(a, rows, lambda b, i=i: b ^ i) for i, a in enumerate(arrays)]


def join_heads(order, x, heads, columns):
    tokens, width = x.shape
    rows, part = tokens // 4, width // 4

    def body(flat_ref, x_ref, *refs):
        parts, weights, (n_ref, own_ref, held) = refs[:4], refs[4:8], refs[8:]
        group, square = group_of(flat_ref[0]), square_of(flat_ref[0])
        for j in range(4):
            cols = window(group ^ j, part)
            held[:, cols] = x_ref[:, cols].astype(WIDE) + sum(
                mm(parts[i][...], weights[j][window(group ^ i ^ square, part), :])
                for i in range(4)
            )
        resid = held[...]
        n_ref[...] = normed_of(resid)[0].astype(LOW)

        @pl.when(pl.program_id(0) == 0)
        def _():
            own_ref[...] = held[...]

    return run(
        body, order, (4,),
        [by_rows(x, rows)] + token_parts(heads, rows) + [whole(w) for w in columns],
        [by_rows(shape_of(tokens, width), rows), whole(shape_of(rows, width, dtype=WIDE))],
        [pltpu.VMEM((rows, width), WIDE)],
        flops=2 * tokens * width * width,
    )


def feed(order, normed, cot, pieces):
    tokens, width = normed.shape
    piece, ff = pieces[0].shape[0], FF // 4
    rows = tokens // 4

    def body(flat_ref, n_ref, cot_ref, *refs):
        weights, (h_ref, d_ref) = refs[:5], refs[5:]
        square = square_of(flat_ref[0])
        cut = [
            (span_of(square, span, piece), rows_of(w, span), w)
            for span, w in zip(spans(pieces), weights)
        ]
        wide = sum(mm(n_ref[:, at], w[of, : 2 * ff]) for at, of, w in cut)
        d_hidden = sum(mm(cot_ref[:, at], w[of, 2 * ff : 3 * ff]) for at, of, w in cut)
        inner, gate = wide[:, :ff], wide[:, ff:]
        cdf = 0.5 * (1.0 + lax.erf(inner * inv_root_two))
        slope = cdf + inner * jnp.exp(-0.5 * inner * inner) * inv_root_tau
        bent = inner * cdf
        h_ref[...] = (bent * gate).astype(LOW)
        d_ref[:, :ff] = (d_hidden * gate * slope).astype(LOW)
        d_ref[:, ff:] = (d_hidden * bent).astype(LOW)

    return run(
        body, order, (4,),
        [by_rows(normed, rows), by_rows(cot, rows)] + [whole(w) for w in pieces],
        [by_rows(shape_of(tokens, ff), rows), by_rows(shape_of(tokens, 2 * ff), rows)],
        flops=6 * tokens * width * ff,
    )


def back_half(order, grads, pieces, far):
    tokens = grads[0][0].shape[0]
    piece = pieces[0].shape[0]
    rows, width, count = tokens // 2, 4 * piece, len(grads)
    out = shape_of(rows, width, dtype=LOW if far else WIDE)

    def body(flat_ref, *refs):
        arrays, weights, out_ref = refs[:count], refs[count : count + 5], refs[count + 5]
        square = square_of(flat_ref[0])
        for span, w in zip(spans(pieces), weights):
            out_ref[:, span_of(square, span, piece)] = sum(
                mm_t(a[...], w[rows_of(w, span), at : at + a.shape[1]])
                for a, (_, at) in zip(arrays, grads)
            ).astype(out.dtype)

    return run(
        body, order, (1,),
        [by_rows(a, rows, lambda b: int(far)) for a, _ in grads] + [whole(p) for p in pieces],
        [whole(out)],
        flops=tokens * width * sum(a.shape[1] for a, _ in grads),
    )[0]


def back_both(order, grad, first, pieces):
    tokens = grad.shape[0]
    piece = pieces[0].shape[0]
    rows, width, columns = tokens // 2, 4 * piece, grad.shape[1]

    def body(flat_ref, grad_ref, *refs):
        weights, (far_ref, near_ref) = refs[:5], refs[5:]
        square = square_of(flat_ref[0])
        for span, w in zip(spans(pieces), weights):
            total = mm_t(grad_ref[...], w[rows_of(w, span), first : first + columns])
            near_ref[:, span_of(square, span, piece)] = total[:rows]
            far_ref[:, span_of(square, span, piece)] = total[rows:].astype(LOW)

    return run(
        body, order, (1,), [whole(grad)] + [whole(p) for p in pieces],
        [whole(shape_of(rows, width)), whole(shape_of(rows, width, dtype=WIDE))],
        flops=2 * tokens * width * columns,
    )


def norm_pull(order, x, terms, base, keep):
    rows, width = base.shape[0] // (4 if keep else 1), base.shape[1]
    step = rows // 4

    def body(flat_ref, x_ref, a_ref, b_ref, c_ref, base_ref, *outs):
        normed, spread = normed_of(x_ref[...].astype(WIDE))
        scaled = a_ref[...] + b_ref[...].astype(WIDE) + c_ref[...].astype(WIDE)
        grad = base_ref[...].astype(WIDE) + spread * (
            scaled
            - jnp.mean(scaled, axis=-1, keepdims=True)
            - normed * jnp.mean(scaled * normed, axis=-1, keepdims=True)
        )
        outs[0][...] = grad.astype(LOW)
        if keep:
            outs[1][...] = grad

    low = shape_of(rows + 16 if keep else rows, width)
    outs = [low] + ([shape_of(rows, width, dtype=WIDE)] if keep else [])
    return run(
        body, order, (4,), [by_rows(a, step) for a in (x, *terms, base)],
        [by_rows(o, step) for o in outs],
    )


def feed_grads(order, normed, cot, d_up, hidden):
    tokens, width = normed.shape
    piece, ff = width // 4, hidden.shape[1]
    out = shape_of(4, piece, lanes(3 * ff))

    def body(flat_ref, n_ref, cot_ref, d_ref, h_ref, out_ref):
        out_ref[0, :, : 2 * ff] = t_mm(n_ref[...], d_ref[...]).astype(LOW)
        out_ref[0, :, 2 * ff : 3 * ff] = t_mm(cot_ref[...], h_ref[...]).astype(LOW)

    return run(
        body, order, (4,),
        [(a, (tokens, piece), lambda b, f: (0, b)) for a in (normed, cot)]
        + [whole(d_up), whole(hidden)],
        [by_rows(out, 1)],
        flops=6 * tokens * width * ff,
    )[0]


def heads_back(order, d_all, heads, columns):
    rows, width = heads[0].shape[0] // 4, d_all[0].shape[1]
    part = width // 4

    def body(flat_ref, *refs):
        blocks, parts, weights = refs[:4], refs[4:8], refs[8:12]
        d_ref, grad_ref, block, held, total = refs[12:]
        group, square = group_of(flat_ref[0]), square_of(flat_ref[0])
        at = pl.program_id(0)
        for k in range(4):

            @pl.when(at == k)
            def _(source=blocks[k]):
                def step(r, carry):
                    block[window(r, 32), :] = source[window(r, 32), :]
                    return carry

                lax.fori_loop(0, rows // 32, step, 0)

            held[k] = parts[k][...]

        @pl.when(at == 0)
        def _():
            total[...] = jnp.zeros_like(total)

        d_ref[...] = sum(
            mm_t(block[:, window(group ^ j, part)], weights[j][window(group ^ square, part), :])
            for j in range(4)
        ).astype(LOW)
        mine = block[:, window(group, part)]
        for i in range(4):
            total[i] += t_mm(held[group ^ square ^ i], mine)

        @pl.when(at == 3)
        def _():
            grad_ref[...] = total[...].astype(LOW)

    return run(
        body, order, (4,),
        [whole(d) for d in d_all] + token_parts(heads, rows) + [whole(w) for w in columns],
        [by_rows(shape_of(4 * rows, part), rows), whole(shape_of(4, part, part))],
        [
            pltpu.VMEM((rows, width), LOW),
            pltpu.VMEM((4, rows, part), LOW),
            pltpu.VMEM((4, part, part), WIDE),
        ],
        flops=4 * 4 * rows * width * part,
    )


def attend_back(order, mix, attended, d_attended, logs, cos_table, sin_table):
    tokens, columns = mix.shape
    part = columns // 3
    rows = tokens // 4
    scale = HEAD_DIM ** (-0.5)
    heads = part // HEAD_DIM

    def rotated(grad, cos, sin):
        halves = [grad[:, t : t + 128] for t in range(0, part, 128)]
        return jnp.concatenate([v * cos - turned(v) * sin for v in halves], axis=1).astype(LOW)

    def body(flat_ref, q_ref, k_ref, v_ref, o_ref, d_ref, log_ref, cos_ref, sin_ref, *refs):
        dq_ref, dk_ref, dv_ref, k_total, v_total = refs
        at = pl.program_id(0)

        @pl.when(at == 0)
        def _():
            k_total[...] = jnp.zeros_like(k_total)
            v_total[...] = jnp.zeros_like(v_total)

        lane = lax.broadcasted_iota(jnp.int32, (rows, part), 1) // HEAD_DIM
        queries = q_ref[...].astype(WIDE) * scale
        grads = d_ref[...].astype(WIDE)
        chosen = lax.broadcasted_iota(jnp.int32, (8, part), 0) == (
            lax.broadcasted_iota(jnp.int32, (8, part), 1) // HEAD_DIM
        )
        deltas = lax.dot_general(
            chosen.astype(WIDE), grads * o_ref[...].astype(WIDE), (((1,), (1,)), ((), ())),
            precision=lax.Precision.HIGHEST, preferred_element_type=WIDE,
        )
        d_query = jnp.zeros((rows, part), WIDE)
        for h in range(heads):
            q_head = jnp.where(lane == h, queries, 0.0).astype(LOW)
            d_head = jnp.where(lane == h, grads, 0.0).astype(LOW)
            probs = jnp.exp(mm_t(k_ref[...], q_head) - log_ref[h : h + 1, :])
            d_probs = mm_t(v_ref[...], d_head)
            d_scores = (probs * (d_probs - deltas[h : h + 1, :])).astype(LOW)
            v_total[...] += mm(probs.astype(LOW), d_head)
            k_total[...] += mm(d_scores, q_head)
            d_query = jnp.where(lane == h, t_mm(d_scores, k_ref[...]), d_query)
        here = window(at, rows)
        dq_ref[...] = rotated(d_query * scale, cos_ref[here, :], sin_ref[here, :])

        @pl.when(at == 3)
        def _():
            dk_ref[...] = rotated(k_total[...], cos_ref[...], sin_ref[...])
            dv_ref[...] = v_total[...].astype(LOW)

    out = shape_of(tokens, part)
    return run(
        body, order, (4,),
        [
            (mix, (rows, part), lambda b, f: (b, 0)),
            (mix, (tokens, part), lambda b, f: (0, 1)),
            (mix, (tokens, part), lambda b, f: (0, 2)),
            by_rows(attended, rows),
            by_rows(d_attended, rows),
            (logs, (8, rows), lambda b, f: (0, b)),
            whole(cos_table),
            whole(sin_table),
        ],
        [by_rows(out, rows), whole(out), whole(out)],
        [pltpu.VMEM((tokens, part), WIDE)] * 2,
        flops=40 * tokens * tokens * part,
    )


def mixed_grads(order, normed, d_mixed, out_grad):
    tokens, width = normed.shape
    rows, piece = tokens // 4, width // 4
    part = d_mixed[0].shape[1]

    def body(flat_ref, n_ref, *refs):
        grads, out_ref, outs, held = refs[:3], refs[3], refs[4:8], refs[8]
        square = square_of(flat_ref[0])

        @pl.when(pl.program_id(0) == 0)
        def _():
            held[...] = jnp.zeros_like(held)

        for i in range(4):
            cols = n_ref[:, window(square ^ i, piece)]
            for t in range(3):
                held[i, :, t * part : (t + 1) * part] += t_mm(cols, grads[t][...])

        @pl.when(pl.program_id(0) == 3)
        def _():
            for i in range(4):
                outs[i][:, : 3 * part] = held[i].astype(LOW)
                outs[i][:, 3 * part :] = out_ref[i]

    return run(
        body, order, (4,),
        [by_rows(normed, rows)] + [by_rows(d, rows) for d in d_mixed] + [whole(out_grad)],
        [whole(shape_of(piece, 4 * part))] * 4, [pltpu.VMEM((4, piece, 3 * part), WIDE)],
        flops=6 * tokens * width * part,
    )


def fold(order, terms, margin=0):
    high, width = terms[0].shape[1:]
    rows = high // 4
    terms = [t.reshape(-1, 2, 2, rows, width) for t in terms]

    def body(flat_ref, *refs):
        ins, (kept_ref, sent_ref) = refs[:-2], refs[-2:]
        half = half_of(flat_ref[0])

        def total(at):
            return sum(r[k, 0, at].astype(WIDE) for r in ins for k in range(r.shape[0]))

        kept_ref[0] = total(half)
        sent_ref[0, :, :width] = total(1 - half).astype(LOW)

    return run(
        body, order, (2,),
        [
            (t, (t.shape[0], 1) + t.shape[2:], lambda b, f: (0, b, 0, 0, 0))
            for t in terms
        ],
        [
            by_rows(shape_of(2, rows, width, dtype=WIDE), 1),
            by_rows(shape_of(2, rows, width + margin), 1),
        ],
    )


def split_rows(order, kept, received):
    _, high, width = kept.shape
    rows = high // 2
    kept, received = kept.reshape(4, rows, width), received.reshape(4, rows, -1)

    def body(flat_ref, kept_ref, received_ref, *outs):
        for i in range(4):
            at = group_of(flat_ref[0]) ^ i
            outs[i][...] = (
                kept_ref[at] + received_ref[at, :, :width].astype(WIDE)
            ).astype(LOW)

    return run(
        body, order, (1,), [whole(kept), whole(received)], [whole(shape_of(rows, width))] * 4
    )


def finish(order, slices, weight, gain, sizes):
    rows, width = slices[0].shape
    count, part, rest = sizes

    def body(flat_ref, *refs):
        w_ref, gain_ref, scaled_ref, gain_out, plain_ref, held = refs[4:]
        for i in range(4):
            held[group_of(flat_ref[0]) ^ i] = refs[i][...].astype(WIDE)
        total = jnp.zeros((rows, 1), WIDE)
        scale = column_of(gain_ref[...].astype(WIDE))
        for s in range(4):
            for t in range(count):
                at = (4 * t + s) * part
                grad = held[s, :, t * part : (t + 1) * part]
                total += jnp.sum(
                    grad * w_ref[:, at : at + part].astype(WIDE), axis=1, keepdims=True
                )
                scaled_ref[:, at : at + part] = grad * scale
            plain_ref[:, s * rest : (s + 1) * rest] = held[s, :, count * part : count * part + rest]
        gain_out[...] = row_of(total)

    return run(
        body, order, (1,), [whole(a) for a in (*slices, weight, gain)],
        [
            whole(shape_of(*weight.shape, dtype=WIDE)),
            whole(shape_of(1, rows, dtype=WIDE)),
            whole(shape_of(rows, 4 * rest, dtype=WIDE)),
        ],
        [pltpu.VMEM((4, rows, width), WIDE)],
    )


TIED = {
    "ac",
    "af",
    "cf",
    "cmov",
    "cs",
    "df",
    "dz",
    "fz",
    "ih2",
    "l1",
    "m1z",
    "mov",
    "out",
    "pull_late",
    "sl1c",
    "t2",
    "tables",
    "wf",
    "x2",
}
WAITS = {
    "blk": 1,
    "ent": 1,
    "cblk": 3,
    "cf": 4,
    "mov": 4,
    "wc": 8,
    "wz": 8,
    "y2": 9,
    "wf": 10,
    "x2": 10,
    "cmov": 11,
    "dz": 14,
    "ofb": 15,
    "ofa": 17,
    "oz": 17,
    "m1c": 19,
    "oh": 21,
    "fz": 22,
    "f1": 24,
    "f2": 25,
}


def quad_device(
    inputs,
    positions,
    attn_gain,
    qkv_weight,
    attn_out_weight,
    mlp_gain,
    up_weight,
    down_weight,
    cotangent,
):
    order = Order([lax.axis_index(FLAT).astype(jnp.int32).reshape(1)])
    tokens, width = inputs.shape[1:]
    part, ff = width // 4, FF // 4
    gain_one, gain_two = attn_gain[None], mlp_gain[None]

    def at(point):
        wait(order, *[sent_as[n] for n, p in WAITS.items() if p == point])

    sent_as = {}

    def go(name, array, pairs):
        sent_as[name] = send(after(order, array) if name in TIED else array, pairs)
        return sent_as[name]

    pos = positions[0]
    pos_row = jnp.concatenate([pos // 128, pos % 128]).astype(LOW)
    pos_row = jnp.pad(pos_row[None], ((0, 15), (0, width - 2 * tokens)))
    block = jnp.concatenate([inputs[0], pos_row])
    first = go("ent", block, ENTER)
    wait(order, block)
    own, sent = split_slices(order, qkv_weight, attn_out_weight, gain_one, 3)
    received = go("sl1c", sent, TO_CORE)
    own_two, sent = split_slices(order, up_weight, down_weight, gain_two, 2)
    received_two = go("sl2c", sent, TO_CORE)
    core_block = go("blk", block, TO_CORE)
    cot_own = jnp.concatenate([cotangent[0], pos_row])
    cot_block = go("cblk", cot_own, TO_CORE)
    own, sent = chip_rows(order, own, received)
    received = go("sl1z", sent, TO_ZL)
    own_two, sent = chip_rows(order, own_two, received_two)
    at(1)
    one = quad_rows(order, own, received)
    at(2)
    one_far = go("zh1", one, TO_ZH)
    received_two = go("sl2z", sent, TO_ZL)
    second = go("mov", first, ENTER_MOVED)
    core_first = go("cf", first, TO_CORE)
    two = quad_rows(order, own_two, received_two)
    at(3)
    two_far = go("zh2", two, TO_ZH)
    one = line_rows(order, one, one_far)
    half = one.shape[0] // 2
    one_x, one_y = go("x1", one, TO_X), go("y1", one, TO_Y)
    at(4)
    core_second = go("cs", second, TO_CORE)
    cot_first = go("cent", cot_own, ENTER)
    one_top = go("t1", one_x[:half], TO_Y)
    one_low = go("l1", one_y[half:], TO_X)
    at(5)
    x, pos_all = join_tokens(
        order, [block, first, second, core_block, core_first, core_second], tokens, 16
    )
    pos_all = pos_all.reshape(4, 16, width)[:, 0, : 2 * tokens].astype(WIDE)
    pos_all = (pos_all[:, :tokens] * 128.0 + pos_all[:, tokens:]).reshape(4 * tokens)
    cos_table, sin_table = rope_lanes(pos_all)
    one = [one, one_x, one_y, one_top, one_low]
    if "tables" in TIED:
        wait(order, cos_table, sin_table)
    at(6)

    w_out = jnp.concatenate([p[:, 3 * part :] for p in one])
    w_side = go("wz", w_out, TO_ZL)
    w_core = go("wc", w_out, TO_CORE)
    normed_one, mix = project(order, x, one, cos_table, sin_table)
    at(7)
    cot_second = go("cmov", cot_first, ENTER_MOVED) if "cot_early" in TIED else None
    two = line_rows(order, two, two_far)
    two_x, two_y = go("x2", two, TO_X), go("y2", two, TO_Y)
    at(8)
    w_far = go("wf", w_side, TO_CORE)
    attended, logs = attend(order, mix)
    att_side = go("az", attended, TO_ZL)
    at(9)
    two_top = go("t2", two_x[: half + 16], TO_Y)
    two_low = go("l2", two_y[half - 16 :], TO_X)
    att_core = go("ac", attended, TO_CORE)
    at(10)
    if cot_second is None:
        cot_second = go("cmov", cot_first, ENTER_MOVED)
    w_out = [w_out, w_side, w_core, w_far]
    heads = [attended, att_side, att_core, go("af", att_side, TO_CORE)]
    at(11)
    normed_two, resid = join_heads(order, x, heads, w_out)

    core_first = go("ccf", cot_first, TO_CORE)
    core_second = go("ccs", cot_second, TO_CORE)
    at(12)
    (cot,) = join_tokens(
        order,
        [cot_own, cot_first, cot_second, cot_block, core_first, core_second],
        tokens,
    )
    two = [two, two_x, two_y, two_top, two_low]
    hidden, d_up = feed(order, normed_two, cot, two)

    grads = [(d_up, 0)]
    far = go("b1c", back_half(order, grads, two, True), TO_CORE)
    near = back_half(order, grads, two, False)
    side = (near[tokens:] + far[tokens:].astype(WIDE)).astype(LOW)
    side = go("b1z", jnp.pad(side, ((0, 16), (0, 0))), TO_ZL)
    ff_terms = feed_grads(order, normed_two, cot, d_up, hidden)
    at(13)
    if "a2a" not in TIED:
        ff_terms = lax.all_to_all(ff_terms, ("y", "x"), split_axis=0, concat_axis=0, tiled=True)
    d_low, d_resid = norm_pull(order, resid, (near, far, side), cot, True)
    if "a2a" in TIED:
        ff_terms = lax.all_to_all(
            after(order, ff_terms), ("y", "x"), split_axis=0, concat_axis=0, tiled=True
        )
    d_side = go("dz", d_low, TO_ZL)
    d_core = go("dc", d_low, TO_CORE)
    out_far, out_near = back_both(order, hidden, 2 * ff, two)
    at(14)
    out_far = [go("ofa", out_far[:tokens], TO_CORE), go("ofb", out_far[tokens:], TO_CORE)]
    out_side = (out_near[tokens:] + out_far[1].astype(WIDE)).astype(LOW)
    out_side = go("oz", out_side, TO_ZL)
    d_all = [d_low, d_side, d_core, go("df", d_side, TO_CORE)]
    at(15)
    d_attended, out_grad = heads_back(order, d_all, heads, w_out)
    at(16)
    d_mixed = attend_back(order, mix, attended, d_attended, logs, cos_table, sin_table)
    at(17)
    grads = [(d, t * part) for t, d in enumerate(d_mixed)]
    far = go("m1c", back_half(order, grads, one, True), TO_CORE)
    at(18)
    output = resid + out_near[:tokens] + out_far[0].astype(WIDE) + out_side.astype(WIDE)
    output = output.astype(LOW)
    if "out" in TIED:
        wait(order, output)
    output = go("oh", output, TO_HOME)
    near = back_half(order, grads, one, False)
    side = (near[tokens:] + far[tokens:].astype(WIDE)).astype(LOW)
    if "side" in TIED:
        wait(order, side)
    side = go("m1z", side, TO_ZL)
    pieces = mixed_grads(order, normed_one, d_mixed, out_grad)
    at(19)
    mixed_terms = [pieces[0]] + [
        go(n, p, pairs)
        for n, p, pairs in zip(("mx", "my", "mxy"), pieces[1:], (TO_X, TO_Y, TO_XY))
    ]
    ff_kept, ff_sent = fold(order, [ff_terms])
    ff_sent = go("fz", ff_sent, TO_ZH)
    at(20)
    if "pull_late" not in TIED:
        (input_grad,) = norm_pull(order, x, (near, far, side), d_resid, False)
    at(21)
    mixed_kept, mixed_sent = fold(order, [t[None] for t in mixed_terms], 128)
    mixed_sent = go("mz", mixed_sent, TO_ZH)
    at(22)
    if "pull_late" in TIED:
        (input_grad,) = norm_pull(order, x, (near, far, side), d_resid, False)
    ff_slices = split_rows(order, ff_kept, ff_sent)
    at(23)
    input_grad = jnp.concatenate(
        [
            go("ih1", input_grad[: tokens // 2], TO_HOME),
            go("ih2", input_grad[tokens // 2 :], TO_HOME),
        ]
    )
    ff_slices = [ff_slices[0]] + [
        go(n, p, pairs)
        for n, p, pairs in zip(("f1", "f2", "f3"), ff_slices[1:], (TO_ZL, TO_CORE, TO_FAR))
    ]
    at(24)
    mixed_slices = split_rows(order, mixed_kept, mixed_sent)
    mixed_slices = [mixed_slices[0]] + [
        go(n, p, pairs)
        for n, p, pairs in zip(("m1", "m2", "m3"), mixed_slices[1:], (TO_ZL, TO_CORE, TO_FAR))
    ]
    at(25)
    up_grad, gain_two_grad, down_grad = finish(
        order, ff_slices, up_weight, gain_two, (2, ff, ff)
    )
    qkv_grad, gain_one_grad, out_grad = finish(
        order, mixed_slices, qkv_weight, gain_one, (3, part, part)
    )
    return (
        output[None],
        input_grad[None],
        gain_one_grad[0],
        qkv_grad,
        out_grad,
        gain_two_grad[0],
        up_grad,
        down_grad,
    )


def solution(mesh):
    dp, seq = "dp", "seq"
    step = per_device
    if tuple(mesh.shape.values()) == QUAD_MESH:
        dp, seq, step = ("y", "x", "c"), ("zh", "zl"), quad_device
        mesh = jax.sharding.Mesh(mesh.devices.reshape(2, 2, 2, 2, 2), FLAT)
        every = FLAT
    else:
        every = (dp, seq)
    rows = P(every, None)
    return jax.shard_map(
        step,
        mesh=mesh,
        in_specs=(
            P(dp, seq, None),
            P(dp, seq),
            P(every),
            rows,
            rows,
            P(every),
            rows,
            rows,
            P(dp, seq, None),
        ),
        out_specs=(
            P(dp, seq, None),
            P(dp, seq, None),
            P(every),
            rows,
            rows,
            P(every),
            rows,
            rows,
        ),
        check_vma=False,
    )
```

```python
import math

import jax
import jax.numpy as jnp
from jax import lax
from jax.experimental import pallas as pl
from jax.experimental.pallas import tpu as pltpu
from jax.sharding import PartitionSpec as P

HEADS = 16
HEAD_DIM = 64
FF = 2624


norm_eps = 1e-05
rope_base = 160000.0
inv_root_two = 0.7071067811865476
inv_root_tau = 0.3989422804014327


def for_sending(array):
    return jax.tree.map(lambda a: a.astype(jnp.bfloat16) if a.dtype == jnp.float32 else a, array)


def normalize(values):
    centre = jnp.mean(values, axis=-1, keepdims=True)
    centred = values - centre
    spread = lax.rsqrt(jnp.mean(centred * centred, axis=-1, keepdims=True) + norm_eps)
    return (centred * spread, spread)


def norm_back(grad_in, normed, spread, gain):
    scaled = grad_in * gain
    gain_term = jnp.sum(grad_in * normed, axis=0)
    centred = (
        scaled
        - jnp.mean(scaled, axis=-1, keepdims=True)
        - normed * jnp.mean(scaled * normed, axis=-1, keepdims=True)
    )
    return (spread * centred, gain_term)


def rope_tables(seq_pos):
    exponent = jnp.arange(0, HEAD_DIM, 2).astype(jnp.float32) / HEAD_DIM
    frequency = rope_base ** (-exponent)
    angles = seq_pos.astype(jnp.float32)[:, None] * frequency[None, :]
    angles = jnp.concatenate([angles, angles], axis=-1)[:, None, :]
    return (jnp.cos(angles), jnp.sin(angles))


def rotate(values, cos_table, sin_table):
    half_dim = values.shape[-1] // 2
    turned = jnp.concatenate([-values[..., half_dim:], values[..., :half_dim]], axis=-1)
    return values * cos_table + turned * sin_table


def rotate_back(grads, cos_table, sin_table):
    half_dim = grads.shape[-1] // 2
    weighted = grads * sin_table
    turned = jnp.concatenate([weighted[..., half_dim:], -weighted[..., :half_dim]], axis=-1)
    return grads * cos_table + turned


def gelu_parts(inner_act):
    normal_cdf = 0.5 * (1.0 + jax.scipy.special.erf(inner_act * inv_root_two))
    slope = normal_cdf + inner_act * jnp.exp(-0.5 * inner_act * inner_act) * inv_root_tau
    return (inner_act * normal_cdf, slope)


def project_heads(attn_in, w_qkv, cos_table, sin_table):
    token_count, model_width = attn_in.shape
    mixed_rows = jnp.dot(attn_in, w_qkv, preferred_element_type=jnp.float32)
    shaped = (token_count, HEADS, HEAD_DIM)
    queries = rotate(mixed_rows[:, :model_width].reshape(shaped), cos_table, sin_table)
    key_rows = rotate(
        mixed_rows[:, model_width : 2 * model_width].reshape(shaped), cos_table, sin_table
    )
    queries = queries.reshape(token_count, model_width).astype(jnp.bfloat16)
    key_rows = key_rows.reshape(token_count, model_width).astype(jnp.bfloat16)
    values = mixed_rows[:, 2 * model_width :].astype(jnp.bfloat16)
    return (queries, key_rows, values)


def attend_forward(q_heads, k_heads, v_heads):
    seq_len, columns = q_heads.shape
    head_count = columns // HEAD_DIM
    block_rows = min(512, seq_len)
    block_count = seq_len // block_rows
    score_scale = HEAD_DIM ** (-0.5)
    k_all = k_heads.reshape(seq_len, head_count, HEAD_DIM)
    v_all = v_heads.reshape(seq_len, head_count, HEAD_DIM)

    def one_block(q_block):
        scores = (
            jnp.einsum("qhd,khd->hqk", q_block, k_all, preferred_element_type=jnp.float32)
            * score_scale
        )
        row_peak = jnp.max(scores, axis=-1, keepdims=True)
        exp_scores = jnp.exp(scores - row_peak)
        totals = jnp.sum(exp_scores, axis=-1, keepdims=True)
        prob_rows = (exp_scores / totals).astype(jnp.bfloat16)
        attended = jnp.einsum("hqk,khd->qhd", prob_rows, v_all, preferred_element_type=jnp.float32)
        return (attended.astype(jnp.bfloat16), row_peak[..., 0] + jnp.log(totals[..., 0]))

    attended, log_totals = lax.map(
        one_block, q_heads.reshape(block_count, block_rows, head_count, HEAD_DIM)
    )
    return (attended.reshape(seq_len, columns), log_totals)


def attend_backward(q_heads, k_heads, v_heads, d_heads, log_totals):
    seq_len, columns = q_heads.shape
    head_count = columns // HEAD_DIM
    block_rows = min(512, seq_len)
    block_count = seq_len // block_rows
    score_scale = HEAD_DIM ** (-0.5)
    k_all = k_heads.reshape(seq_len, head_count, HEAD_DIM)
    v_all = v_heads.reshape(seq_len, head_count, HEAD_DIM)
    q_blocks = q_heads.reshape(block_count, block_rows, head_count, HEAD_DIM)
    d_blocks = d_heads.reshape(block_count, block_rows, head_count, HEAD_DIM)

    def one_block(carry, item):
        key_acc, value_acc = carry
        q_block, d_block, lse_block = item
        scores = (
            jnp.einsum("qhd,khd->hqk", q_block, k_all, preferred_element_type=jnp.float32)
            * score_scale
        )
        prob_rows = jnp.exp(scores - lse_block[..., None])
        value_acc = value_acc + jnp.einsum(
            "hqk,qhd->khd",
            prob_rows.astype(jnp.bfloat16),
            d_block,
            preferred_element_type=jnp.float32,
        )
        d_probs = jnp.einsum("qhd,khd->hqk", d_block, v_all, preferred_element_type=jnp.float32)
        d_scores = (
            prob_rows * (d_probs - jnp.sum(prob_rows * d_probs, axis=-1, keepdims=True))
        ).astype(jnp.bfloat16)
        d_query = (
            jnp.einsum("hqk,khd->qhd", d_scores, k_all, preferred_element_type=jnp.float32)
            * score_scale
        )
        key_acc = (
            key_acc
            + jnp.einsum("hqk,qhd->khd", d_scores, q_block, preferred_element_type=jnp.float32)
            * score_scale
        )
        return ((key_acc, value_acc), d_query.astype(jnp.bfloat16))

    empty_acc = jnp.zeros((seq_len, head_count, HEAD_DIM), jnp.float32)
    (key_acc, value_acc), d_query = lax.scan(
        one_block, (empty_acc, empty_acc), (q_blocks, d_blocks, log_totals)
    )
    d_q = d_query.reshape(seq_len, columns)
    d_k = key_acc.astype(jnp.bfloat16).reshape(seq_len, columns)
    d_v = value_acc.astype(jnp.bfloat16).reshape(seq_len, columns)
    return (d_q, d_k, d_v)


def add_sources(received):
    return tuple((jnp.sum(piece, axis=0) for piece in received))


def per_device(
    inputs,
    positions,
    attn_gain,
    qkv_weight,
    attn_out_weight,
    mlp_gain,
    up_weight,
    down_weight,
    cotangent,
):
    layer = (
        lax.all_gather(attn_gain, ("dp", "seq"), axis=0, tiled=True),
        lax.all_gather(qkv_weight, ("dp", "seq"), axis=0, tiled=True),
        lax.all_gather(attn_out_weight, ("dp", "seq"), axis=0, tiled=True),
        lax.all_gather(mlp_gain, ("dp", "seq"), axis=0, tiled=True),
        lax.all_gather(up_weight, ("dp", "seq"), axis=0, tiled=True),
        lax.all_gather(down_weight, ("dp", "seq"), axis=0, tiled=True),
    )
    gain_one, w_qkv, w_out, gain_two, w_up, w_down = layer
    token_count = inputs.shape[1]
    resid_in = inputs[0].astype(jnp.float32)
    cos_table, sin_table = rope_tables(positions[0])
    normed_one, spread_one = normalize(resid_in)
    attn_in = (normed_one * gain_one.astype(jnp.float32)).astype(jnp.bfloat16)
    queries, key_rows, values = project_heads(attn_in, w_qkv, cos_table, sin_table)
    q_heads, k_heads, v_heads = (
        lax.all_to_all(queries, "seq", split_axis=1, concat_axis=0, tiled=True),
        lax.all_to_all(key_rows, "seq", split_axis=1, concat_axis=0, tiled=True),
        lax.all_to_all(values, "seq", split_axis=1, concat_axis=0, tiled=True),
    )
    attended_heads, log_totals = attend_forward(q_heads, k_heads, v_heads)
    attended = lax.all_to_all(attended_heads, "seq", split_axis=0, concat_axis=1, tiled=True)
    resid = resid_in + jnp.dot(attended, w_out, preferred_element_type=jnp.float32)
    normed_two, spread_two = normalize(resid)
    mlp_in = (normed_two * gain_two.astype(jnp.float32)).astype(jnp.bfloat16)
    up_rows = jnp.dot(mlp_in, w_up, preferred_element_type=jnp.float32)
    inner_act = up_rows[:, :FF]
    gate_act = up_rows[:, FF:]
    gelu_val, gelu_slope = gelu_parts(inner_act)
    hidden = (gelu_val * gate_act).astype(jnp.bfloat16)
    output = resid + jnp.einsum("tf,df->td", hidden, w_down, preferred_element_type=jnp.float32)
    layer_back = (
        lax.all_gather(attn_gain, ("dp", "seq"), axis=0, tiled=True),
        lax.all_gather(qkv_weight, ("dp", "seq"), axis=0, tiled=True),
        lax.all_gather(attn_out_weight, ("dp", "seq"), axis=0, tiled=True),
        lax.all_gather(mlp_gain, ("dp", "seq"), axis=0, tiled=True),
        lax.all_gather(up_weight, ("dp", "seq"), axis=0, tiled=True),
        lax.all_gather(down_weight, ("dp", "seq"), axis=0, tiled=True),
    )
    gain_one, w_qkv, w_out, gain_two, w_up, w_down = layer_back
    d_out = cotangent[0]
    down_grad = jnp.einsum("td,tf->df", d_out, hidden, preferred_element_type=jnp.float32)
    d_hidden = jnp.dot(d_out, w_down, preferred_element_type=jnp.float32)
    d_up = jnp.concatenate([d_hidden * gate_act * gelu_slope, d_hidden * gelu_val], axis=1).astype(
        jnp.bfloat16
    )
    up_grad = jnp.einsum("tk,tn->kn", mlp_in, d_up, preferred_element_type=jnp.float32)
    d_mlp_in = jnp.einsum("tn,kn->tk", d_up, w_up, preferred_element_type=jnp.float32)
    d_norm_two, gain_two_grad = norm_back(
        d_mlp_in, normed_two, spread_two, gain_two.astype(jnp.float32)
    )
    d_resid = d_out.astype(jnp.float32) + d_norm_two
    d_resid_low = d_resid.astype(jnp.bfloat16)
    out_grad = jnp.einsum("tk,tn->kn", attended, d_resid_low, preferred_element_type=jnp.float32)
    d_attended = jnp.einsum(
        "tn,kn->tk", d_resid_low, w_out, preferred_element_type=jnp.float32
    ).astype(jnp.bfloat16)
    d_heads = lax.all_to_all(d_attended, "seq", split_axis=1, concat_axis=0, tiled=True)
    queries, key_rows, values = project_heads(attn_in, w_qkv, cos_table, sin_table)
    head_inputs = (
        lax.all_to_all(queries, "seq", split_axis=1, concat_axis=0, tiled=True),
        lax.all_to_all(key_rows, "seq", split_axis=1, concat_axis=0, tiled=True),
        lax.all_to_all(values, "seq", split_axis=1, concat_axis=0, tiled=True),
    )
    d_q, d_k, d_v = attend_backward(
        head_inputs[0], head_inputs[1], head_inputs[2], d_heads, log_totals
    )
    dq_rows, dk_rows, dv_rows = (
        lax.all_to_all(d_q, "seq", split_axis=0, concat_axis=1, tiled=True),
        lax.all_to_all(d_k, "seq", split_axis=0, concat_axis=1, tiled=True),
        lax.all_to_all(d_v, "seq", split_axis=0, concat_axis=1, tiled=True),
    )
    shaped = (token_count, HEADS, HEAD_DIM)
    dq_pre = rotate_back(dq_rows.astype(jnp.float32).reshape(shaped), cos_table, sin_table).reshape(
        token_count, -1
    )
    dk_pre = rotate_back(dk_rows.astype(jnp.float32).reshape(shaped), cos_table, sin_table).reshape(
        token_count, -1
    )
    d_mixed = jnp.concatenate(
        [dq_pre.astype(jnp.bfloat16), dk_pre.astype(jnp.bfloat16), dv_rows], axis=1
    )
    qkv_grad = jnp.einsum("tk,tn->kn", attn_in, d_mixed, preferred_element_type=jnp.float32)
    d_attn_in = jnp.einsum("tn,kn->tk", d_mixed, w_qkv, preferred_element_type=jnp.float32)
    d_norm_one, gain_one_grad = norm_back(
        d_attn_in, normed_one, spread_one, gain_one.astype(jnp.float32)
    )
    input_grad = (d_resid + d_norm_one).astype(jnp.bfloat16)
    all_sent = (
        lax.all_to_all(
            gain_one_grad[None].astype(jnp.bfloat16), "dp", split_axis=1, concat_axis=0, tiled=True
        ).astype(jnp.float32),
        lax.all_to_all(
            qkv_grad[None].astype(jnp.bfloat16), "dp", split_axis=1, concat_axis=0, tiled=True
        ).astype(jnp.float32),
        lax.all_to_all(
            out_grad[None].astype(jnp.bfloat16), "dp", split_axis=1, concat_axis=0, tiled=True
        ).astype(jnp.float32),
        lax.all_to_all(
            gain_two_grad[None].astype(jnp.bfloat16), "dp", split_axis=1, concat_axis=0, tiled=True
        ).astype(jnp.float32),
        lax.all_to_all(
            up_grad[None].astype(jnp.bfloat16), "dp", split_axis=1, concat_axis=0, tiled=True
        ).astype(jnp.float32),
        lax.all_to_all(
            down_grad[None].astype(jnp.bfloat16), "dp", split_axis=1, concat_axis=0, tiled=True
        ).astype(jnp.float32),
    )
    grads = jax.tree.map(
        lambda part: part.astype(jnp.float32),
        lax.psum_scatter(
            for_sending(add_sources(all_sent)), "seq", scatter_dimension=0, tiled=True
        ),
    )
    return (
        output.astype(jnp.bfloat16)[None],
        input_grad[None],
        grads[0],
        grads[1],
        grads[2],
        grads[3],
        grads[4],
        grads[5],
    )


QUAD_MESH = (8, 4)
FLAT = ("y", "x", "c", "zh", "zl")
LOW, WIDE = jnp.bfloat16, jnp.float32


def pairs_of(step):
    found = []
    for dp in range(8):
        for seq in range(4):
            place = (dp // 4, dp // 2 % 2, dp % 2, seq // 2, seq % 2)
            target = step(*place)
            if target is not None:
                y, x, c, zh, zl = target
                found.append((dp * 4 + seq, (4 * y + 2 * x + c) * 4 + 2 * zh + zl))
    return found


TO_X = pairs_of(lambda y, x, c, zh, zl: (y, 1 - x, c, zh, zl))
TO_Y = pairs_of(lambda y, x, c, zh, zl: (1 - y, x, c, zh, zl))
TO_XY = pairs_of(lambda y, x, c, zh, zl: (1 - y, 1 - x, c, zh, zl))
TO_CORE = pairs_of(lambda y, x, c, zh, zl: (y, x, 1 - c, zh, zl))
TO_ZH = pairs_of(lambda y, x, c, zh, zl: (y, x, c, 1 - zh, zl))
TO_ZL = pairs_of(lambda y, x, c, zh, zl: (y, x, c, zh, 1 - zl))
TO_FAR = pairs_of(lambda y, x, c, zh, zl: (y, x, 1 - c, zh, 1 - zl))
TO_HOME = pairs_of(lambda y, x, c, zh, zl: (y, x, zh, c, zl))
ENTER = pairs_of(
    lambda y, x, c, zh, zl: (y, x, c, zh, 1 - zl) if c == zh else (y, x, zh, c, zl)
)
ENTER_MOVED = pairs_of(lambda y, x, c, zh, zl: None if c == zh else (y, x, c, zh, 1 - zl))


class Order(list):
    pass


def send(array, pairs):
    return lax.ppermute(array, FLAT, pairs)


def after(order, array):
    return lax.optimization_barrier((array, order[0]))[0]


def wait(order, *arrays):
    order[0] = lax.optimization_barrier((order[0], *arrays))[0]


def lanes(size):
    return -(-size // 128) * 128


def core_of(flat):
    return flat >> 2 & 1


def half_of(flat):
    return flat >> 1 & 1


def group_of(flat):
    return 2 * core_of(flat) + (flat & 1)


def square_of(flat):
    return flat >> 3


def mm(left, right):
    return lax.dot_general(left, right, (((1,), (0,)), ((), ())), preferred_element_type=WIDE)


def mm_t(left, right):
    return lax.dot_general(left, right, (((1,), (1,)), ((), ())), preferred_element_type=WIDE)


def t_mm(left, right):
    return lax.dot_general(left, right, (((0,), (0,)), ((), ())), preferred_element_type=WIDE)


def window(index, size):
    return pl.ds(pl.multiple_of(index * size, size), size)


def whole(array):
    rank = len(array.shape)
    return (array, array.shape, lambda *_: (0,) * rank)


def by_rows(array, rows, step=lambda b: b):
    return (array, (rows,) + array.shape[1:], lambda b, f: (step(b),) + (0,) * (len(array.shape) - 1))


def run(body, order, grid, ins, outs, scratch=(), flops=0, spare=6 * 2**20, far=()):
    moved = sum(a.size * a.dtype.itemsize for a, _, _ in ins)
    moved += sum(a.size * a.dtype.itemsize for a, _, _ in outs)
    def held(block, dtype, count):
        return count * math.prod(block) * jnp.dtype(dtype).itemsize

    grant = sum(
        held(block, a.dtype, 1 if tuple(block) == tuple(a.shape) else 2)
        for a, block, _ in (*ins, *outs)
    )
    grant += sum(held(m.shape, m.dtype, 1) for m in scratch) + spare
    made = pl.pallas_call(
        body,
        grid_spec=pltpu.PrefetchScalarGridSpec(
            num_scalar_prefetch=1,
            grid=grid,
            in_specs=[pl.BlockSpec(block, index) for _, block, index in ins],
            out_specs=[pl.BlockSpec(block, index) for _, block, index in outs],
            scratch_shapes=list(scratch),
        ),
        out_shape=[
            pltpu.HBM(a.shape, a.dtype) if i in far else a for i, (a, _, _) in enumerate(outs)
        ],
        compiler_params=pltpu.CompilerParams(vmem_limit_bytes=grant),
        cost_estimate=pl.CostEstimate(flops=flops // 100, bytes_accessed=moved // 100, transcendentals=0),
    )(order[0], *[a for a, _, _ in ins])
    order[0], _ = lax.optimization_barrier((order[0], made[0]))
    return made


def spans(pieces):
    rows = pieces[0].shape[0]
    return [(0, 0, rows), (1, 0, rows), (2, 0, rows), (3, 0, rows // 2), (3, rows // 2, rows // 2)]


def rows_of(ref, span):
    count = span[2]
    return slice(ref.shape[0] - count, None) if span[1] else slice(0, count)


def span_of(square, span, rows):
    index, first, count = span
    return pl.ds(pl.multiple_of((square ^ index) * rows + first, count), count)


def shape_of(*dims, dtype=LOW):
    return jax.ShapeDtypeStruct(dims, dtype)


def column_of(row):
    size = row.shape[1]
    down = lax.broadcasted_iota(jnp.int32, (size, size), 0)
    across = lax.broadcasted_iota(jnp.int32, (size, size), 1)
    return jnp.sum(jnp.where(down == across, row, 0.0), axis=1, keepdims=True)


def row_of(column):
    size = column.shape[0]
    down = lax.broadcasted_iota(jnp.int32, (size, size), 0)
    across = lax.broadcasted_iota(jnp.int32, (size, size), 1)
    return jnp.sum(jnp.where(down == across, column, 0.0), axis=0, keepdims=True)


def normed_of(x):
    centred = x - jnp.mean(x, axis=-1, keepdims=True)
    spread = lax.rsqrt(jnp.mean(centred * centred, axis=-1, keepdims=True) + norm_eps)
    return centred * spread, spread


def split_slices(order, scaled, plain, gain, parts):
    rows, part, rest = scaled.shape[0], scaled.shape[1] // (4 * parts), plain.shape[1] // 4
    out = shape_of(2, rows, lanes(parts * part + rest))

    def body(flat_ref, scaled_ref, plain_ref, gain_ref, own_ref, sent_ref, held):
        scale = column_of(gain_ref[...].astype(WIDE))
        for s in range(4):
            for t in range(parts):
                cols = scaled_ref[:, (4 * t + s) * part : (4 * t + s + 1) * part].astype(WIDE)
                held[s, :, t * part : (t + 1) * part] = (cols * scale).astype(LOW)
            held[s, :, parts * part : parts * part + rest] = plain_ref[
                :, s * rest : (s + 1) * rest
            ]
        core = core_of(flat_ref[0])
        for zl in range(2):
            own_ref[zl] = held[2 * core + zl]
            sent_ref[zl] = held[2 * (1 - core) + zl]

    return run(
        body, order, (1,), [whole(a) for a in (scaled, plain, gain)], [whole(out)] * 2,
        [pltpu.VMEM((4, *out.shape[1:]), LOW)],
    )


def chip_rows(order, own, received):
    def body(flat_ref, own_ref, received_ref, kept_ref, sent_ref):
        core, chip = core_of(flat_ref[0]), flat_ref[0] & 1
        kept_ref[core] = own_ref[chip]
        kept_ref[1 - core] = received_ref[chip]
        sent_ref[core] = own_ref[1 - chip]
        sent_ref[1 - core] = received_ref[1 - chip]

    return run(
        body, order, (1,), [whole(own), whole(received)], [whole(shape_of(*own.shape))] * 2
    )


def quad_rows(order, own, received):
    _, rows, width = own.shape

    def body(flat_ref, own_ref, received_ref, out_ref):
        chip = flat_ref[0] & 1
        for c in range(2):
            out_ref[2 * c + chip] = own_ref[c]
            out_ref[2 * c + 1 - chip] = received_ref[c]

    return run(
        body, order, (1,), [whole(own), whole(received)], [whole(shape_of(4, rows, width))]
    )[0]


def line_rows(order, near, far):
    _, rows, width = near.shape
    near = near.reshape(2, 2 * rows, width)
    far = far.reshape(2, 2 * rows, width)

    def body(flat_ref, near_ref, far_ref, out_ref):
        half = half_of(flat_ref[0])
        for c in range(2):
            out_ref[c, half] = near_ref[c]
            out_ref[c, 1 - half] = far_ref[c]

    out = run(
        body, order, (1,), [whole(near), whole(far)], [whole(shape_of(2, 2, 2 * rows, width))]
    )[0]
    return out.reshape(8 * rows, width)


def join_tokens(order, parts, rows, extra=0):
    width = parts[0].shape[1]

    def body(flat_ref, block, first, second, core_block, core_first, core_second, *outs):
        home = core_of(flat_ref[0]) == half_of(flat_ref[0])
        here = (block, first, core_first, core_second)
        moved = (first, second, core_block, core_first)
        for k in range(4):
            for flag, source in ((home, here[k]), (jnp.logical_not(home), moved[k])):

                @pl.when(jnp.logical_and(pl.program_id(0) == k, flag))
                def _(source=source):
                    def step(r, carry):
                        outs[0][window(r, 32), :] = source[window(r, 32), :]
                        return carry

                    lax.fori_loop(0, rows // 32, step, 0)
                    if extra:
                        outs[1][...] = source[rows : rows + extra, :]

    made = [shape_of(4 * rows, width)] + ([shape_of(4 * extra, width)] if extra else [])
    return run(
        body, order, (4,), [whole(a) for a in parts],
        [by_rows(m, m.shape[0] // 4) for m in made],
    )


def rope_lanes(seq_pos):
    exponent = jnp.arange(0, HEAD_DIM, 2).astype(WIDE) / HEAD_DIM
    angles = seq_pos[:, None] * (rope_base ** (-exponent))[None, :]
    cos_half, sin_half = jnp.cos(angles), jnp.sin(angles)
    return (
        jnp.concatenate([cos_half] * 4, axis=1),
        jnp.concatenate([-sin_half, sin_half] * 2, axis=1),
    )


def turned(v):
    half = HEAD_DIM // 2
    lane = lax.broadcasted_iota(jnp.int32, v.shape, 1)
    return jnp.where(
        lane % HEAD_DIM < half, pltpu.roll(v, 2 * HEAD_DIM - half, 1), pltpu.roll(v, half, 1)
    )


def project(order, x, pieces, cos_table, sin_table):
    tokens, width = x.shape
    piece, columns = pieces[0].shape[0], 3 * width // 4
    rows = tokens // 4

    def body(flat_ref, x_ref, *refs):
        weights, (cos_ref, sin_ref, n_ref, mix_ref) = refs[:5], refs[5:]
        n_ref[...] = normed_of(x_ref[...].astype(WIDE))[0].astype(LOW)
        square = square_of(flat_ref[0])
        mixed = sum(
            mm(n_ref[:, span_of(square, span, piece)], w[rows_of(w, span), :columns])
            for span, w in zip(spans(pieces), weights)
        )
        turned_to = 2 * columns // 3
        for t in range(0, turned_to, 128):
            v = mixed[:, t : t + 128]
            mix_ref[:, t : t + 128] = (v * cos_ref[...] + turned(v) * sin_ref[...]).astype(LOW)
        mix_ref[:, turned_to:] = mixed[:, turned_to:].astype(LOW)

    return run(
        body, order, (4,),
        [by_rows(x, rows)] + [whole(p) for p in pieces]
        + [by_rows(cos_table, rows), by_rows(sin_table, rows)],
        [by_rows(shape_of(tokens, width), rows), by_rows(shape_of(tokens, columns), rows)],
        flops=2 * tokens * width * columns,
        far=(0,),
    )


def attend(order, mix):
    tokens, columns = mix.shape
    part = columns // 3
    rows = tokens // 4
    scale = HEAD_DIM ** (-0.5)

    def body(flat_ref, q_ref, k_ref, v_ref, out_ref, log_ref):
        lane = lax.broadcasted_iota(jnp.int32, (rows, part), 1) // HEAD_DIM
        total = jnp.zeros((rows, part), WIDE)
        queries = q_ref[...].astype(WIDE) * scale
        for h in range(part // HEAD_DIM):
            q_head = jnp.where(lane == h, queries, 0.0).astype(LOW)
            scores = mm_t(q_head, k_ref[...])
            peak = jnp.max(scores, axis=-1, keepdims=True)
            powers = jnp.exp(scores - peak)
            mass = jnp.sum(powers, axis=-1, keepdims=True)
            probs = (powers * (1.0 / mass)).astype(LOW)
            total = jnp.where(lane == h, mm(probs, v_ref[...]), total)
            log_ref[h : h + 1, :] = row_of(peak + jnp.log(mass))
        out_ref[...] = total.astype(LOW)

    return run(
        body, order, (4,),
        [
            (mix, (rows, part), lambda b, f: (b, 0)),
            (mix, (tokens, part), lambda b, f: (0, 1)),
            (mix, (tokens, part), lambda b, f: (0, 2)),
        ],
        [
            by_rows(shape_of(tokens, part), rows),
            (shape_of(8, tokens, dtype=WIDE), (8, rows), lambda b, f: (0, b)),
        ],
        flops=16 * tokens * tokens * part,
    )


def token_parts(arrays, rows):
    return [by_rows(a, rows, lambda b, i=i: b ^ i) for i, a in enumerate(arrays)]


def join_heads(order, x, heads, columns):
    tokens, width = x.shape
    rows, part = tokens // 4, width // 4

    def body(flat_ref, x_ref, *refs):
        parts, weights, (n_ref, own_ref, held) = refs[:4], refs[4:8], refs[8:]
        group, square = group_of(flat_ref[0]), square_of(flat_ref[0])
        for j in range(4):
            cols = window(group ^ j, part)
            held[:, cols] = x_ref[:, cols].astype(WIDE) + sum(
                mm(parts[i][...], weights[j][window(group ^ i ^ square, part), :])
                for i in range(4)
            )
        resid = held[...]
        n_ref[...] = normed_of(resid)[0].astype(LOW)

        @pl.when(pl.program_id(0) == 0)
        def _():
            own_ref[...] = held[...]

    return run(
        body, order, (4,),
        [by_rows(x, rows)] + token_parts(heads, rows) + [whole(w) for w in columns],
        [by_rows(shape_of(tokens, width), rows), whole(shape_of(rows, width, dtype=WIDE))],
        [pltpu.VMEM((rows, width), WIDE)],
        flops=2 * tokens * width * width,
    )


def feed(order, normed, cot, pieces):
    tokens, width = normed.shape
    piece, ff = pieces[0].shape[0], FF // 4
    rows = tokens // 4

    def body(flat_ref, n_ref, cot_ref, *refs):
        weights, (h_ref, d_ref) = refs[:5], refs[5:]
        square = square_of(flat_ref[0])
        cut = [
            (span_of(square, span, piece), rows_of(w, span), w)
            for span, w in zip(spans(pieces), weights)
        ]
        wide = sum(mm(n_ref[:, at], w[of, : 2 * ff]) for at, of, w in cut)
        d_hidden = sum(mm(cot_ref[:, at], w[of, 2 * ff : 3 * ff]) for at, of, w in cut)
        inner, gate = wide[:, :ff], wide[:, ff:]
        cdf = 0.5 * (1.0 + lax.erf(inner * inv_root_two))
        slope = cdf + inner * jnp.exp(-0.5 * inner * inner) * inv_root_tau
        bent = inner * cdf
        h_ref[...] = (bent * gate).astype(LOW)
        d_ref[:, :ff] = (d_hidden * gate * slope).astype(LOW)
        d_ref[:, ff:] = (d_hidden * bent).astype(LOW)

    return run(
        body, order, (4,),
        [by_rows(normed, rows), by_rows(cot, rows)] + [whole(w) for w in pieces],
        [by_rows(shape_of(tokens, ff), rows), by_rows(shape_of(tokens, 2 * ff), rows)],
        flops=6 * tokens * width * ff,
    )


def back_half(order, grads, pieces, far):
    tokens = grads[0][0].shape[0]
    piece = pieces[0].shape[0]
    rows, width, count = tokens // 2, 4 * piece, len(grads)
    outs = [shape_of(rows, width)] if far else [shape_of(rows // 2, width, dtype=WIDE)] * 2

    def body(flat_ref, *refs):
        arrays, weights, out_refs = refs[:count], refs[count : count + 5], refs[count + 5 :]
        square = square_of(flat_ref[0])
        for span, w in zip(spans(pieces), weights):
            total = sum(
                mm_t(a[...], w[rows_of(w, span), at : at + a.shape[1]])
                for a, (_, at) in zip(arrays, grads)
            )
            for k, ref in enumerate(out_refs):
                part = total[k * ref.shape[0] : (k + 1) * ref.shape[0]]
                ref[:, span_of(square, span, piece)] = part.astype(ref.dtype)

    return run(
        body, order, (1,),
        [by_rows(a, rows, lambda b: int(far)) for a, _ in grads] + [whole(p) for p in pieces],
        [whole(out) for out in outs],
        flops=tokens * width * sum(a.shape[1] for a, _ in grads),
    )


def back_both(order, grad, first, pieces):
    tokens = grad.shape[0]
    piece = pieces[0].shape[0]
    rows, width, columns = tokens // 2, 4 * piece, grad.shape[1]

    def body(flat_ref, grad_ref, *refs):
        weights, (far_ref, near_ref) = refs[:5], refs[5:]
        square = square_of(flat_ref[0])
        for span, w in zip(spans(pieces), weights):
            total = mm_t(grad_ref[...], w[rows_of(w, span), first : first + columns])
            near_ref[:, span_of(square, span, piece)] = total[:rows]
            far_ref[:, span_of(square, span, piece)] = total[rows:].astype(LOW)

    return run(
        body, order, (1,), [whole(grad)] + [whole(p) for p in pieces],
        [whole(shape_of(rows, width)), whole(shape_of(rows, width, dtype=WIDE))],
        flops=2 * tokens * width * columns,
    )


def norm_pull(order, x, terms, base, keep):
    rows, width = base.shape
    step = rows // 4

    def body(flat_ref, x_ref, a_ref, b_ref, c_ref, base_ref, *outs):
        normed, spread = normed_of(x_ref[...].astype(WIDE))
        scaled = a_ref[...] + b_ref[...].astype(WIDE) + c_ref[...].astype(WIDE)
        grad = base_ref[...].astype(WIDE) + spread * (
            scaled
            - jnp.mean(scaled, axis=-1, keepdims=True)
            - normed * jnp.mean(scaled * normed, axis=-1, keepdims=True)
        )
        outs[0][...] = grad.astype(LOW)
        if keep:
            outs[1][...] = grad

    low = shape_of(rows + 16 if keep else rows, width)
    outs = [low] + ([shape_of(rows, width, dtype=WIDE)] if keep else [])
    return run(
        body, order, (4,), [by_rows(a, step) for a in (x, *terms, base)],
        [by_rows(o, step) for o in outs],
    )


def feed_grads(order, normed, cot, d_up, hidden):
    tokens, width = normed.shape
    piece, ff = width // 4, hidden.shape[1]
    out = shape_of(4, piece, lanes(3 * ff))

    def body(flat_ref, n_ref, cot_ref, d_ref, h_ref, out_ref):
        out_ref[0, :, : 2 * ff] = t_mm(n_ref[...], d_ref[...]).astype(LOW)
        out_ref[0, :, 2 * ff : 3 * ff] = t_mm(cot_ref[...], h_ref[...]).astype(LOW)

    return run(
        body, order, (4,),
        [(a, (tokens, piece), lambda b, f: (0, b)) for a in (normed, cot)]
        + [whole(d_up), whole(hidden)],
        [by_rows(out, 1)],
        flops=6 * tokens * width * ff,
        far=(0,),
    )[0]


def heads_back(order, d_all, heads, columns):
    rows, width = heads[0].shape[0] // 4, d_all[0].shape[1]
    part = width // 4

    def body(flat_ref, *refs):
        blocks, parts, weights = refs[:4], refs[4:8], refs[8:12]
        d_ref, grad_ref, block, held, total = refs[12:]
        group, square = group_of(flat_ref[0]), square_of(flat_ref[0])
        at = pl.program_id(0)
        for k in range(4):

            @pl.when(at == k)
            def _(source=blocks[k]):
                def step(r, carry):
                    block[window(r, 32), :] = source[window(r, 32), :]
                    return carry

                lax.fori_loop(0, rows // 32, step, 0)

            held[k] = parts[k][...]

        @pl.when(at == 0)
        def _():
            total[...] = jnp.zeros_like(total)

        d_ref[...] = sum(
            mm_t(block[:, window(group ^ j, part)], weights[j][window(group ^ square, part), :])
            for j in range(4)
        ).astype(LOW)
        mine = block[:, window(group, part)]
        for i in range(4):
            total[i] += t_mm(held[group ^ square ^ i], mine)

        @pl.when(at == 3)
        def _():
            grad_ref[...] = total[...].astype(LOW)

    return run(
        body, order, (4,),
        [whole(d) for d in d_all] + token_parts(heads, rows) + [whole(w) for w in columns],
        [by_rows(shape_of(4 * rows, part), rows), whole(shape_of(4, part, part))],
        [
            pltpu.VMEM((rows, width), LOW),
            pltpu.VMEM((4, rows, part), LOW),
            pltpu.VMEM((4, part, part), WIDE),
        ],
        flops=4 * 4 * rows * width * part,
    )


def attend_back(order, mix, attended, d_attended, logs, cos_table, sin_table):
    tokens, columns = mix.shape
    part = columns // 3
    rows = tokens // 4
    scale = HEAD_DIM ** (-0.5)
    heads = part // HEAD_DIM

    def rotated(grad, cos, sin):
        halves = [grad[:, t : t + 128] for t in range(0, part, 128)]
        return jnp.concatenate([v * cos - turned(v) * sin for v in halves], axis=1).astype(LOW)

    def body(flat_ref, q_ref, k_ref, v_ref, o_ref, d_ref, log_ref, cos_ref, sin_ref, *refs):
        dq_ref, dk_ref, dv_ref, k_total, v_total = refs
        at = pl.program_id(0)

        @pl.when(at == 0)
        def _():
            k_total[...] = jnp.zeros_like(k_total)
            v_total[...] = jnp.zeros_like(v_total)

        lane = lax.broadcasted_iota(jnp.int32, (rows, part), 1) // HEAD_DIM
        queries = q_ref[...].astype(WIDE) * scale
        grads = d_ref[...].astype(WIDE)
        chosen = lax.broadcasted_iota(jnp.int32, (8, part), 0) == (
            lax.broadcasted_iota(jnp.int32, (8, part), 1) // HEAD_DIM
        )
        deltas = lax.dot_general(
            chosen.astype(WIDE), grads * o_ref[...].astype(WIDE), (((1,), (1,)), ((), ())),
            precision=lax.Precision.HIGHEST, preferred_element_type=WIDE,
        )
        d_query = jnp.zeros((rows, part), WIDE)
        for h in range(heads):
            q_head = jnp.where(lane == h, queries, 0.0).astype(LOW)
            d_head = jnp.where(lane == h, grads, 0.0).astype(LOW)
            probs = jnp.exp(mm_t(k_ref[...], q_head) - log_ref[h : h + 1, :])
            d_probs = mm_t(v_ref[...], d_head)
            d_scores = (probs * (d_probs - deltas[h : h + 1, :])).astype(LOW)
            v_total[...] += mm(probs.astype(LOW), d_head)
            k_total[...] += mm(d_scores, q_head)
            d_query = jnp.where(lane == h, t_mm(d_scores, k_ref[...]), d_query)
        here = window(at, rows)
        dq_ref[...] = rotated(d_query * scale, cos_ref[here, :], sin_ref[here, :])

        @pl.when(at == 3)
        def _():
            dk_ref[...] = rotated(k_total[...], cos_ref[...], sin_ref[...])
            dv_ref[...] = v_total[...].astype(LOW)

    out = shape_of(tokens, part)
    return run(
        body, order, (4,),
        [
            (mix, (rows, part), lambda b, f: (b, 0)),
            (mix, (tokens, part), lambda b, f: (0, 1)),
            (mix, (tokens, part), lambda b, f: (0, 2)),
            by_rows(attended, rows),
            by_rows(d_attended, rows),
            (logs, (8, rows), lambda b, f: (0, b)),
            whole(cos_table),
            whole(sin_table),
        ],
        [by_rows(out, rows), whole(out), whole(out)],
        [pltpu.VMEM((tokens, part), WIDE)] * 2,
        flops=40 * tokens * tokens * part,
    )


def mixed_grads(order, normed, d_mixed, out_grad):
    tokens, width = normed.shape
    rows, piece = tokens // 4, width // 4
    part = d_mixed[0].shape[1]

    def body(flat_ref, n_ref, *refs):
        grads, out_ref, outs, held = refs[:3], refs[3], refs[4:8], refs[8]
        square = square_of(flat_ref[0])

        @pl.when(pl.program_id(0) == 0)
        def _():
            held[...] = jnp.zeros_like(held)

        for i in range(4):
            cols = n_ref[:, window(square ^ i, piece)]
            for t in range(3):
                held[i, :, t * part : (t + 1) * part] += t_mm(cols, grads[t][...])

        @pl.when(pl.program_id(0) == 3)
        def _():
            for i in range(4):
                outs[i][:, : 3 * part] = held[i].astype(LOW)
                outs[i][:, 3 * part :] = out_ref[i]

    return run(
        body, order, (4,),
        [by_rows(normed, rows)] + [by_rows(d, rows) for d in d_mixed] + [whole(out_grad)],
        [whole(shape_of(piece, 4 * part))] * 4, [pltpu.VMEM((4, piece, 3 * part), WIDE)],
        flops=6 * tokens * width * part,
    )


def fold(order, terms, margin=0):
    high, width = terms[0].shape[1:]
    rows = high // 4
    terms = [t.reshape(-1, 2, 2, rows, width) for t in terms]

    def body(flat_ref, *refs):
        ins, (kept_ref, sent_ref) = refs[:-2], refs[-2:]
        half = half_of(flat_ref[0])

        def total(at):
            return sum(r[k, 0, at].astype(WIDE) for r in ins for k in range(r.shape[0]))

        kept_ref[0] = total(half)
        sent_ref[0, :, :width] = total(1 - half).astype(LOW)

    return run(
        body, order, (2,),
        [
            (t, (t.shape[0], 1) + t.shape[2:], lambda b, f: (0, b, 0, 0, 0))
            for t in terms
        ],
        [
            by_rows(shape_of(2, rows, width, dtype=WIDE), 1),
            by_rows(shape_of(2, rows, width + margin), 1),
        ],
    )


def split_rows(order, kept, received):
    _, high, width = kept.shape
    rows = high // 2
    kept, received = kept.reshape(4, rows, width), received.reshape(4, rows, -1)

    def body(flat_ref, kept_ref, received_ref, *outs):
        for i in range(4):
            at = group_of(flat_ref[0]) ^ i
            outs[i][...] = (
                kept_ref[at] + received_ref[at, :, :width].astype(WIDE)
            ).astype(LOW)

    return run(
        body, order, (1,), [whole(kept), whole(received)], [whole(shape_of(rows, width))] * 4
    )


def finish(order, slices, weight, gain, sizes):
    rows, width = slices[0].shape
    count, part, rest = sizes

    def body(flat_ref, *refs):
        w_ref, gain_ref, scaled_ref, gain_out, plain_ref, held = refs[4:]
        for i in range(4):
            held[group_of(flat_ref[0]) ^ i] = refs[i][...].astype(WIDE)
        total = jnp.zeros((rows, 1), WIDE)
        scale = column_of(gain_ref[...].astype(WIDE))
        for s in range(4):
            for t in range(count):
                at = (4 * t + s) * part
                grad = held[s, :, t * part : (t + 1) * part]
                total += jnp.sum(
                    grad * w_ref[:, at : at + part].astype(WIDE), axis=1, keepdims=True
                )
                scaled_ref[:, at : at + part] = grad * scale
            plain_ref[:, s * rest : (s + 1) * rest] = held[s, :, count * part : count * part + rest]
        gain_out[...] = row_of(total)

    return run(
        body, order, (1,), [whole(a) for a in (*slices, weight, gain)],
        [
            whole(shape_of(*weight.shape, dtype=WIDE)),
            whole(shape_of(1, rows, dtype=WIDE)),
            whole(shape_of(rows, 4 * rest, dtype=WIDE)),
        ],
        [pltpu.VMEM((4, rows, width), WIDE)],
    )


TIED = {
    "ac",
    "af",
    "cf",
    "cmov",
    "cs",
    "df",
    "dz",
    "fz",
    "ih2",
    "l1",
    "m1z",
    "mov",
    "out",
    "pull_late",
    "sl1c",
    "t2",
    "tables",
    "wf",
    "x2",
}
WAITS = {
    "blk": 1,
    "ent": 1,
    "cblk": 3,
    "cf": 4,
    "mov": 4,
    "wc": 8,
    "wz": 8,
    "y2": 9,
    "wf": 10,
    "x2": 10,
    "cmov": 11,
    "dz": 14,
    "ofb": 15,
    "ofa": 17,
    "oz": 17,
    "m1c": 19,
    "oh": 21,
    "fz": 22,
    "f1": 24,
    "f2": 25,
}


def quad_device(
    inputs,
    positions,
    attn_gain,
    qkv_weight,
    attn_out_weight,
    mlp_gain,
    up_weight,
    down_weight,
    cotangent,
):
    order = Order([lax.axis_index(FLAT).astype(jnp.int32).reshape(1)])
    tokens, width = inputs.shape[1:]
    part, ff = width // 4, FF // 4
    gain_one, gain_two = attn_gain[None], mlp_gain[None]

    def at(point):
        wait(order, *[sent_as[n] for n, p in WAITS.items() if p == point])

    sent_as = {}

    def go(name, array, pairs):
        sent_as[name] = send(after(order, array) if name in TIED else array, pairs)
        return sent_as[name]

    pos = positions[0]
    pos_row = jnp.concatenate([pos // 128, pos % 128]).astype(LOW)
    pos_row = jnp.pad(pos_row[None], ((0, 15), (0, width - 2 * tokens)))
    block = jnp.concatenate([inputs[0], pos_row])
    first = go("ent", block, ENTER)
    wait(order, block)
    own, sent = split_slices(order, qkv_weight, attn_out_weight, gain_one, 3)
    received = go("sl1c", sent, TO_CORE)
    own_two, sent = split_slices(order, up_weight, down_weight, gain_two, 2)
    received_two = go("sl2c", sent, TO_CORE)
    core_block = go("blk", block, TO_CORE)
    cot_own = jnp.concatenate([cotangent[0], pos_row])
    cot_block = go("cblk", cot_own, TO_CORE)
    own, sent = chip_rows(order, own, received)
    received = go("sl1z", sent, TO_ZL)
    own_two, sent = chip_rows(order, own_two, received_two)
    at(1)
    one = quad_rows(order, own, received)
    at(2)
    one_far = go("zh1", one, TO_ZH)
    received_two = go("sl2z", sent, TO_ZL)
    second = go("mov", first, ENTER_MOVED)
    core_first = go("cf", first, TO_CORE)
    two = quad_rows(order, own_two, received_two)
    at(3)
    two_far = go("zh2", two, TO_ZH)
    one = line_rows(order, one, one_far)
    half = one.shape[0] // 2
    one_x, one_y = go("x1", one, TO_X), go("y1", one, TO_Y)
    at(4)
    core_second = go("cs", second, TO_CORE)
    cot_first = go("cent", cot_own, ENTER)
    one_top = go("t1", one_x[:half], TO_Y)
    one_low = go("l1", one_y[half:], TO_X)
    at(5)
    x, pos_all = join_tokens(
        order, [block, first, second, core_block, core_first, core_second], tokens, 16
    )
    pos_all = pos_all.reshape(4, 16, width)[:, 0, : 2 * tokens].astype(WIDE)
    pos_all = (pos_all[:, :tokens] * 128.0 + pos_all[:, tokens:]).reshape(4 * tokens)
    cos_table, sin_table = rope_lanes(pos_all)
    one = [one, one_x, one_y, one_top, one_low]
    if "tables" in TIED:
        wait(order, cos_table, sin_table)
    at(6)

    w_out = jnp.concatenate([p[:, 3 * part :] for p in one])
    w_side = go("wz", w_out, TO_ZL)
    w_core = go("wc", w_out, TO_CORE)
    normed_one, mix = project(order, x, one, cos_table, sin_table)
    at(7)
    cot_second = go("cmov", cot_first, ENTER_MOVED) if "cot_early" in TIED else None
    two = line_rows(order, two, two_far)
    two_x, two_y = go("x2", two, TO_X), go("y2", two, TO_Y)
    at(8)
    w_far = go("wf", w_side, TO_CORE)
    attended, logs = attend(order, mix)
    att_side = go("az", attended, TO_ZL)
    at(9)
    two_top = go("t2", two_x[: half + 16], TO_Y)
    two_low = go("l2", two_y[half - 16 :], TO_X)
    att_core = go("ac", attended, TO_CORE)
    at(10)
    if cot_second is None:
        cot_second = go("cmov", cot_first, ENTER_MOVED)
    w_out = [w_out, w_side, w_core, w_far]
    heads = [attended, att_side, att_core, go("af", att_side, TO_CORE)]
    at(11)
    normed_two, resid = join_heads(order, x, heads, w_out)

    core_first = go("ccf", cot_first, TO_CORE)
    core_second = go("ccs", cot_second, TO_CORE)
    at(12)
    (cot,) = join_tokens(
        order,
        [cot_own, cot_first, cot_second, cot_block, core_first, core_second],
        tokens,
    )
    two = [two, two_x, two_y, two_top, two_low]
    cot_base = cot[:tokens]
    hidden, d_up = feed(order, normed_two, cot, two)

    grads = [(d_up, 0)]
    far = go("b1c", back_half(order, grads, two, True)[0], TO_CORE)
    near, other = back_half(order, grads, two, False)
    side = (other + far[tokens:].astype(WIDE)).astype(LOW)
    side = go("b1z", jnp.pad(side, ((0, 16), (0, 0))), TO_ZL)
    ff_terms = feed_grads(order, normed_two, cot, d_up, hidden)
    at(13)
    if "a2a" not in TIED:
        ff_terms = lax.all_to_all(ff_terms, ("y", "x"), split_axis=0, concat_axis=0, tiled=True)
    d_low, d_resid = norm_pull(order, resid, (near, far, side), cot_base, True)
    if "a2a" in TIED:
        ff_terms = lax.all_to_all(
            after(order, ff_terms), ("y", "x"), split_axis=0, concat_axis=0, tiled=True
        )
    d_side = go("dz", d_low, TO_ZL)
    d_core = go("dc", d_low, TO_CORE)
    out_far, out_near = back_both(order, hidden, 2 * ff, two)
    at(14)
    out_far = [go("ofa", out_far[:tokens], TO_CORE), go("ofb", out_far[tokens:], TO_CORE)]
    out_side = (out_near[tokens:] + out_far[1].astype(WIDE)).astype(LOW)
    out_side = go("oz", out_side, TO_ZL)
    d_all = [d_low, d_side, d_core, go("df", d_side, TO_CORE)]
    at(15)
    d_attended, out_grad = heads_back(order, d_all, heads, w_out)
    at(16)
    d_mixed = attend_back(order, mix, attended, d_attended, logs, cos_table, sin_table)
    at(17)
    grads = [(d, t * part) for t, d in enumerate(d_mixed)]
    far = go("m1c", back_half(order, grads, one, True)[0], TO_CORE)
    at(18)
    output = resid + out_near[:tokens] + out_far[0].astype(WIDE) + out_side.astype(WIDE)
    output = output.astype(LOW)
    if "out" in TIED:
        wait(order, output)
    output = go("oh", output, TO_HOME)
    near, other = back_half(order, grads, one, False)
    side = (other + far[tokens:].astype(WIDE)).astype(LOW)
    if "side" in TIED:
        wait(order, side)
    side = go("m1z", side, TO_ZL)
    pieces = mixed_grads(order, normed_one, d_mixed, out_grad)
    at(19)
    mixed_terms = [pieces[0]] + [
        go(n, p, pairs)
        for n, p, pairs in zip(("mx", "my", "mxy"), pieces[1:], (TO_X, TO_Y, TO_XY))
    ]
    ff_kept, ff_sent = fold(order, [ff_terms])
    ff_sent = go("fz", ff_sent, TO_ZH)
    at(20)
    if "pull_late" not in TIED:
        (input_grad,) = norm_pull(order, x, (near, far, side), d_resid, False)
    at(21)
    mixed_kept, mixed_sent = fold(order, [t[None] for t in mixed_terms], 128)
    mixed_sent = go("mz", mixed_sent, TO_ZH)
    at(22)
    if "pull_late" in TIED:
        (input_grad,) = norm_pull(order, x, (near, far, side), d_resid, False)
    ff_slices = split_rows(order, ff_kept, ff_sent)
    at(23)
    input_grad = jnp.concatenate(
        [
            go("ih1", input_grad[: tokens // 2], TO_HOME),
            go("ih2", input_grad[tokens // 2 :], TO_HOME),
        ]
    )
    ff_slices = [ff_slices[0]] + [
        go(n, p, pairs)
        for n, p, pairs in zip(("f1", "f2", "f3"), ff_slices[1:], (TO_ZL, TO_CORE, TO_FAR))
    ]
    at(24)
    mixed_slices = split_rows(order, mixed_kept, mixed_sent)
    mixed_slices = [mixed_slices[0]] + [
        go(n, p, pairs)
        for n, p, pairs in zip(("m1", "m2", "m3"), mixed_slices[1:], (TO_ZL, TO_CORE, TO_FAR))
    ]
    at(25)
    up_grad, gain_two_grad, down_grad = finish(
        order, ff_slices, up_weight, gain_two, (2, ff, ff)
    )
    qkv_grad, gain_one_grad, out_grad = finish(
        order, mixed_slices, qkv_weight, gain_one, (3, part, part)
    )
    return (
        output[None],
        input_grad[None],
        gain_one_grad[0],
        qkv_grad,
        out_grad,
        gain_two_grad[0],
        up_grad,
        down_grad,
    )


def solution(mesh):
    dp, seq = "dp", "seq"
    step = per_device
    if tuple(mesh.shape.values()) == QUAD_MESH:
        dp, seq, step = ("y", "x", "c"), ("zh", "zl"), quad_device
        mesh = jax.sharding.Mesh(mesh.devices.reshape(2, 2, 2, 2, 2), FLAT)
        every = FLAT
    else:
        every = (dp, seq)
    rows = P(every, None)
    return jax.shard_map(
        step,
        mesh=mesh,
        in_specs=(
            P(dp, seq, None),
            P(dp, seq),
            P(every),
            rows,
            rows,
            P(every),
            rows,
            rows,
            P(dp, seq, None),
        ),
        out_specs=(
            P(dp, seq, None),
            P(dp, seq, None),
            P(every),
            rows,
            rows,
            P(every),
            rows,
            rows,
        ),
        check_vma=False,
    )
```

```python
import math

import jax
import jax.numpy as jnp
from jax import lax
from jax.experimental import pallas as pl
from jax.experimental.pallas import tpu as pltpu
from jax.sharding import PartitionSpec as P

HEADS = 16
HEAD_DIM = 64
FF = 2624


norm_eps = 1e-05
rope_base = 160000.0
inv_root_two = 0.7071067811865476
inv_root_tau = 0.3989422804014327


def for_sending(array):
    return jax.tree.map(lambda a: a.astype(jnp.bfloat16) if a.dtype == jnp.float32 else a, array)


def normalize(values):
    centre = jnp.mean(values, axis=-1, keepdims=True)
    centred = values - centre
    spread = lax.rsqrt(jnp.mean(centred * centred, axis=-1, keepdims=True) + norm_eps)
    return (centred * spread, spread)


def norm_back(grad_in, normed, spread, gain):
    scaled = grad_in * gain
    gain_term = jnp.sum(grad_in * normed, axis=0)
    centred = (
        scaled
        - jnp.mean(scaled, axis=-1, keepdims=True)
        - normed * jnp.mean(scaled * normed, axis=-1, keepdims=True)
    )
    return (spread * centred, gain_term)


def rope_tables(seq_pos):
    exponent = jnp.arange(0, HEAD_DIM, 2).astype(jnp.float32) / HEAD_DIM
    frequency = rope_base ** (-exponent)
    angles = seq_pos.astype(jnp.float32)[:, None] * frequency[None, :]
    angles = jnp.concatenate([angles, angles], axis=-1)[:, None, :]
    return (jnp.cos(angles), jnp.sin(angles))


def rotate(values, cos_table, sin_table):
    half_dim = values.shape[-1] // 2
    turned = jnp.concatenate([-values[..., half_dim:], values[..., :half_dim]], axis=-1)
    return values * cos_table + turned * sin_table


def rotate_back(grads, cos_table, sin_table):
    half_dim = grads.shape[-1] // 2
    weighted = grads * sin_table
    turned = jnp.concatenate([weighted[..., half_dim:], -weighted[..., :half_dim]], axis=-1)
    return grads * cos_table + turned


def gelu_parts(inner_act):
    normal_cdf = 0.5 * (1.0 + jax.scipy.special.erf(inner_act * inv_root_two))
    slope = normal_cdf + inner_act * jnp.exp(-0.5 * inner_act * inner_act) * inv_root_tau
    return (inner_act * normal_cdf, slope)


def project_heads(attn_in, w_qkv, cos_table, sin_table):
    token_count, model_width = attn_in.shape
    mixed_rows = jnp.dot(attn_in, w_qkv, preferred_element_type=jnp.float32)
    shaped = (token_count, HEADS, HEAD_DIM)
    queries = rotate(mixed_rows[:, :model_width].reshape(shaped), cos_table, sin_table)
    key_rows = rotate(
        mixed_rows[:, model_width : 2 * model_width].reshape(shaped), cos_table, sin_table
    )
    queries = queries.reshape(token_count, model_width).astype(jnp.bfloat16)
    key_rows = key_rows.reshape(token_count, model_width).astype(jnp.bfloat16)
    values = mixed_rows[:, 2 * model_width :].astype(jnp.bfloat16)
    return (queries, key_rows, values)


def attend_forward(q_heads, k_heads, v_heads):
    seq_len, columns = q_heads.shape
    head_count = columns // HEAD_DIM
    block_rows = min(512, seq_len)
    block_count = seq_len // block_rows
    score_scale = HEAD_DIM ** (-0.5)
    k_all = k_heads.reshape(seq_len, head_count, HEAD_DIM)
    v_all = v_heads.reshape(seq_len, head_count, HEAD_DIM)

    def one_block(q_block):
        scores = (
            jnp.einsum("qhd,khd->hqk", q_block, k_all, preferred_element_type=jnp.float32)
            * score_scale
        )
        row_peak = jnp.max(scores, axis=-1, keepdims=True)
        exp_scores = jnp.exp(scores - row_peak)
        totals = jnp.sum(exp_scores, axis=-1, keepdims=True)
        prob_rows = (exp_scores / totals).astype(jnp.bfloat16)
        attended = jnp.einsum("hqk,khd->qhd", prob_rows, v_all, preferred_element_type=jnp.float32)
        return (attended.astype(jnp.bfloat16), row_peak[..., 0] + jnp.log(totals[..., 0]))

    attended, log_totals = lax.map(
        one_block, q_heads.reshape(block_count, block_rows, head_count, HEAD_DIM)
    )
    return (attended.reshape(seq_len, columns), log_totals)


def attend_backward(q_heads, k_heads, v_heads, d_heads, log_totals):
    seq_len, columns = q_heads.shape
    head_count = columns // HEAD_DIM
    block_rows = min(512, seq_len)
    block_count = seq_len // block_rows
    score_scale = HEAD_DIM ** (-0.5)
    k_all = k_heads.reshape(seq_len, head_count, HEAD_DIM)
    v_all = v_heads.reshape(seq_len, head_count, HEAD_DIM)
    q_blocks = q_heads.reshape(block_count, block_rows, head_count, HEAD_DIM)
    d_blocks = d_heads.reshape(block_count, block_rows, head_count, HEAD_DIM)

    def one_block(carry, item):
        key_acc, value_acc = carry
        q_block, d_block, lse_block = item
        scores = (
            jnp.einsum("qhd,khd->hqk", q_block, k_all, preferred_element_type=jnp.float32)
            * score_scale
        )
        prob_rows = jnp.exp(scores - lse_block[..., None])
        value_acc = value_acc + jnp.einsum(
            "hqk,qhd->khd",
            prob_rows.astype(jnp.bfloat16),
            d_block,
            preferred_element_type=jnp.float32,
        )
        d_probs = jnp.einsum("qhd,khd->hqk", d_block, v_all, preferred_element_type=jnp.float32)
        d_scores = (
            prob_rows * (d_probs - jnp.sum(prob_rows * d_probs, axis=-1, keepdims=True))
        ).astype(jnp.bfloat16)
        d_query = (
            jnp.einsum("hqk,khd->qhd", d_scores, k_all, preferred_element_type=jnp.float32)
            * score_scale
        )
        key_acc = (
            key_acc
            + jnp.einsum("hqk,qhd->khd", d_scores, q_block, preferred_element_type=jnp.float32)
            * score_scale
        )
        return ((key_acc, value_acc), d_query.astype(jnp.bfloat16))

    empty_acc = jnp.zeros((seq_len, head_count, HEAD_DIM), jnp.float32)
    (key_acc, value_acc), d_query = lax.scan(
        one_block, (empty_acc, empty_acc), (q_blocks, d_blocks, log_totals)
    )
    d_q = d_query.reshape(seq_len, columns)
    d_k = key_acc.astype(jnp.bfloat16).reshape(seq_len, columns)
    d_v = value_acc.astype(jnp.bfloat16).reshape(seq_len, columns)
    return (d_q, d_k, d_v)


def add_sources(received):
    return tuple((jnp.sum(piece, axis=0) for piece in received))


def per_device(
    inputs,
    positions,
    attn_gain,
    qkv_weight,
    attn_out_weight,
    mlp_gain,
    up_weight,
    down_weight,
    cotangent,
):
    layer = (
        lax.all_gather(attn_gain, ("dp", "seq"), axis=0, tiled=True),
        lax.all_gather(qkv_weight, ("dp", "seq"), axis=0, tiled=True),
        lax.all_gather(attn_out_weight, ("dp", "seq"), axis=0, tiled=True),
        lax.all_gather(mlp_gain, ("dp", "seq"), axis=0, tiled=True),
        lax.all_gather(up_weight, ("dp", "seq"), axis=0, tiled=True),
        lax.all_gather(down_weight, ("dp", "seq"), axis=0, tiled=True),
    )
    gain_one, w_qkv, w_out, gain_two, w_up, w_down = layer
    token_count = inputs.shape[1]
    resid_in = inputs[0].astype(jnp.float32)
    cos_table, sin_table = rope_tables(positions[0])
    normed_one, spread_one = normalize(resid_in)
    attn_in = (normed_one * gain_one.astype(jnp.float32)).astype(jnp.bfloat16)
    queries, key_rows, values = project_heads(attn_in, w_qkv, cos_table, sin_table)
    q_heads, k_heads, v_heads = (
        lax.all_to_all(queries, "seq", split_axis=1, concat_axis=0, tiled=True),
        lax.all_to_all(key_rows, "seq", split_axis=1, concat_axis=0, tiled=True),
        lax.all_to_all(values, "seq", split_axis=1, concat_axis=0, tiled=True),
    )
    attended_heads, log_totals = attend_forward(q_heads, k_heads, v_heads)
    attended = lax.all_to_all(attended_heads, "seq", split_axis=0, concat_axis=1, tiled=True)
    resid = resid_in + jnp.dot(attended, w_out, preferred_element_type=jnp.float32)
    normed_two, spread_two = normalize(resid)
    mlp_in = (normed_two * gain_two.astype(jnp.float32)).astype(jnp.bfloat16)
    up_rows = jnp.dot(mlp_in, w_up, preferred_element_type=jnp.float32)
    inner_act = up_rows[:, :FF]
    gate_act = up_rows[:, FF:]
    gelu_val, gelu_slope = gelu_parts(inner_act)
    hidden = (gelu_val * gate_act).astype(jnp.bfloat16)
    output = resid + jnp.einsum("tf,df->td", hidden, w_down, preferred_element_type=jnp.float32)
    layer_back = (
        lax.all_gather(attn_gain, ("dp", "seq"), axis=0, tiled=True),
        lax.all_gather(qkv_weight, ("dp", "seq"), axis=0, tiled=True),
        lax.all_gather(attn_out_weight, ("dp", "seq"), axis=0, tiled=True),
        lax.all_gather(mlp_gain, ("dp", "seq"), axis=0, tiled=True),
        lax.all_gather(up_weight, ("dp", "seq"), axis=0, tiled=True),
        lax.all_gather(down_weight, ("dp", "seq"), axis=0, tiled=True),
    )
    gain_one, w_qkv, w_out, gain_two, w_up, w_down = layer_back
    d_out = cotangent[0]
    down_grad = jnp.einsum("td,tf->df", d_out, hidden, preferred_element_type=jnp.float32)
    d_hidden = jnp.dot(d_out, w_down, preferred_element_type=jnp.float32)
    d_up = jnp.concatenate([d_hidden * gate_act * gelu_slope, d_hidden * gelu_val], axis=1).astype(
        jnp.bfloat16
    )
    up_grad = jnp.einsum("tk,tn->kn", mlp_in, d_up, preferred_element_type=jnp.float32)
    d_mlp_in = jnp.einsum("tn,kn->tk", d_up, w_up, preferred_element_type=jnp.float32)
    d_norm_two, gain_two_grad = norm_back(
        d_mlp_in, normed_two, spread_two, gain_two.astype(jnp.float32)
    )
    d_resid = d_out.astype(jnp.float32) + d_norm_two
    d_resid_low = d_resid.astype(jnp.bfloat16)
    out_grad = jnp.einsum("tk,tn->kn", attended, d_resid_low, preferred_element_type=jnp.float32)
    d_attended = jnp.einsum(
        "tn,kn->tk", d_resid_low, w_out, preferred_element_type=jnp.float32
    ).astype(jnp.bfloat16)
    d_heads = lax.all_to_all(d_attended, "seq", split_axis=1, concat_axis=0, tiled=True)
    queries, key_rows, values = project_heads(attn_in, w_qkv, cos_table, sin_table)
    head_inputs = (
        lax.all_to_all(queries, "seq", split_axis=1, concat_axis=0, tiled=True),
        lax.all_to_all(key_rows, "seq", split_axis=1, concat_axis=0, tiled=True),
        lax.all_to_all(values, "seq", split_axis=1, concat_axis=0, tiled=True),
    )
    d_q, d_k, d_v = attend_backward(
        head_inputs[0], head_inputs[1], head_inputs[2], d_heads, log_totals
    )
    dq_rows, dk_rows, dv_rows = (
        lax.all_to_all(d_q, "seq", split_axis=0, concat_axis=1, tiled=True),
        lax.all_to_all(d_k, "seq", split_axis=0, concat_axis=1, tiled=True),
        lax.all_to_all(d_v, "seq", split_axis=0, concat_axis=1, tiled=True),
    )
    shaped = (token_count, HEADS, HEAD_DIM)
    dq_pre = rotate_back(dq_rows.astype(jnp.float32).reshape(shaped), cos_table, sin_table).reshape(
        token_count, -1
    )
    dk_pre = rotate_back(dk_rows.astype(jnp.float32).reshape(shaped), cos_table, sin_table).reshape(
        token_count, -1
    )
    d_mixed = jnp.concatenate(
        [dq_pre.astype(jnp.bfloat16), dk_pre.astype(jnp.bfloat16), dv_rows], axis=1
    )
    qkv_grad = jnp.einsum("tk,tn->kn", attn_in, d_mixed, preferred_element_type=jnp.float32)
    d_attn_in = jnp.einsum("tn,kn->tk", d_mixed, w_qkv, preferred_element_type=jnp.float32)
    d_norm_one, gain_one_grad = norm_back(
        d_attn_in, normed_one, spread_one, gain_one.astype(jnp.float32)
    )
    input_grad = (d_resid + d_norm_one).astype(jnp.bfloat16)
    all_sent = (
        lax.all_to_all(
            gain_one_grad[None].astype(jnp.bfloat16), "dp", split_axis=1, concat_axis=0, tiled=True
        ).astype(jnp.float32),
        lax.all_to_all(
            qkv_grad[None].astype(jnp.bfloat16), "dp", split_axis=1, concat_axis=0, tiled=True
        ).astype(jnp.float32),
        lax.all_to_all(
            out_grad[None].astype(jnp.bfloat16), "dp", split_axis=1, concat_axis=0, tiled=True
        ).astype(jnp.float32),
        lax.all_to_all(
            gain_two_grad[None].astype(jnp.bfloat16), "dp", split_axis=1, concat_axis=0, tiled=True
        ).astype(jnp.float32),
        lax.all_to_all(
            up_grad[None].astype(jnp.bfloat16), "dp", split_axis=1, concat_axis=0, tiled=True
        ).astype(jnp.float32),
        lax.all_to_all(
            down_grad[None].astype(jnp.bfloat16), "dp", split_axis=1, concat_axis=0, tiled=True
        ).astype(jnp.float32),
    )
    grads = jax.tree.map(
        lambda part: part.astype(jnp.float32),
        lax.psum_scatter(
            for_sending(add_sources(all_sent)), "seq", scatter_dimension=0, tiled=True
        ),
    )
    return (
        output.astype(jnp.bfloat16)[None],
        input_grad[None],
        grads[0],
        grads[1],
        grads[2],
        grads[3],
        grads[4],
        grads[5],
    )


QUAD_MESH = (8, 4)
FLAT = ("y", "x", "c", "zh", "zl")
LOW, WIDE = jnp.bfloat16, jnp.float32


def pairs_of(step):
    found = []
    for dp in range(8):
        for seq in range(4):
            place = (dp // 4, dp // 2 % 2, dp % 2, seq // 2, seq % 2)
            target = step(*place)
            if target is not None:
                y, x, c, zh, zl = target
                found.append((dp * 4 + seq, (4 * y + 2 * x + c) * 4 + 2 * zh + zl))
    return found


TO_X = pairs_of(lambda y, x, c, zh, zl: (y, 1 - x, c, zh, zl))
TO_Y = pairs_of(lambda y, x, c, zh, zl: (1 - y, x, c, zh, zl))
TO_XY = pairs_of(lambda y, x, c, zh, zl: (1 - y, 1 - x, c, zh, zl))
TO_CORE = pairs_of(lambda y, x, c, zh, zl: (y, x, 1 - c, zh, zl))
TO_ZH = pairs_of(lambda y, x, c, zh, zl: (y, x, c, 1 - zh, zl))
TO_ZL = pairs_of(lambda y, x, c, zh, zl: (y, x, c, zh, 1 - zl))
TO_FAR = pairs_of(lambda y, x, c, zh, zl: (y, x, 1 - c, zh, 1 - zl))
TO_HOME = pairs_of(lambda y, x, c, zh, zl: (y, x, zh, c, zl))
ENTER = pairs_of(
    lambda y, x, c, zh, zl: (y, x, c, zh, 1 - zl) if c == zh else (y, x, zh, c, zl)
)
ENTER_MOVED = pairs_of(lambda y, x, c, zh, zl: None if c == zh else (y, x, c, zh, 1 - zl))


class Order(list):
    pass


def send(array, pairs):
    return lax.ppermute(array, FLAT, pairs)


def after(order, array):
    return lax.optimization_barrier((array, order[0]))[0]


def wait(order, *arrays):
    order[0] = lax.optimization_barrier((order[0], *arrays))[0]


def lanes(size):
    return -(-size // 128) * 128


def core_of(flat):
    return flat >> 2 & 1


def half_of(flat):
    return flat >> 1 & 1


def group_of(flat):
    return 2 * core_of(flat) + (flat & 1)


def square_of(flat):
    return flat >> 3


def mm(left, right):
    return lax.dot_general(left, right, (((1,), (0,)), ((), ())), preferred_element_type=WIDE)


def mm_t(left, right):
    return lax.dot_general(left, right, (((1,), (1,)), ((), ())), preferred_element_type=WIDE)


def t_mm(left, right):
    return lax.dot_general(left, right, (((0,), (0,)), ((), ())), preferred_element_type=WIDE)


def window(index, size):
    return pl.ds(pl.multiple_of(index * size, size), size)


def whole(array):
    rank = len(array.shape)
    return (array, array.shape, lambda *_: (0,) * rank)


def by_rows(array, rows, step=lambda b: b):
    return (array, (rows,) + array.shape[1:], lambda b, f: (step(b),) + (0,) * (len(array.shape) - 1))


def run(body, order, grid, ins, outs, scratch=(), flops=0, spare=6 * 2**20, far=()):
    moved = sum(a.size * a.dtype.itemsize for a, _, _ in ins)
    moved += sum(a.size * a.dtype.itemsize for a, _, _ in outs)
    def held(block, dtype, count):
        return count * math.prod(block) * jnp.dtype(dtype).itemsize

    grant = sum(
        held(block, a.dtype, 1 if tuple(block) == tuple(a.shape) else 2)
        for a, block, _ in (*ins, *outs)
    )
    grant += sum(held(m.shape, m.dtype, 1) for m in scratch) + spare
    made = pl.pallas_call(
        body,
        grid_spec=pltpu.PrefetchScalarGridSpec(
            num_scalar_prefetch=1,
            grid=grid,
            in_specs=[pl.BlockSpec(block, index) for _, block, index in ins],
            out_specs=[pl.BlockSpec(block, index) for _, block, index in outs],
            scratch_shapes=list(scratch),
        ),
        out_shape=[
            pltpu.HBM(a.shape, a.dtype) if i in far else a for i, (a, _, _) in enumerate(outs)
        ],
        compiler_params=pltpu.CompilerParams(vmem_limit_bytes=grant),
        cost_estimate=pl.CostEstimate(flops=flops // 100, bytes_accessed=moved // 100, transcendentals=0),
    )(order[0], *[a for a, _, _ in ins])
    order[0], _ = lax.optimization_barrier((order[0], made[0]))
    return made


def spans(pieces):
    rows = pieces[0].shape[0]
    return [(0, 0, rows), (1, 0, rows), (2, 0, rows), (3, 0, rows // 2), (3, rows // 2, rows // 2)]


def rows_of(ref, span):
    count = span[2]
    return slice(ref.shape[0] - count, None) if span[1] else slice(0, count)


def span_of(square, span, rows):
    index, first, count = span
    return pl.ds(pl.multiple_of((square ^ index) * rows + first, count), count)


def shape_of(*dims, dtype=LOW):
    return jax.ShapeDtypeStruct(dims, dtype)


def column_of(row):
    size = row.shape[1]
    down = lax.broadcasted_iota(jnp.int32, (size, size), 0)
    across = lax.broadcasted_iota(jnp.int32, (size, size), 1)
    return jnp.sum(jnp.where(down == across, row, 0.0), axis=1, keepdims=True)


def row_of(column):
    size = column.shape[0]
    down = lax.broadcasted_iota(jnp.int32, (size, size), 0)
    across = lax.broadcasted_iota(jnp.int32, (size, size), 1)
    return jnp.sum(jnp.where(down == across, column, 0.0), axis=0, keepdims=True)


def normed_of(x):
    centred = x - jnp.mean(x, axis=-1, keepdims=True)
    spread = lax.rsqrt(jnp.mean(centred * centred, axis=-1, keepdims=True) + norm_eps)
    return centred * spread, spread


def split_slices(order, scaled, plain, gain, parts):
    rows, part, rest = scaled.shape[0], scaled.shape[1] // (4 * parts), plain.shape[1] // 4
    out = shape_of(2, rows, lanes(parts * part + rest))

    def body(flat_ref, scaled_ref, plain_ref, gain_ref, own_ref, sent_ref, held):
        scale = column_of(gain_ref[...].astype(WIDE))
        for s in range(4):
            for t in range(parts):
                cols = scaled_ref[:, (4 * t + s) * part : (4 * t + s + 1) * part].astype(WIDE)
                held[s, :, t * part : (t + 1) * part] = (cols * scale).astype(LOW)
            held[s, :, parts * part : parts * part + rest] = plain_ref[
                :, s * rest : (s + 1) * rest
            ]
        core = core_of(flat_ref[0])
        for zl in range(2):
            own_ref[zl] = held[2 * core + zl]
            sent_ref[zl] = held[2 * (1 - core) + zl]

    return run(
        body, order, (1,), [whole(a) for a in (scaled, plain, gain)], [whole(out)] * 2,
        [pltpu.VMEM((4, *out.shape[1:]), LOW)],
    )


def chip_rows(order, own, received):
    def body(flat_ref, own_ref, received_ref, kept_ref, sent_ref):
        core, chip = core_of(flat_ref[0]), flat_ref[0] & 1
        kept_ref[core] = own_ref[chip]
        kept_ref[1 - core] = received_ref[chip]
        sent_ref[core] = own_ref[1 - chip]
        sent_ref[1 - core] = received_ref[1 - chip]

    return run(
        body, order, (1,), [whole(own), whole(received)], [whole(shape_of(*own.shape))] * 2
    )


def quad_rows(order, own, received):
    _, rows, width = own.shape

    def body(flat_ref, own_ref, received_ref, out_ref):
        chip = flat_ref[0] & 1
        for c in range(2):
            out_ref[2 * c + chip] = own_ref[c]
            out_ref[2 * c + 1 - chip] = received_ref[c]

    return run(
        body, order, (1,), [whole(own), whole(received)], [whole(shape_of(4, rows, width))]
    )[0]


def line_rows(order, near, far):
    _, rows, width = near.shape
    near = near.reshape(2, 2 * rows, width)
    far = far.reshape(2, 2 * rows, width)

    def body(flat_ref, near_ref, far_ref, out_ref):
        half = half_of(flat_ref[0])
        for c in range(2):
            out_ref[c, half] = near_ref[c]
            out_ref[c, 1 - half] = far_ref[c]

    out = run(
        body, order, (1,), [whole(near), whole(far)], [whole(shape_of(2, 2, 2 * rows, width))]
    )[0]
    return out.reshape(8 * rows, width)


def join_tokens(order, parts, rows, extra=0):
    width = parts[0].shape[1]

    def body(flat_ref, block, first, second, core_block, core_first, core_second, *outs):
        home = core_of(flat_ref[0]) == half_of(flat_ref[0])
        here = (block, first, core_first, core_second)
        moved = (first, second, core_block, core_first)
        for k in range(4):
            for flag, source in ((home, here[k]), (jnp.logical_not(home), moved[k])):

                @pl.when(jnp.logical_and(pl.program_id(0) == k, flag))
                def _(source=source):
                    def step(r, carry):
                        outs[0][window(r, 32), :] = source[window(r, 32), :]
                        return carry

                    lax.fori_loop(0, rows // 32, step, 0)
                    if extra:
                        outs[1][...] = source[rows : rows + extra, :]

    made = [shape_of(4 * rows, width)] + ([shape_of(4 * extra, width)] if extra else [])
    return run(
        body, order, (4,), [whole(a) for a in parts],
        [by_rows(m, m.shape[0] // 4) for m in made],
    )


def rope_lanes(seq_pos):
    exponent = jnp.arange(0, HEAD_DIM, 2).astype(WIDE) / HEAD_DIM
    angles = seq_pos[:, None] * (rope_base ** (-exponent))[None, :]
    cos_half, sin_half = jnp.cos(angles), jnp.sin(angles)
    return (
        jnp.concatenate([cos_half] * 4, axis=1),
        jnp.concatenate([-sin_half, sin_half] * 2, axis=1),
    )


def turned(v):
    half = HEAD_DIM // 2
    lane = lax.broadcasted_iota(jnp.int32, v.shape, 1)
    return jnp.where(
        lane % HEAD_DIM < half, pltpu.roll(v, 2 * HEAD_DIM - half, 1), pltpu.roll(v, half, 1)
    )


def project(order, x, pieces, cos_table, sin_table):
    tokens, width = x.shape
    piece, columns = pieces[0].shape[0], 3 * width // 4
    rows = tokens // 4

    def body(flat_ref, x_ref, *refs):
        weights, (cos_ref, sin_ref, n_ref, mix_ref) = refs[:5], refs[5:]
        n_ref[...] = normed_of(x_ref[...].astype(WIDE))[0].astype(LOW)
        square = square_of(flat_ref[0])
        mixed = sum(
            mm(n_ref[:, span_of(square, span, piece)], w[rows_of(w, span), :columns])
            for span, w in zip(spans(pieces), weights)
        )
        turned_to = 2 * columns // 3
        for t in range(0, turned_to, 128):
            v = mixed[:, t : t + 128]
            mix_ref[:, t : t + 128] = (v * cos_ref[...] + turned(v) * sin_ref[...]).astype(LOW)
        mix_ref[:, turned_to:] = mixed[:, turned_to:].astype(LOW)

    return run(
        body, order, (4,),
        [by_rows(x, rows)] + [whole(p) for p in pieces]
        + [by_rows(cos_table, rows), by_rows(sin_table, rows)],
        [by_rows(shape_of(tokens, width), rows), by_rows(shape_of(tokens, columns), rows)],
        flops=2 * tokens * width * columns,
        far=(0,),
    )


def attend(order, mix):
    tokens, columns = mix.shape
    part = columns // 3
    rows = tokens // 4
    scale = HEAD_DIM ** (-0.5)

    def body(flat_ref, q_ref, k_ref, v_ref, out_ref, log_ref):
        lane = lax.broadcasted_iota(jnp.int32, (rows, part), 1) // HEAD_DIM
        total = jnp.zeros((rows, part), WIDE)
        queries = q_ref[...].astype(WIDE) * scale
        for h in range(part // HEAD_DIM):
            q_head = jnp.where(lane == h, queries, 0.0).astype(LOW)
            scores = mm_t(q_head, k_ref[...])
            peak = jnp.max(scores, axis=-1, keepdims=True)
            powers = jnp.exp(scores - peak)
            mass = jnp.sum(powers, axis=-1, keepdims=True)
            probs = (powers * (1.0 / mass)).astype(LOW)
            total = jnp.where(lane == h, mm(probs, v_ref[...]), total)
            log_ref[h : h + 1, :] = row_of(peak + jnp.log(mass))
        out_ref[...] = total.astype(LOW)

    return run(
        body, order, (4,),
        [
            (mix, (rows, part), lambda b, f: (b, 0)),
            (mix, (tokens, part), lambda b, f: (0, 1)),
            (mix, (tokens, part), lambda b, f: (0, 2)),
        ],
        [
            by_rows(shape_of(tokens, part), rows),
            (shape_of(8, tokens, dtype=WIDE), (8, rows), lambda b, f: (0, b)),
        ],
        flops=16 * tokens * tokens * part,
    )


def token_parts(arrays, rows):
    return [by_rows(a, rows, lambda b, i=i: b ^ i) for i, a in enumerate(arrays)]


def join_heads(order, x, heads, columns):
    tokens, width = x.shape
    rows, part = tokens // 4, width // 4

    def body(flat_ref, x_ref, *refs):
        parts, weights, (n_ref, own_ref, held) = refs[:4], refs[4:8], refs[8:]
        group, square = group_of(flat_ref[0]), square_of(flat_ref[0])
        for j in range(4):
            cols = window(group ^ j, part)
            held[:, cols] = x_ref[:, cols].astype(WIDE) + sum(
                mm(parts[i][...], weights[j][window(group ^ i ^ square, part), :])
                for i in range(4)
            )
        resid = held[...]
        n_ref[...] = normed_of(resid)[0].astype(LOW)

        @pl.when(pl.program_id(0) == 0)
        def _():
            own_ref[...] = held[...]

    return run(
        body, order, (4,),
        [by_rows(x, rows)] + token_parts(heads, rows) + [whole(w) for w in columns],
        [by_rows(shape_of(tokens, width), rows), whole(shape_of(rows, width, dtype=WIDE))],
        [pltpu.VMEM((rows, width), WIDE)],
        flops=2 * tokens * width * width,
    )


def feed(order, normed, cot, pieces):
    tokens, width = normed.shape
    piece, ff = pieces[0].shape[0], FF // 4
    rows = tokens // 4

    def body(flat_ref, n_ref, cot_ref, *refs):
        weights, (h_ref, d_ref) = refs[:5], refs[5:]
        square = square_of(flat_ref[0])
        cut = [
            (span_of(square, span, piece), rows_of(w, span), w)
            for span, w in zip(spans(pieces), weights)
        ]
        wide = sum(mm(n_ref[:, at], w[of, : 2 * ff]) for at, of, w in cut)
        d_hidden = sum(mm(cot_ref[:, at], w[of, 2 * ff : 3 * ff]) for at, of, w in cut)
        inner, gate = wide[:, :ff], wide[:, ff:]
        cdf = 0.5 * (1.0 + lax.erf(inner * inv_root_two))
        slope = cdf + inner * jnp.exp(-0.5 * inner * inner) * inv_root_tau
        bent = inner * cdf
        h_ref[...] = (bent * gate).astype(LOW)
        d_ref[:, :ff] = (d_hidden * gate * slope).astype(LOW)
        d_ref[:, ff:] = (d_hidden * bent).astype(LOW)

    return run(
        body, order, (4,),
        [by_rows(normed, rows), by_rows(cot, rows)] + [whole(w) for w in pieces],
        [by_rows(shape_of(tokens, ff), rows), by_rows(shape_of(tokens, 2 * ff), rows)],
        flops=6 * tokens * width * ff,
    )


def back_half(order, grads, pieces, far):
    tokens = grads[0][0].shape[0]
    piece = pieces[0].shape[0]
    rows, width, count = tokens // 2, 4 * piece, len(grads)
    outs = [shape_of(rows, width)] if far else [shape_of(rows // 2, width, dtype=WIDE)] * 2

    def body(flat_ref, *refs):
        arrays, weights, out_refs = refs[:count], refs[count : count + 5], refs[count + 5 :]
        square = square_of(flat_ref[0])
        for span, w in zip(spans(pieces), weights):
            total = sum(
                mm_t(a[...], w[rows_of(w, span), at : at + a.shape[1]])
                for a, (_, at) in zip(arrays, grads)
            )
            for k, ref in enumerate(out_refs):
                part = total[k * ref.shape[0] : (k + 1) * ref.shape[0]]
                ref[:, span_of(square, span, piece)] = part.astype(ref.dtype)

    return run(
        body, order, (1,),
        [by_rows(a, rows, lambda b: int(far)) for a, _ in grads] + [whole(p) for p in pieces],
        [whole(out) for out in outs],
        flops=tokens * width * sum(a.shape[1] for a, _ in grads),
    )


def back_both(order, grad, first, pieces):
    tokens = grad.shape[0]
    piece = pieces[0].shape[0]
    rows, width, columns = tokens // 2, 4 * piece, grad.shape[1]

    def body(flat_ref, grad_ref, *refs):
        weights, (far_ref, own_ref, other_ref) = refs[:5], refs[5:]
        square = square_of(flat_ref[0])
        for span, w in zip(spans(pieces), weights):
            total = mm_t(grad_ref[...], w[rows_of(w, span), first : first + columns])
            own_ref[:, span_of(square, span, piece)] = total[: rows // 2]
            other_ref[:, span_of(square, span, piece)] = total[rows // 2 : rows]
            far_ref[:, span_of(square, span, piece)] = total[rows:].astype(LOW)

    return run(
        body, order, (1,), [whole(grad)] + [whole(p) for p in pieces],
        [whole(shape_of(rows, width))] + [whole(shape_of(rows // 2, width, dtype=WIDE))] * 2,
        flops=2 * tokens * width * columns,
    )


def norm_pull(order, x, terms, base, keep):
    rows, width = base.shape
    step = rows // 4

    def body(flat_ref, x_ref, a_ref, b_ref, c_ref, base_ref, *outs):
        normed, spread = normed_of(x_ref[...].astype(WIDE))
        scaled = a_ref[...] + b_ref[...].astype(WIDE) + c_ref[...].astype(WIDE)
        grad = base_ref[...].astype(WIDE) + spread * (
            scaled
            - jnp.mean(scaled, axis=-1, keepdims=True)
            - normed * jnp.mean(scaled * normed, axis=-1, keepdims=True)
        )
        outs[0][...] = grad.astype(LOW)
        if keep:
            outs[1][...] = grad

    low = shape_of(rows + 16 if keep else rows, width)
    outs = [low] + ([shape_of(rows, width, dtype=WIDE)] if keep else [])
    return run(
        body, order, (4,), [by_rows(a, step) for a in (x, *terms, base)],
        [by_rows(o, step) for o in outs],
    )


def feed_grads(order, normed, cot, d_up, hidden):
    tokens, width = normed.shape
    piece, ff = width // 4, hidden.shape[1]
    out = shape_of(4, piece, lanes(3 * ff))

    def body(flat_ref, n_ref, cot_ref, d_ref, h_ref, out_ref):
        out_ref[0, :, : 2 * ff] = t_mm(n_ref[...], d_ref[...]).astype(LOW)
        out_ref[0, :, 2 * ff : 3 * ff] = t_mm(cot_ref[...], h_ref[...]).astype(LOW)

    return run(
        body, order, (4,),
        [(a, (tokens, piece), lambda b, f: (0, b)) for a in (normed, cot)]
        + [whole(d_up), whole(hidden)],
        [by_rows(out, 1)],
        flops=6 * tokens * width * ff,
        far=(0,),
    )[0]


def heads_back(order, d_all, heads, columns):
    rows, width = heads[0].shape[0] // 4, d_all[0].shape[1]
    part = width // 4

    def body(flat_ref, *refs):
        blocks, parts, weights = refs[:4], refs[4:8], refs[8:12]
        d_ref, grad_ref, block, held, total = refs[12:]
        group, square = group_of(flat_ref[0]), square_of(flat_ref[0])
        at = pl.program_id(0)
        for k in range(4):

            @pl.when(at == k)
            def _(source=blocks[k]):
                def step(r, carry):
                    block[window(r, 32), :] = source[window(r, 32), :]
                    return carry

                lax.fori_loop(0, rows // 32, step, 0)

            held[k] = parts[k][...]

        @pl.when(at == 0)
        def _():
            total[...] = jnp.zeros_like(total)

        d_ref[...] = sum(
            mm_t(block[:, window(group ^ j, part)], weights[j][window(group ^ square, part), :])
            for j in range(4)
        ).astype(LOW)
        mine = block[:, window(group, part)]
        for i in range(4):
            total[i] += t_mm(held[group ^ square ^ i], mine)

        @pl.when(at == 3)
        def _():
            grad_ref[...] = total[...].astype(LOW)

    return run(
        body, order, (4,),
        [whole(d) for d in d_all] + token_parts(heads, rows) + [whole(w) for w in columns],
        [by_rows(shape_of(4 * rows, part), rows), whole(shape_of(4, part, part))],
        [
            pltpu.VMEM((rows, width), LOW),
            pltpu.VMEM((4, rows, part), LOW),
            pltpu.VMEM((4, part, part), WIDE),
        ],
        flops=4 * 4 * rows * width * part,
    )


def attend_back(order, mix, attended, d_attended, logs, cos_table, sin_table):
    tokens, columns = mix.shape
    part = columns // 3
    rows = tokens // 4
    scale = HEAD_DIM ** (-0.5)
    heads = part // HEAD_DIM

    def rotated(grad, cos, sin):
        halves = [grad[:, t : t + 128] for t in range(0, part, 128)]
        return jnp.concatenate([v * cos - turned(v) * sin for v in halves], axis=1).astype(LOW)

    def body(flat_ref, q_ref, k_ref, v_ref, o_ref, d_ref, log_ref, cos_ref, sin_ref, *refs):
        dq_ref, dk_ref, dv_ref, k_total, v_total = refs
        at = pl.program_id(0)

        @pl.when(at == 0)
        def _():
            k_total[...] = jnp.zeros_like(k_total)
            v_total[...] = jnp.zeros_like(v_total)

        lane = lax.broadcasted_iota(jnp.int32, (rows, part), 1) // HEAD_DIM
        queries = q_ref[...].astype(WIDE) * scale
        grads = d_ref[...].astype(WIDE)
        chosen = lax.broadcasted_iota(jnp.int32, (8, part), 0) == (
            lax.broadcasted_iota(jnp.int32, (8, part), 1) // HEAD_DIM
        )
        deltas = lax.dot_general(
            chosen.astype(WIDE), grads * o_ref[...].astype(WIDE), (((1,), (1,)), ((), ())),
            precision=lax.Precision.HIGHEST, preferred_element_type=WIDE,
        )
        d_query = jnp.zeros((rows, part), WIDE)
        for h in range(heads):
            q_head = jnp.where(lane == h, queries, 0.0).astype(LOW)
            d_head = jnp.where(lane == h, grads, 0.0).astype(LOW)
            probs = jnp.exp(mm_t(k_ref[...], q_head) - log_ref[h : h + 1, :])
            d_probs = mm_t(v_ref[...], d_head)
            d_scores = (probs * (d_probs - deltas[h : h + 1, :])).astype(LOW)
            v_total[...] += mm(probs.astype(LOW), d_head)
            k_total[...] += mm(d_scores, q_head)
            d_query = jnp.where(lane == h, t_mm(d_scores, k_ref[...]), d_query)
        here = window(at, rows)
        dq_ref[...] = rotated(d_query * scale, cos_ref[here, :], sin_ref[here, :])

        @pl.when(at == 3)
        def _():
            dk_ref[...] = rotated(k_total[...], cos_ref[...], sin_ref[...])
            dv_ref[...] = v_total[...].astype(LOW)

    out = shape_of(tokens, part)
    return run(
        body, order, (4,),
        [
            (mix, (rows, part), lambda b, f: (b, 0)),
            (mix, (tokens, part), lambda b, f: (0, 1)),
            (mix, (tokens, part), lambda b, f: (0, 2)),
            by_rows(attended, rows),
            by_rows(d_attended, rows),
            (logs, (8, rows), lambda b, f: (0, b)),
            whole(cos_table),
            whole(sin_table),
        ],
        [by_rows(out, rows), whole(out), whole(out)],
        [pltpu.VMEM((tokens, part), WIDE)] * 2,
        flops=40 * tokens * tokens * part,
    )


def mixed_grads(order, normed, d_mixed, out_grad):
    tokens, width = normed.shape
    rows, piece = tokens // 4, width // 4
    part = d_mixed[0].shape[1]

    def body(flat_ref, n_ref, *refs):
        grads, out_ref, outs, held = refs[:3], refs[3], refs[4:8], refs[8]
        square = square_of(flat_ref[0])

        @pl.when(pl.program_id(0) == 0)
        def _():
            held[...] = jnp.zeros_like(held)

        for i in range(4):
            cols = n_ref[:, window(square ^ i, piece)]
            for t in range(3):
                held[i, :, t * part : (t + 1) * part] += t_mm(cols, grads[t][...])

        @pl.when(pl.program_id(0) == 3)
        def _():
            for i in range(4):
                outs[i][:, : 3 * part] = held[i].astype(LOW)
                outs[i][:, 3 * part :] = out_ref[i]

    return run(
        body, order, (4,),
        [by_rows(normed, rows)] + [by_rows(d, rows) for d in d_mixed] + [whole(out_grad)],
        [whole(shape_of(piece, 4 * part))] * 4, [pltpu.VMEM((4, piece, 3 * part), WIDE)],
        flops=6 * tokens * width * part,
    )


def fold(order, terms, margin=0):
    high, width = terms[0].shape[1:]
    rows = high // 4
    terms = [t.reshape(-1, 2, 2, rows, width) for t in terms]

    def body(flat_ref, *refs):
        ins, (kept_ref, sent_ref) = refs[:-2], refs[-2:]
        half = half_of(flat_ref[0])

        def total(at):
            return sum(r[k, 0, at].astype(WIDE) for r in ins for k in range(r.shape[0]))

        kept_ref[0] = total(half)
        sent_ref[0, :, :width] = total(1 - half).astype(LOW)

    return run(
        body, order, (2,),
        [
            (t, (t.shape[0], 1) + t.shape[2:], lambda b, f: (0, b, 0, 0, 0))
            for t in terms
        ],
        [
            by_rows(shape_of(2, rows, width, dtype=WIDE), 1),
            by_rows(shape_of(2, rows, width + margin), 1),
        ],
    )


def split_rows(order, kept, received):
    _, high, width = kept.shape
    rows = high // 2
    kept, received = kept.reshape(4, rows, width), received.reshape(4, rows, -1)

    def body(flat_ref, kept_ref, received_ref, *outs):
        for i in range(4):
            at = group_of(flat_ref[0]) ^ i
            outs[i][...] = (
                kept_ref[at] + received_ref[at, :, :width].astype(WIDE)
            ).astype(LOW)

    return run(
        body, order, (1,), [whole(kept), whole(received)], [whole(shape_of(rows, width))] * 4
    )


def finish(order, slices, weight, gain, sizes):
    rows, width = slices[0].shape
    count, part, rest = sizes

    def body(flat_ref, *refs):
        w_ref, gain_ref, scaled_ref, gain_out, plain_ref, held = refs[4:]
        for i in range(4):
            held[group_of(flat_ref[0]) ^ i] = refs[i][...].astype(WIDE)
        total = jnp.zeros((rows, 1), WIDE)
        scale = column_of(gain_ref[...].astype(WIDE))
        for s in range(4):
            for t in range(count):
                at = (4 * t + s) * part
                grad = held[s, :, t * part : (t + 1) * part]
                total += jnp.sum(
                    grad * w_ref[:, at : at + part].astype(WIDE), axis=1, keepdims=True
                )
                scaled_ref[:, at : at + part] = grad * scale
            plain_ref[:, s * rest : (s + 1) * rest] = held[s, :, count * part : count * part + rest]
        gain_out[...] = row_of(total)

    return run(
        body, order, (1,), [whole(a) for a in (*slices, weight, gain)],
        [
            whole(shape_of(*weight.shape, dtype=WIDE)),
            whole(shape_of(1, rows, dtype=WIDE)),
            whole(shape_of(rows, 4 * rest, dtype=WIDE)),
        ],
        [pltpu.VMEM((4, rows, width), WIDE)],
    )


TIED = {
    "ac",
    "af",
    "cf",
    "cmov",
    "cs",
    "df",
    "dz",
    "fz",
    "ih2",
    "l1",
    "m1z",
    "mov",
    "out",
    "pull_late",
    "sl1c",
    "t2",
    "tables",
    "wf",
    "x2",
}
WAITS = {
    "blk": 1,
    "ent": 1,
    "cblk": 3,
    "cf": 4,
    "mov": 4,
    "wc": 8,
    "wz": 8,
    "y2": 9,
    "wf": 10,
    "x2": 10,
    "cmov": 11,
    "dz": 14,
    "ofb": 15,
    "ofa": 17,
    "oz": 17,
    "m1c": 19,
    "oh": 21,
    "fz": 22,
    "f1": 24,
    "f2": 25,
}


def quad_device(
    inputs,
    positions,
    attn_gain,
    qkv_weight,
    attn_out_weight,
    mlp_gain,
    up_weight,
    down_weight,
    cotangent,
):
    order = Order([lax.axis_index(FLAT).astype(jnp.int32).reshape(1)])
    tokens, width = inputs.shape[1:]
    part, ff = width // 4, FF // 4
    gain_one, gain_two = attn_gain[None], mlp_gain[None]

    def at(point):
        wait(order, *[sent_as[n] for n, p in WAITS.items() if p == point])

    sent_as = {}

    def go(name, array, pairs):
        sent_as[name] = send(after(order, array) if name in TIED else array, pairs)
        return sent_as[name]

    pos = positions[0]
    pos_row = jnp.concatenate([pos // 128, pos % 128]).astype(LOW)
    pos_row = jnp.pad(pos_row[None], ((0, 15), (0, width - 2 * tokens)))
    block = jnp.concatenate([inputs[0], pos_row])
    first = go("ent", block, ENTER)
    wait(order, block)
    own, sent = split_slices(order, qkv_weight, attn_out_weight, gain_one, 3)
    received = go("sl1c", sent, TO_CORE)
    own_two, sent = split_slices(order, up_weight, down_weight, gain_two, 2)
    received_two = go("sl2c", sent, TO_CORE)
    core_block = go("blk", block, TO_CORE)
    cot_own = jnp.concatenate([cotangent[0], pos_row])
    cot_block = go("cblk", cot_own, TO_CORE)
    own, sent = chip_rows(order, own, received)
    received = go("sl1z", sent, TO_ZL)
    own_two, sent = chip_rows(order, own_two, received_two)
    at(1)
    one = quad_rows(order, own, received)
    at(2)
    one_far = go("zh1", one, TO_ZH)
    received_two = go("sl2z", sent, TO_ZL)
    second = go("mov", first, ENTER_MOVED)
    core_first = go("cf", first, TO_CORE)
    two = quad_rows(order, own_two, received_two)
    at(3)
    two_far = go("zh2", two, TO_ZH)
    one = line_rows(order, one, one_far)
    half = one.shape[0] // 2
    one_x, one_y = go("x1", one, TO_X), go("y1", one, TO_Y)
    at(4)
    core_second = go("cs", second, TO_CORE)
    cot_first = go("cent", cot_own, ENTER)
    one_top = go("t1", one_x[:half], TO_Y)
    one_low = go("l1", one_y[half:], TO_X)
    at(5)
    x, pos_all = join_tokens(
        order, [block, first, second, core_block, core_first, core_second], tokens, 16
    )
    pos_all = pos_all.reshape(4, 16, width)[:, 0, : 2 * tokens].astype(WIDE)
    pos_all = (pos_all[:, :tokens] * 128.0 + pos_all[:, tokens:]).reshape(4 * tokens)
    cos_table, sin_table = rope_lanes(pos_all)
    one = [one, one_x, one_y, one_top, one_low]
    if "tables" in TIED:
        wait(order, cos_table, sin_table)
    at(6)

    w_out = jnp.concatenate([p[:, 3 * part :] for p in one])
    w_side = go("wz", w_out, TO_ZL)
    w_core = go("wc", w_out, TO_CORE)
    normed_one, mix = project(order, x, one, cos_table, sin_table)
    at(7)
    cot_second = go("cmov", cot_first, ENTER_MOVED) if "cot_early" in TIED else None
    two = line_rows(order, two, two_far)
    two_x, two_y = go("x2", two, TO_X), go("y2", two, TO_Y)
    at(8)
    w_far = go("wf", w_side, TO_CORE)
    attended, logs = attend(order, mix)
    att_side = go("az", attended, TO_ZL)
    at(9)
    two_top = go("t2", two_x[: half + 16], TO_Y)
    two_low = go("l2", two_y[half - 16 :], TO_X)
    att_core = go("ac", attended, TO_CORE)
    at(10)
    if cot_second is None:
        cot_second = go("cmov", cot_first, ENTER_MOVED)
    w_out = [w_out, w_side, w_core, w_far]
    heads = [attended, att_side, att_core, go("af", att_side, TO_CORE)]
    at(11)
    normed_two, resid = join_heads(order, x, heads, w_out)

    core_first = go("ccf", cot_first, TO_CORE)
    core_second = go("ccs", cot_second, TO_CORE)
    at(12)
    (cot,) = join_tokens(
        order,
        [cot_own, cot_first, cot_second, cot_block, core_first, core_second],
        tokens,
    )
    two = [two, two_x, two_y, two_top, two_low]
    cot_base = cot[:tokens]
    hidden, d_up = feed(order, normed_two, cot, two)

    grads = [(d_up, 0)]
    far = go("b1c", back_half(order, grads, two, True)[0], TO_CORE)
    near, other = back_half(order, grads, two, False)
    side = (other + far[tokens:].astype(WIDE)).astype(LOW)
    side = go("b1z", jnp.pad(side, ((0, 16), (0, 0))), TO_ZL)
    ff_terms = feed_grads(order, normed_two, cot, d_up, hidden)
    at(13)
    if "a2a" not in TIED:
        ff_terms = lax.all_to_all(ff_terms, ("y", "x"), split_axis=0, concat_axis=0, tiled=True)
    d_low, d_resid = norm_pull(order, resid, (near, far, side), cot_base, True)
    if "a2a" in TIED:
        ff_terms = lax.all_to_all(
            after(order, ff_terms), ("y", "x"), split_axis=0, concat_axis=0, tiled=True
        )
    d_side = go("dz", d_low, TO_ZL)
    d_core = go("dc", d_low, TO_CORE)
    out_far, out_near, out_other = back_both(order, hidden, 2 * ff, two)
    at(14)
    out_far = [go("ofa", out_far[:tokens], TO_CORE), go("ofb", out_far[tokens:], TO_CORE)]
    out_side = (out_other + out_far[1].astype(WIDE)).astype(LOW)
    out_side = go("oz", out_side, TO_ZL)
    d_all = [d_low, d_side, d_core, go("df", d_side, TO_CORE)]
    at(15)
    d_attended, out_grad = heads_back(order, d_all, heads, w_out)
    at(16)
    d_mixed = attend_back(order, mix, attended, d_attended, logs, cos_table, sin_table)
    at(17)
    grads = [(d, t * part) for t, d in enumerate(d_mixed)]
    far = go("m1c", back_half(order, grads, one, True)[0], TO_CORE)
    at(18)
    output = resid + out_near + out_far[0].astype(WIDE) + out_side.astype(WIDE)
    output = output.astype(LOW)
    if "out" in TIED:
        wait(order, output)
    output = go("oh", output, TO_HOME)
    near, other = back_half(order, grads, one, False)
    side = (other + far[tokens:].astype(WIDE)).astype(LOW)
    if "side" in TIED:
        wait(order, side)
    side = go("m1z", side, TO_ZL)
    pieces = mixed_grads(order, normed_one, d_mixed, out_grad)
    at(19)
    mixed_terms = [pieces[0]] + [
        go(n, p, pairs)
        for n, p, pairs in zip(("mx", "my", "mxy"), pieces[1:], (TO_X, TO_Y, TO_XY))
    ]
    ff_kept, ff_sent = fold(order, [ff_terms])
    ff_sent = go("fz", ff_sent, TO_ZH)
    at(20)
    if "pull_late" not in TIED:
        (input_grad,) = norm_pull(order, x, (near, far, side), d_resid, False)
    at(21)
    mixed_kept, mixed_sent = fold(order, [t[None] for t in mixed_terms], 128)
    mixed_sent = go("mz", mixed_sent, TO_ZH)
    at(22)
    if "pull_late" in TIED:
        (input_grad,) = norm_pull(order, x, (near, far, side), d_resid, False)
    ff_slices = split_rows(order, ff_kept, ff_sent)
    at(23)
    input_grad = jnp.concatenate(
        [
            go("ih1", input_grad[: tokens // 2], TO_HOME),
            go("ih2", input_grad[tokens // 2 :], TO_HOME),
        ]
    )
    ff_slices = [ff_slices[0]] + [
        go(n, p, pairs)
        for n, p, pairs in zip(("f1", "f2", "f3"), ff_slices[1:], (TO_ZL, TO_CORE, TO_FAR))
    ]
    at(24)
    mixed_slices = split_rows(order, mixed_kept, mixed_sent)
    mixed_slices = [mixed_slices[0]] + [
        go(n, p, pairs)
        for n, p, pairs in zip(("m1", "m2", "m3"), mixed_slices[1:], (TO_ZL, TO_CORE, TO_FAR))
    ]
    at(25)
    up_grad, gain_two_grad, down_grad = finish(
        order, ff_slices, up_weight, gain_two, (2, ff, ff)
    )
    qkv_grad, gain_one_grad, out_grad = finish(
        order, mixed_slices, qkv_weight, gain_one, (3, part, part)
    )
    return (
        output[None],
        input_grad[None],
        gain_one_grad[0],
        qkv_grad,
        out_grad,
        gain_two_grad[0],
        up_grad,
        down_grad,
    )


def solution(mesh):
    dp, seq = "dp", "seq"
    step = per_device
    if tuple(mesh.shape.values()) == QUAD_MESH:
        dp, seq, step = ("y", "x", "c"), ("zh", "zl"), quad_device
        mesh = jax.sharding.Mesh(mesh.devices.reshape(2, 2, 2, 2, 2), FLAT)
        every = FLAT
    else:
        every = (dp, seq)
    rows = P(every, None)
    return jax.shard_map(
        step,
        mesh=mesh,
        in_specs=(
            P(dp, seq, None),
            P(dp, seq),
            P(every),
            rows,
            rows,
            P(every),
            rows,
            rows,
            P(dp, seq, None),
        ),
        out_specs=(
            P(dp, seq, None),
            P(dp, seq, None),
            P(every),
            rows,
            rows,
            P(every),
            rows,
            rows,
        ),
        check_vma=False,
    )
```
